128 devices in a mesh: gen: 32 (over z, y, core), ref: 4 (over x).
Axes of the slice: x: 4, y: 4, z: 4, core: 2. Of those that a mesh axis runs over, the one named last changes fastest.
Arguments:
- gen_features: bfloat16 [16384, 2048], P('gen'), may hold values from 0 to 40
- gen_weight: float32 [16384], P('gen'), may hold values from 0.5 to 18
- ref_features: bfloat16 [16384, 2048], P('ref'), may hold values from 0 to 40
- ref_weight: float32 [16384], P('ref'), may hold values from 0.5 to 18
- ref_self: float32 [16384], P('ref'), may hold values from 0 to 2
Outputs:
- gen_gap: float32 [16384], P('gen')
- ref_gap: float32 [16384], P('ref')
- divergence: float32 [], replicated
The draws below stay inside these ranges and needn't reach their ends.
All inputs are finite; a program needn't handle non-finite values.
Results may differ from the reference program's by a relative error of at most 0.0003.
Values may be sent and summed in bfloat16 or wider, within the bound.
No kernel may reach another device: no remote copies, remote signals or barrier semaphores. Data moves between devices by JAX's collectives and lax.ppermute only.
A program may use at most 128 MiB of HBM per device.

```python
import jax
import jax.numpy as jnp
from jax import lax

D = 2048
GEN_DEV = 512
ITERS = 2
GEN_ROWS = 16384
REF_ROWS = 16384
N_GEN = 32


def feature_pair(key):
    key_list = jax.random.split(jax.random.fold_in(key, 11), 8)
    mean_profile = jnp.exp(jax.random.uniform(key_list[7], (1, D), jnp.float32, jnp.log(0.3), jnp.log(1.5)))
    gen_values = mean_profile * jax.random.exponential(key_list[0], (GEN_ROWS, D), jnp.float32)
    ref_values = mean_profile * jax.random.exponential(key_list[1], (REF_ROWS, D), jnp.float32)
    gen_values = gen_values * jnp.exp(jax.random.uniform(key_list[2], (GEN_ROWS, 1), jnp.float32, jnp.log(0.7), jnp.log(1.4)))
    ref_values = ref_values * jnp.exp(jax.random.uniform(key_list[3], (REF_ROWS, 1), jnp.float32, jnp.log(0.7), jnp.log(1.4)))
    return (jnp.clip(gen_values, 0.0, 40.0), jnp.clip(ref_values, 0.0, 40.0))


def draw_gen_features(key, part):
    return feature_pair(key)[0].astype(jnp.bfloat16)


def draw_ref_features(key, part):
    return feature_pair(key)[1].astype(jnp.bfloat16)


def rising_weight(key, row_span):
    base_weight = jnp.exp(jax.random.uniform(key, (row_span,), jnp.float32, jnp.log(0.5), jnp.log(2.0)))
    ramp_height = 2.0
    ramp_factor = 1.0 + ramp_height * jnp.arange(row_span, dtype=jnp.float32) / max(row_span - 1, 1)
    return base_weight * ramp_factor


def draw_gen_weight(key, part):
    return rising_weight(jax.random.fold_in(key, 23), GEN_ROWS)


def draw_ref_weight(key, part):
    return rising_weight(jax.random.fold_in(key, 29), REF_ROWS)


def level_of(stream_key, extent, cuts, low, high):
    def one(dim, parts):
        heights = jax.random.uniform(jax.random.fold_in(jax.random.fold_in(stream_key, 6), dim), (parts,), jnp.float32, low / len(cuts), high / len(cuts))
        return jnp.repeat(jnp.exp(heights), extent[dim] // parts).reshape((-1,) + (1,) * (len(extent) - dim - 1))

    loudness = one(*cuts[0])
    for cut in cuts[1:]:
        loudness = loudness * one(*cut)
    return loudness


def setup_inputs(seed: int = 0) -> dict:
    arg_keys = jax.random.split(jax.random.key(seed), 6)
    return {
        "gen_features": draw_gen_features(jax.random.fold_in(arg_keys[5], 71), 0),
        "gen_weight": draw_gen_weight(jax.random.fold_in(arg_keys[5], 71), 0),
        "ref_features": draw_ref_features(jax.random.fold_in(arg_keys[5], 71), 0),
        "ref_weight": draw_ref_weight(jax.random.fold_in(arg_keys[5], 71), 0),
        "ref_self": jnp.clip(2.0 * jax.random.uniform(arg_keys[4], (REF_ROWS,), jnp.float32) ** level_of(arg_keys[4], (REF_ROWS,), ((0, 4),), -0.2, 0.2), 0.0, 2.0),
    }


blur_scale = 0.1


def half_norms(features):
    values = features.astype(jnp.float32)
    return 0.5 * jnp.sum(values * values, axis=1) / D


def pair_cost(left_rows, left_half, right_rows, right_half):
    inner_dots = lax.dot_general(left_rows, right_rows, (((1,), (1,)), ((), ())), preferred_element_type=jnp.float32)
    return (left_half[:, None] + right_half[None, :]) - inner_dots / D


def log_sum_exp(scores, reduce_axis):
    top_value = jnp.max(scores, axis=reduce_axis, keepdims=True)
    return jnp.squeeze(top_value, reduce_axis) + jnp.log(jnp.sum(jnp.exp(scores - top_value), axis=reduce_axis))


def reference(gen_features, gen_weight, ref_features, ref_weight, ref_self):
    gen_mass = jnp.sum(gen_weight)
    ref_mass = jnp.sum(ref_weight)
    gen_share = gen_weight / gen_mass
    ref_share = ref_weight / ref_mass
    gen_log = jnp.log(gen_weight) - jnp.log(gen_mass)
    ref_log = jnp.log(ref_weight) - jnp.log(ref_mass)
    gen_half = half_norms(gen_features)
    ref_half = half_norms(ref_features)
    gen_blocks = gen_features.reshape(N_GEN, GEN_DEV, D)
    half_blocks = gen_half.reshape(N_GEN, GEN_DEV)
    cross_gen = jnp.zeros((GEN_ROWS,), jnp.float32)
    cross_ref = jnp.zeros((REF_ROWS,), jnp.float32)
    self_gen = jnp.zeros((GEN_ROWS,), jnp.float32)
    for pass_index in range(ITERS + 1):
        ref_terms = ref_log + cross_ref / blur_scale
        gen_terms = gen_log + cross_gen / blur_scale
        self_terms = gen_log + self_gen / blur_scale

        def block_pass(running, block_data):
            row_block, rows_half, rows_terms = block_data
            cross_cost = pair_cost(row_block, rows_half, ref_features, ref_half)
            new_gen = -blur_scale * log_sum_exp(ref_terms[None, :] - cross_cost / blur_scale, 1)
            column_scores = rows_terms[:, None] - cross_cost / blur_scale
            running_peak, running_sum = running
            column_peak = jnp.maximum(running_peak, jnp.max(column_scores, axis=0))
            column_sum = running_sum * jnp.exp(running_peak - column_peak) + jnp.sum(jnp.exp(column_scores - column_peak[None, :]), axis=0)
            self_cost = pair_cost(row_block, rows_half, gen_features, gen_half)
            new_self = -blur_scale * log_sum_exp(self_terms[None, :] - self_cost / blur_scale, 1)
            return (column_peak, column_sum), (new_gen, new_self)

        initial = (jnp.full((REF_ROWS,), -jnp.inf, jnp.float32), jnp.zeros((REF_ROWS,), jnp.float32))
        (column_peak, column_sum), (new_gen, new_self) = lax.scan(block_pass, initial, (gen_blocks, half_blocks, gen_terms.reshape(N_GEN, GEN_DEV)))
        new_gen = new_gen.reshape(GEN_ROWS)
        new_self = new_self.reshape(GEN_ROWS)
        new_ref = -blur_scale * (column_peak + jnp.log(column_sum))
        if pass_index == 0:
            cross_gen, cross_ref, self_gen = new_gen, new_ref, new_self
        else:
            cross_gen = 0.5 * (cross_gen + new_gen)
            cross_ref = 0.5 * (cross_ref + new_ref)
            self_gen = 0.5 * (self_gen + new_self)
    gen_gap = cross_gen - self_gen
    ref_gap = cross_ref - ref_self
    divergence = jnp.sum(gen_share * gen_gap) + jnp.sum(ref_share * ref_gap)
    return gen_gap, ref_gap, divergence
```

```python
import functools

import jax
import jax.numpy as jnp
import numpy as np
from jax import lax
from jax.experimental import pallas as pl
from jax.experimental.pallas import tpu as pltpu
from jax.sharding import PartitionSpec as P

ITERS = 2
EPS = 0.1
LOG2E = 1.4426950408889634
F32 = jnp.float32
LANES = 128
TILE = 512
ROWS = 32
LOW = 2.0**-80
HIGH = 2.0**120


def spread(vec_ref, out_ref, count):
    for q in range(count):
        block = jnp.broadcast_to(vec_ref[q : q + 1, :], (LANES, LANES))
        out_ref[q * LANES : (q + 1) * LANES, :] = block.T


def lane_fold(acc, op):
    return op(acc.T, axis=0, keepdims=True)


def norms(feat_ref, start, count, scale):
    width = feat_ref.shape[1]
    out = []
    for q in range(count):
        acc = jnp.zeros((LANES, LANES), F32)
        for c in range(width // LANES):
            x = feat_ref[start + q * LANES : start + (q + 1) * LANES, c * LANES : (c + 1) * LANES].astype(F32)
            acc = acc + x * x
        out.append(lane_fold(acc, jnp.sum) * scale)
    return out


def sweep(d_ref, base, chunks, u, vs_ref, rowacc_ref):
    rows = d_ref.shape[0]

    def body(r, cols):
        at = pl.ds(pl.multiple_of(r * ROWS, ROWS), ROWS)
        vs = vs_ref[at, :]
        racc = rowacc_ref[at, :]
        out = []
        for c in range(chunks):
            p = jnp.exp2((d_ref[at, base + c * LANES : base + (c + 1) * LANES] + u[c]) + vs)
            racc = racc + p
            out.append(cols[c] + jnp.sum(p.reshape(ROWS // 8, 8, LANES), axis=0))
        rowacc_ref[at, :] = racc
        return tuple(out)

    zero = jnp.zeros((8, LANES), F32)
    cols = lax.fori_loop(0, rows // ROWS, body, (zero,) * chunks, unroll=2)
    return [jnp.sum(c, axis=0, keepdims=True) for c in cols]


def tile_peak(d_ref, u, vs_ref):
    rows = d_ref.shape[0]
    best = jnp.full((8, LANES), -3.0e38, F32)

    def body(r, best):
        at = pl.ds(pl.multiple_of(r * ROWS, ROWS), ROWS)
        val = (d_ref[at, 0:LANES] + u) + vs_ref[at, :]
        return jnp.maximum(best, jnp.max(val.reshape(ROWS // 8, 8, LANES), axis=0))

    best = lax.fori_loop(0, rows // ROWS, body, best, unroll=2)
    return jnp.max(jnp.max(best, axis=0, keepdims=True), axis=1, keepdims=True)


def finish(d_ref, u_ref, v_ref, vs_ref, rowacc_ref, colsum_ref, peak_ref, lrow_ref, lcol_ref):
    rows, cols = d_ref.shape
    nq, nc = rows // LANES, cols // LANES
    rowsum = [lane_fold(rowacc_ref[q * LANES : (q + 1) * LANES, :], jnp.sum) for q in range(nq)]
    rowsum = jnp.concatenate(rowsum, axis=0)
    colsum = colsum_ref[...]
    low = jnp.minimum(jnp.min(rowsum), jnp.min(colsum))
    high = jnp.maximum(jnp.max(rowsum), jnp.max(colsum))
    good = jnp.logical_and(low >= LOW, high <= HIGH)
    peak = peak_ref[0:1, :]

    @pl.when(good)
    def _():
        lrow_ref[...] = (jnp.log2(rowsum) + peak) - v_ref[...]
        lcol_ref[...] = (jnp.log2(colsum) + peak) - u_ref[...]

    @pl.when(jnp.logical_not(good))
    def _():
        spread(v_ref, vs_ref, nq)
        for q in range(nq):
            part = slice(q * LANES, (q + 1) * LANES)

            def row_peak(c, best):
                at = pl.ds(pl.multiple_of(c * LANES, LANES), LANES)
                return jnp.maximum(best, d_ref[part, at] + u_ref[pl.ds(c, 1), :])

            best = lax.fori_loop(0, nc, row_peak, jnp.full((LANES, LANES), -3.0e38, F32))
            top = jnp.max(best, axis=1, keepdims=True)

            def row_sum(c, acc):
                at = pl.ds(pl.multiple_of(c * LANES, LANES), LANES)
                return acc + jnp.exp2((d_ref[part, at] + u_ref[pl.ds(c, 1), :]) - top)

            acc = lax.fori_loop(0, nc, row_sum, jnp.zeros((LANES, LANES), F32))
            log_sum = jnp.log2(jnp.sum(acc, axis=1, keepdims=True)) + top
            lrow_ref[q : q + 1, :] = lane_fold(jnp.broadcast_to(log_sum, (LANES, LANES)), jnp.max)

        def column(c, carry):
            at = pl.ds(pl.multiple_of(c * LANES, LANES), LANES)
            val = d_ref[:, at] + vs_ref[...]
            top = jnp.max(val, axis=0, keepdims=True)
            lcol_ref[pl.ds(c, 1), :] = top + jnp.log2(jnp.sum(jnp.exp2(val - top), axis=0, keepdims=True))
            return carry

        lax.fori_loop(0, nc, column, 0)


def start_peak(d_ref, u0, v_ref, vs_ref, peak_ref, rowacc_ref):
    rows = d_ref.shape[0]
    spread(v_ref, vs_ref, rows // LANES)
    peak = jnp.broadcast_to(tile_peak(d_ref, u0, vs_ref), (8, LANES))
    peak_ref[...] = peak
    vs_ref[...] = vs_ref[...] - peak[0:1, :]
    rowacc_ref[...] = jnp.zeros_like(rowacc_ref)


def first_kernel(
    gen_ref, ref_ref, glog_ref, rlog_ref, d_hbm, lrow_ref, lcol_ref, hrow_ref, hcol_ref,
    d_ref, u_ref, v_ref, vs_ref, rowacc_ref, colsum_ref, peak_ref, sem,
):
    rows, width = gen_ref.shape
    chunks = TILE // LANES
    j = pl.program_id(0)
    steps = pl.num_programs(0)
    half_scale = 0.5 * LOG2E / (EPS * width)
    dot_scale = LOG2E / (EPS * width)
    base = pl.multiple_of(j * TILE, TILE)

    @pl.when(j == 0)
    def _():
        for q, part in enumerate(norms(gen_ref, 0, rows // LANES, half_scale)):
            hrow_ref[q : q + 1, :] = part
            v_ref[q : q + 1, :] = glog_ref[q : q + 1, :] - part

    half = norms(ref_ref, 0, chunks, half_scale)
    u = []
    for c in range(chunks):
        row = pl.ds(j * chunks + c, 1)
        hcol_ref[row, :] = half[c]
        u.append(rlog_ref[row, :] - half[c])
        u_ref[row, :] = u[c]
    dots = lax.dot_general(
        gen_ref[...], ref_ref[...], (((1,), (1,)), ((), ())), preferred_element_type=F32
    )
    d_ref[:, pl.ds(base, TILE)] = dots * dot_scale
    view = d_ref.at[:, pl.ds(base, TILE)]
    pltpu.make_async_copy(view, d_hbm.at[:, pl.ds(base, TILE)], sem.at[j]).start()

    @pl.when(j == 0)
    def _():
        start_peak(view, u[0], v_ref, vs_ref, peak_ref, rowacc_ref)

    for c, part in enumerate(sweep(view, 0, chunks, u, vs_ref, rowacc_ref)):
        colsum_ref[pl.ds(j * chunks + c, 1), :] = part

    @pl.when(j == steps - 1)
    def _():
        finish(d_ref, u_ref, v_ref, vs_ref, rowacc_ref, colsum_ref, peak_ref, lrow_ref, lcol_ref)
        for t in range(d_ref.shape[1] // TILE):
            part = pl.ds(t * TILE, TILE)
            pltpu.make_async_copy(d_ref.at[:, part], d_hbm.at[:, part], sem.at[t]).wait()


def first_pass(gen, ref, glog, rlog):
    rows, width = gen.shape
    cols = ref.shape[0]
    nq, nc = rows // LANES, cols // LANES
    whole = lambda shape: pl.BlockSpec(shape, lambda j: (0, 0))
    vec = lambda n: jax.ShapeDtypeStruct((n, LANES), F32)
    return pl.pallas_call(
        first_kernel,
        grid=(cols // TILE,),
        in_specs=[
            whole((rows, width)),
            pl.BlockSpec((TILE, width), lambda j: (j, 0)),
            whole((nq, LANES)),
            whole((nc, LANES)),
        ],
        out_shape=(jax.ShapeDtypeStruct((rows, cols), F32), vec(nq), vec(nc), vec(nq), vec(nc)),
        out_specs=(
            pl.BlockSpec(memory_space=pl.ANY),
            whole((nq, LANES)),
            whole((nc, LANES)),
            whole((nq, LANES)),
            whole((nc, LANES)),
        ),
        scratch_shapes=[
            pltpu.VMEM((rows, cols), F32),
            pltpu.VMEM((nc, LANES), F32),
            pltpu.VMEM((nq, LANES), F32),
            pltpu.VMEM((rows, LANES), F32),
            pltpu.VMEM((rows, LANES), F32),
            pltpu.VMEM((nc, LANES), F32),
            pltpu.VMEM((8, LANES), F32),
            pltpu.SemaphoreType.DMA((cols // TILE,)),
        ],
        compiler_params=pltpu.CompilerParams(vmem_limit_bytes=40 << 20),
        name="cross_first",
    )(gen, ref, glog, rlog)


def load_tiles(src_hbm, dst_ref, sem):
    cols = dst_ref.shape[1]
    copies = []
    for t in range(cols // TILE):
        part = pl.ds(t * TILE, TILE)
        copies.append(pltpu.make_async_copy(src_hbm.at[:, part], dst_ref.at[:, part], sem.at[t]))
        copies[-1].start()
    return copies


def next_kernel(
    d_hbm, u_ref, v_ref, lrow_ref, lcol_ref, d_ref, vs_ref, rowacc_ref, colsum_ref, peak_ref, sem
):
    chunks = TILE // LANES
    copies = load_tiles(d_hbm, d_ref, sem)
    for t, copy in enumerate(copies):
        copy.wait()
        if t == 0:
            start_peak(d_ref, u_ref[0:1, :], v_ref, vs_ref, peak_ref, rowacc_ref)
        u = [u_ref[t * chunks + c : t * chunks + c + 1, :] for c in range(chunks)]
        for c, part in enumerate(sweep(d_ref, t * TILE, chunks, u, vs_ref, rowacc_ref)):
            colsum_ref[t * chunks + c : t * chunks + c + 1, :] = part
    finish(d_ref, u_ref, v_ref, vs_ref, rowacc_ref, colsum_ref, peak_ref, lrow_ref, lcol_ref)


def next_pass(d, u, v):
    rows, cols = d.shape
    nq, nc = rows // LANES, cols // LANES
    vmem = pl.BlockSpec(memory_space=pltpu.VMEM)
    return pl.pallas_call(
        next_kernel,
        in_specs=[pl.BlockSpec(memory_space=pl.ANY), vmem, vmem],
        out_shape=(jax.ShapeDtypeStruct((nq, LANES), F32), jax.ShapeDtypeStruct((nc, LANES), F32)),
        out_specs=(vmem, vmem),
        scratch_shapes=[
            pltpu.VMEM((rows, cols), F32),
            pltpu.VMEM((rows, LANES), F32),
            pltpu.VMEM((rows, LANES), F32),
            pltpu.VMEM((nc, LANES), F32),
            pltpu.VMEM((8, LANES), F32),
            pltpu.SemaphoreType.DMA((cols // TILE,)),
        ],
        compiler_params=pltpu.CompilerParams(vmem_limit_bytes=40 << 20),
        name="cross_next",
    )(d, u, v)


def self_first_kernel(
    gen_ref, piece_ref, hrow_ref, weight_ref, e_ref, y_ref, hs_ref, rowacc_ref
):
    rows, width = gen_ref.shape
    chunks = TILE // LANES
    j = pl.program_id(0)
    half_scale = 0.5 * LOG2E / (EPS * width)
    dot_scale = LOG2E / (EPS * width)

    @pl.when(j == 0)
    def _():
        spread(hrow_ref, hs_ref, rows // LANES)
        rowacc_ref[...] = jnp.zeros_like(rowacc_ref)

    half = norms(piece_ref, 0, chunks, half_scale)
    e_ref[...] = lax.dot_general(
        gen_ref[...], piece_ref[...], (((1,), (1,)), ((), ())), preferred_element_type=F32
    )
    weight = [weight_ref[pl.ds(j * chunks + c, 1), :] for c in range(chunks)]

    def body(r, carry):
        at = pl.ds(pl.multiple_of(r * ROWS, ROWS), ROWS)
        hs = hs_ref[at, :]
        racc = rowacc_ref[at, :]
        for c in range(chunks):
            part = slice(c * LANES, (c + 1) * LANES)
            e = jnp.exp2(e_ref[at, part] * dot_scale - (hs + half[c]))
            e_ref[at, part] = e
            racc = racc + e * weight[c]
        rowacc_ref[at, :] = racc
        return carry

    lax.fori_loop(0, rows // ROWS, body, 0, unroll=2)

    @pl.when(j == pl.num_programs(0) - 1)
    def _():
        for q in range(rows // LANES):
            y_ref[q : q + 1, :] = lane_fold(rowacc_ref[q * LANES : (q + 1) * LANES, :], jnp.sum)


def self_first(gen, pieces, hrow, weight):
    rows, width = gen.shape
    cols = pieces.shape[0]
    nq, nc = rows // LANES, cols // LANES
    whole = lambda shape: pl.BlockSpec(shape, lambda j: (0, 0))
    return pl.pallas_call(
        self_first_kernel,
        grid=(cols // TILE,),
        in_specs=[
            whole((rows, width)),
            pl.BlockSpec((TILE, width), lambda j: (j, 0)),
            whole((nq, LANES)),
            whole((nc, LANES)),
        ],
        out_shape=(jax.ShapeDtypeStruct((rows, cols), F32), jax.ShapeDtypeStruct((nq, LANES), F32)),
        out_specs=(pl.BlockSpec((rows, TILE), lambda j: (0, j)), whole((nq, LANES))),
        scratch_shapes=[pltpu.VMEM((rows, LANES), F32), pltpu.VMEM((rows, LANES), F32)],
        compiler_params=pltpu.CompilerParams(vmem_limit_bytes=40 << 20),
        name="self_first",
    )(gen, pieces, hrow, weight)


def self_cols_kernel(e_hbm, w_ref, z_ref, e_ref, ws_ref, sem):
    rows, cols = e_ref.shape
    chunks = TILE // LANES
    copies = load_tiles(e_hbm, e_ref, sem)
    spread(w_ref, ws_ref, rows // LANES)
    zero = jnp.zeros((8, LANES), F32)
    for t, copy in enumerate(copies):
        copy.wait()

        def body(r, acc):
            at = pl.ds(pl.multiple_of(r * ROWS, ROWS), ROWS)
            ws = ws_ref[at, :]
            out = []
            for c in range(chunks):
                e = e_ref[at, t * TILE + c * LANES : t * TILE + (c + 1) * LANES] * ws
                out.append(acc[c] + jnp.sum(e.reshape(ROWS // 8, 8, LANES), axis=0))
            return tuple(out)

        acc = lax.fori_loop(0, rows // ROWS, body, (zero,) * chunks, unroll=2)
        for c in range(chunks):
            z_ref[t * chunks + c : t * chunks + c + 1, :] = jnp.sum(acc[c], axis=0, keepdims=True)


def self_rows_kernel(e_hbm, w_ref, y_ref, e_ref, rowacc_ref, sem):
    rows, cols = e_ref.shape
    chunks = TILE // LANES
    copies = load_tiles(e_hbm, e_ref, sem)
    rowacc_ref[...] = jnp.zeros_like(rowacc_ref)
    for t, copy in enumerate(copies):
        copy.wait()

        def body(r, carry):
            at = pl.ds(pl.multiple_of(r * ROWS, ROWS), ROWS)
            acc = rowacc_ref[at, :]
            for c in range(chunks):
                acc = acc + (
                    e_ref[at, t * TILE + c * LANES : t * TILE + (c + 1) * LANES]
                    * w_ref[t * chunks + c : t * chunks + c + 1, :]
                )
            rowacc_ref[at, :] = acc
            return carry

        lax.fori_loop(0, rows // ROWS, body, 0, unroll=2)
    for q in range(rows // LANES):
        y_ref[q : q + 1, :] = lane_fold(rowacc_ref[q * LANES : (q + 1) * LANES, :], jnp.sum)


def self_apply(kernel, name, e, w, out_rows):
    rows, cols = e.shape
    vmem = pl.BlockSpec(memory_space=pltpu.VMEM)
    return pl.pallas_call(
        kernel,
        in_specs=[pl.BlockSpec(memory_space=pl.ANY), vmem],
        out_shape=jax.ShapeDtypeStruct((out_rows, LANES), F32),
        out_specs=vmem,
        scratch_shapes=[
            pltpu.VMEM((rows, cols), F32),
            pltpu.VMEM((rows, LANES), F32),
            pltpu.SemaphoreType.DMA((cols // TILE,)),
        ],
        compiler_params=pltpu.CompilerParams(vmem_limit_bytes=40 << 20),
        name=name,
    )(e, w)


def log_add(parts):
    top = functools.reduce(jnp.maximum, parts)
    return top + jnp.log2(sum(jnp.exp2(part - top) for part in parts))


def build(n_z, n_y, n_core, n_ref):
    n_gen = n_z * n_y * n_core

    def place(g):
        return g // (n_y * n_core), (g // n_core) % n_y, g % n_core

    def gen_perm(dz, dy, dc):
        out = []
        for g in range(n_gen):
            z, y, c = place(g)
            out.append((g, (((z + dz) % n_z) * n_y + (y + dy) % n_y) * n_core + (c + dc) % n_core))
        return out

    stages = (
        [gen_perm(0, 0, k) for k in range(1, n_core)],
        [gen_perm(0, k, 0) for k in range(1, n_y)],
        [gen_perm(k, 0, 0) for k in range(1, n_z)],
    )
    ref_stage = [[(i, (i + k) % n_ref) for i in range(n_ref)] for k in range(1, n_ref)]

    def exchange(value, axis, perms):
        return [value] + [lax.ppermute(value, axis, perm) for perm in perms]

    def merge(parts, logs):
        if logs == 0:
            return sum(parts)
        top = log_add([part[:logs] for part in parts])
        if parts[0].shape[0] == logs:
            return top
        return jnp.concatenate([top, sum(part[logs:] for part in parts)], axis=0)

    def over_gen(value, logs):
        for perms in stages:
            value = merge(exchange(value, "gen", perms), logs)
        return value

    def over_ref(value, logs):
        return merge(exchange(value, "ref", ref_stage), logs)

    def per_device(gen_features, gen_weight, ref_features, ref_weight, ref_self):
        gen_count, width = gen_features.shape
        ref_count = ref_features.shape[0]
        nq, nc = gen_count // LANES, ref_count // LANES
        g = lax.axis_index("gen")
        x = lax.axis_index("ref")
        quarter = gen_count // n_ref
        pieces = lax.all_gather(
            lax.dynamic_slice_in_dim(gen_features, x * quarter, quarter, 0), "gen", axis=0, tiled=True
        )
        wg = gen_weight.reshape(nq, LANES)
        wr = ref_weight.reshape(nc, LANES)
        glog = jnp.log2(wg)
        rlog = jnp.log2(wr)
        at_g = lax.broadcasted_iota(jnp.int32, (n_gen, LANES), 0) == g
        at_x = lax.broadcasted_iota(jnp.int32, (n_ref, LANES), 0) == x

        def to_cols(rows):
            return jnp.where(at_g, lax.dynamic_slice_in_dim(rows, x, 1, 0), 0.0)

        def to_rows(cols):
            return jnp.where(at_x, lax.dynamic_slice_in_dim(cols, g, 1, 0), 0.0)

        d, lrow, lcol, hrow, hcol = first_pass(gen_features, ref_features, glog, rlog)
        row_part = jnp.concatenate([lrow, jnp.full((nq, LANES), jnp.sum(wr))], axis=0)
        col_part = jnp.concatenate([lcol, to_cols(wg)], axis=0)
        row_part = over_ref(row_part, nq)
        col_part = over_gen(col_part, nc)
        wcols = col_part[nc:]
        gmass = over_gen(jnp.full((8, LANES), jnp.sum(wg)), 0)[0:1, :]
        rmass = row_part[nq : nq + 1]
        gmass_log = jnp.log2(gmass)
        rmass_log = jnp.log2(rmass)
        f = hrow - (row_part[:nq] - rmass_log)
        c = hcol - (col_part[:nc] - gmass_log)
        ubase = rlog - rmass_log - hcol
        vbase = glog - gmass_log - hrow
        for _ in range(ITERS):
            lrow, lcol = next_pass(d, ubase + c, vbase + f)
            lrow = over_ref(lrow, nq)
            lcol = over_gen(lcol, nc)
            f = 0.5 * (f + (hrow - lrow))
            c = 0.5 * (c + (hcol - lcol))
        unit = EPS / LOG2E
        ref_gap = c * unit - ref_self.reshape(nc, LANES)

        e, y1 = self_first(gen_features, pieces, hrow, wcols)
        y1 = over_ref(y1, 0) / gmass
        z2 = self_apply(self_cols_kernel, "self_cols", e, (wg / gmass) / y1, n_gen)
        both = over_gen(jnp.concatenate([z2, to_cols(y1)], axis=0), 0)
        z2, y1_cols = both[:n_gen], both[n_gen:]
        s2_cols = -0.5 * (jnp.log2(y1_cols) + jnp.log2(z2))
        w3 = (wcols / gmass) * jnp.exp2(s2_cols)
        y3 = self_apply(self_rows_kernel, "self_rows", e, w3, nq)
        both = over_ref(jnp.concatenate([y3, to_rows(s2_cols)], axis=0), 0)
        s = 0.5 * (both[nq:] - jnp.log2(both[:nq]))
        gen_gap = (f - s) * unit

        gen_part = jnp.sum((wg / gmass) * gen_gap)
        ref_part = jnp.sum((wr / rmass) * ref_gap)
        gen_part = over_gen(jnp.full((8, LANES), gen_part), 0)
        ref_part = over_ref(jnp.full((8, LANES), ref_part), 0)
        divergence = (gen_part + ref_part)[0, 0]
        return gen_gap.reshape(gen_count), ref_gap.reshape(ref_count), divergence

    return per_device


def solution(mesh):
    n_gen, n_ref = mesh.shape["gen"], mesh.shape["ref"]
    n_core = 2
    n_y = 1
    while n_y * n_y * n_core < n_gen:
        n_y *= 2
    placed = (P("gen", None), P("gen"), P("ref", None), P("ref"), P("ref"))
    return jax.shard_map(
        build(n_gen // (n_y * n_core), n_y, n_core, n_ref),
        mesh=mesh,
        in_specs=placed,
        out_specs=(P("gen"), P("ref"), P()),
        check_vma=False,
    )
```

```python
import functools

import jax
import jax.numpy as jnp
import numpy as np
from jax import lax
from jax.experimental import pallas as pl
from jax.experimental.pallas import tpu as pltpu
from jax.sharding import PartitionSpec as P

ITERS = 2
EPS = 0.1
LOG2E = 1.4426950408889634
F32 = jnp.float32
LANES = 128
TILE = 512
ROWS = 32
LOW = 2.0**-80
HIGH = 2.0**120


def spread(vec_ref, out_ref, count):
    for q in range(count):
        block = jnp.broadcast_to(vec_ref[q : q + 1, :], (LANES, LANES))
        out_ref[q * LANES : (q + 1) * LANES, :] = block.T


def lane_fold(acc, op):
    return op(acc.T, axis=0, keepdims=True)


def norms(feat_ref, start, count, scale):
    width = feat_ref.shape[1]
    out = []
    for q in range(count):
        acc = jnp.zeros((LANES, LANES), F32)
        for c in range(width // LANES):
            x = feat_ref[start + q * LANES : start + (q + 1) * LANES, c * LANES : (c + 1) * LANES].astype(F32)
            acc = acc + x * x
        out.append(lane_fold(acc, jnp.sum) * scale)
    return out


def sweep(d_ref, base, chunks, u, vs_ref, rowacc_ref):
    rows = d_ref.shape[0]

    def body(r, cols):
        at = pl.ds(pl.multiple_of(r * ROWS, ROWS), ROWS)
        vs = vs_ref[at, :]
        racc = rowacc_ref[at, :]
        out = []
        for c in range(chunks):
            p = jnp.exp2((d_ref[at, base + c * LANES : base + (c + 1) * LANES] + u[c]) + vs)
            racc = racc + p
            out.append(cols[c] + jnp.sum(p.reshape(ROWS // 8, 8, LANES), axis=0))
        rowacc_ref[at, :] = racc
        return tuple(out)

    zero = jnp.zeros((8, LANES), F32)
    cols = lax.fori_loop(0, rows // ROWS, body, (zero,) * chunks, unroll=2)
    return [jnp.sum(c, axis=0, keepdims=True) for c in cols]


def tile_peak(d_ref, u, vs_ref):
    rows = d_ref.shape[0]
    best = jnp.full((8, LANES), -3.0e38, F32)

    def body(r, best):
        at = pl.ds(pl.multiple_of(r * ROWS, ROWS), ROWS)
        val = (d_ref[at, 0:LANES] + u) + vs_ref[at, :]
        return jnp.maximum(best, jnp.max(val.reshape(ROWS // 8, 8, LANES), axis=0))

    best = lax.fori_loop(0, rows // ROWS, body, best, unroll=2)
    return jnp.max(jnp.max(best, axis=0, keepdims=True), axis=1, keepdims=True)


def finish(d_ref, u_ref, v_ref, vs_ref, rowacc_ref, colsum_ref, peak_ref, lrow_ref, lcol_ref):
    rows, cols = d_ref.shape
    nq, nc = rows // LANES, cols // LANES
    rowsum = [lane_fold(rowacc_ref[q * LANES : (q + 1) * LANES, :], jnp.sum) for q in range(nq)]
    rowsum = jnp.concatenate(rowsum, axis=0)
    colsum = colsum_ref[...]
    low = jnp.minimum(jnp.min(rowsum), jnp.min(colsum))
    high = jnp.maximum(jnp.max(rowsum), jnp.max(colsum))
    good = jnp.logical_and(low >= LOW, high <= HIGH)
    peak = peak_ref[0:1, :]

    @pl.when(good)
    def _():
        lrow_ref[...] = (jnp.log2(rowsum) + peak) - v_ref[...]
        lcol_ref[...] = (jnp.log2(colsum) + peak) - u_ref[...]

    @pl.when(jnp.logical_not(good))
    def _():
        spread(v_ref, vs_ref, nq)
        for q in range(nq):
            part = slice(q * LANES, (q + 1) * LANES)

            def row_peak(c, best):
                at = pl.ds(pl.multiple_of(c * LANES, LANES), LANES)
                return jnp.maximum(best, d_ref[part, at] + u_ref[pl.ds(c, 1), :])

            best = lax.fori_loop(0, nc, row_peak, jnp.full((LANES, LANES), -3.0e38, F32))
            top = jnp.max(best, axis=1, keepdims=True)

            def row_sum(c, acc):
                at = pl.ds(pl.multiple_of(c * LANES, LANES), LANES)
                return acc + jnp.exp2((d_ref[part, at] + u_ref[pl.ds(c, 1), :]) - top)

            acc = lax.fori_loop(0, nc, row_sum, jnp.zeros((LANES, LANES), F32))
            log_sum = jnp.log2(jnp.sum(acc, axis=1, keepdims=True)) + top
            lrow_ref[q : q + 1, :] = lane_fold(jnp.broadcast_to(log_sum, (LANES, LANES)), jnp.max)

        def column(c, carry):
            at = pl.ds(pl.multiple_of(c * LANES, LANES), LANES)
            val = d_ref[:, at] + vs_ref[...]
            top = jnp.max(val, axis=0, keepdims=True)
            lcol_ref[pl.ds(c, 1), :] = top + jnp.log2(jnp.sum(jnp.exp2(val - top), axis=0, keepdims=True))
            return carry

        lax.fori_loop(0, nc, column, 0)


def start_peak(d_ref, u0, v_ref, vs_ref, peak_ref, rowacc_ref):
    rows = d_ref.shape[0]
    spread(v_ref, vs_ref, rows // LANES)
    peak = jnp.broadcast_to(tile_peak(d_ref, u0, vs_ref), (8, LANES))
    peak_ref[...] = peak
    vs_ref[...] = vs_ref[...] - peak[0:1, :]
    rowacc_ref[...] = jnp.zeros_like(rowacc_ref)


def first_kernel(
    gen_ref, ref_ref, glog_ref, rlog_ref, d_hbm, lrow_ref, lcol_ref, hrow_ref, hcol_ref,
    d_ref, u_ref, v_ref, vs_ref, rowacc_ref, colsum_ref, peak_ref, sem,
):
    rows, width = gen_ref.shape
    chunks = TILE // LANES
    j = pl.program_id(0)
    steps = pl.num_programs(0)
    half_scale = 0.5 * LOG2E / (EPS * width)
    dot_scale = LOG2E / (EPS * width)
    base = pl.multiple_of(j * TILE, TILE)

    @pl.when(j == 0)
    def _():
        for q, part in enumerate(norms(gen_ref, 0, rows // LANES, half_scale)):
            hrow_ref[q : q + 1, :] = part
            v_ref[q : q + 1, :] = glog_ref[q : q + 1, :] - part

    half = norms(ref_ref, 0, chunks, half_scale)
    u = []
    for c in range(chunks):
        row = pl.ds(j * chunks + c, 1)
        hcol_ref[row, :] = half[c]
        u.append(rlog_ref[row, :] - half[c])
        u_ref[row, :] = u[c]
    dots = lax.dot_general(
        gen_ref[...], ref_ref[...], (((1,), (1,)), ((), ())), preferred_element_type=F32
    )
    d_ref[:, pl.ds(base, TILE)] = dots * dot_scale
    view = d_ref.at[:, pl.ds(base, TILE)]
    pltpu.make_async_copy(view, d_hbm.at[:, pl.ds(base, TILE)], sem.at[j]).start()

    @pl.when(j == 0)
    def _():
        start_peak(view, u[0], v_ref, vs_ref, peak_ref, rowacc_ref)

    for c, part in enumerate(sweep(view, 0, chunks, u, vs_ref, rowacc_ref)):
        colsum_ref[pl.ds(j * chunks + c, 1), :] = part

    @pl.when(j == steps - 1)
    def _():
        finish(d_ref, u_ref, v_ref, vs_ref, rowacc_ref, colsum_ref, peak_ref, lrow_ref, lcol_ref)
        for t in range(d_ref.shape[1] // TILE):
            part = pl.ds(t * TILE, TILE)
            pltpu.make_async_copy(d_ref.at[:, part], d_hbm.at[:, part], sem.at[t]).wait()


def first_pass(gen, ref, glog, rlog, piece, pieces):
    rows, width = gen.shape
    cols = ref.shape[0] // pieces
    nq, nc = rows // LANES, cols // LANES
    offset = piece * (cols // TILE)
    whole = lambda shape: pl.BlockSpec(shape, lambda j: (0, 0))
    vec = lambda n: jax.ShapeDtypeStruct((n, LANES), F32)
    return pl.pallas_call(
        first_kernel,
        grid=(cols // TILE,),
        in_specs=[
            whole((rows, width)),
            pl.BlockSpec((TILE, width), lambda j: (j + offset, 0)),
            whole((nq, LANES)),
            pl.BlockSpec((nc, LANES), lambda j: (piece, 0)),
        ],
        out_shape=(jax.ShapeDtypeStruct((rows, cols), F32), vec(nq), vec(nc), vec(nq), vec(nc)),
        out_specs=(
            pl.BlockSpec(memory_space=pltpu.HBM),
            whole((nq, LANES)),
            whole((nc, LANES)),
            whole((nq, LANES)),
            whole((nc, LANES)),
        ),
        scratch_shapes=[
            pltpu.VMEM((rows, cols), F32),
            pltpu.VMEM((nc, LANES), F32),
            pltpu.VMEM((nq, LANES), F32),
            pltpu.VMEM((rows, LANES), F32),
            pltpu.VMEM((rows, LANES), F32),
            pltpu.VMEM((nc, LANES), F32),
            pltpu.VMEM((8, LANES), F32),
            pltpu.SemaphoreType.DMA((cols // TILE,)),
        ],
        compiler_params=pltpu.CompilerParams(vmem_limit_bytes=32 << 20),
        name=f"cross_first_{piece}",
    )(gen, ref, glog, rlog)


def load_tiles(sources, dst_ref, sem, tile):
    copies = []
    for src in sources:
        for t in range(src.shape[1] // tile):
            at = len(copies)
            copies.append(
                pltpu.make_async_copy(
                    src.at[:, pl.ds(t * tile, tile)], dst_ref.at[:, pl.ds(at * tile, tile)], sem.at[at]
                )
            )
            copies[-1].start()
    return copies


def next_kernel(count, *refs):
    sources = refs[:count]
    u_ref, v_ref, lrow_ref, lcol_ref, d_ref, vs_ref, rowacc_ref, colsum_ref, peak_ref, sem = refs[count:]
    chunks = TILE // LANES
    copies = load_tiles(sources, d_ref, sem, TILE)
    for t, copy in enumerate(copies):
        copy.wait()
        if t == 0:
            start_peak(d_ref, u_ref[0:1, :], v_ref, vs_ref, peak_ref, rowacc_ref)
        u = [u_ref[t * chunks + c : t * chunks + c + 1, :] for c in range(chunks)]
        for c, part in enumerate(sweep(d_ref, t * TILE, chunks, u, vs_ref, rowacc_ref)):
            colsum_ref[t * chunks + c : t * chunks + c + 1, :] = part
    finish(d_ref, u_ref, v_ref, vs_ref, rowacc_ref, colsum_ref, peak_ref, lrow_ref, lcol_ref)


def next_pass(parts, u, v, name):
    rows = parts[0].shape[0]
    cols = sum(part.shape[1] for part in parts)
    nq, nc = rows // LANES, cols // LANES
    vmem = pl.BlockSpec(memory_space=pltpu.VMEM)
    return pl.pallas_call(
        functools.partial(next_kernel, len(parts)),
        in_specs=[pl.BlockSpec(memory_space=pltpu.HBM)] * len(parts) + [vmem, vmem],
        out_shape=(jax.ShapeDtypeStruct((nq, LANES), F32), jax.ShapeDtypeStruct((nc, LANES), F32)),
        out_specs=(vmem, vmem),
        scratch_shapes=[
            pltpu.VMEM((rows, cols), F32),
            pltpu.VMEM((rows, LANES), F32),
            pltpu.VMEM((rows, LANES), F32),
            pltpu.VMEM((nc, LANES), F32),
            pltpu.VMEM((8, LANES), F32),
            pltpu.SemaphoreType.DMA((cols // TILE,)),
        ],
        compiler_params=pltpu.CompilerParams(vmem_limit_bytes=32 << 20),
        name=name,
    )(*parts, u, v)


def self_first_kernel(count, first, *refs):
    own_hbm, mate_hbm = refs[:2]
    sources = refs[2 : 2 + count]
    half_ref, weight_ref, place_ref, e_hbm, z_ref = refs[2 + count : 7 + count]
    rows_ref, piece_ref, e_ref, hs_ref, ws_ref, sem = refs[7 + count :]
    rows, width = rows_ref.shape
    half = rows // 2
    tall = piece_ref.shape[0] // count
    chunks = tall // LANES
    half_scale = 0.5 * LOG2E / (EPS * width)
    dot_scale = LOG2E / (EPS * width)
    loads = [
        pltpu.make_async_copy(own_hbm, rows_ref.at[:half, :], sem.at[0]),
        pltpu.make_async_copy(mate_hbm, rows_ref.at[half:, :], sem.at[1]),
    ]
    for t, src in enumerate(sources):
        loads.append(pltpu.make_async_copy(src, piece_ref.at[t * tall : (t + 1) * tall, :], sem.at[2 + t]))
    for copy in loads:
        copy.start()
    spread(half_ref, hs_ref, rows // LANES)
    spread(weight_ref, ws_ref, rows // LANES)
    z_ref[...] = jnp.zeros_like(z_ref)
    stores = []
    zero = jnp.zeros((8, LANES), F32)
    loads[0].wait()
    loads[1].wait()
    for t in range(count):
        loads[2 + t].wait()
        base = t * tall
        piece_half = norms(piece_ref, base, chunks, half_scale)
        piece = piece_ref[base : base + tall, :]
        e_ref[:, base : base + tall] = lax.dot_general(
            rows_ref[...], piece, (((1,), (1,)), ((), ())), preferred_element_type=F32
        )

        def body(r, acc):
            at = pl.ds(pl.multiple_of(r * ROWS, ROWS), ROWS)
            hs = hs_ref[at, :]
            ws = ws_ref[at, :]
            out = []
            for c in range(chunks):
                part = slice(base + c * LANES, base + (c + 1) * LANES)
                e = jnp.exp2(e_ref[at, part] * dot_scale - (hs + piece_half[c]))
                e_ref[at, part] = e
                out.append(acc[c] + jnp.sum((e * ws).reshape(ROWS // 8, 8, LANES), axis=0))
            return tuple(out)

        acc = lax.fori_loop(0, rows // ROWS, body, (zero,) * chunks, unroll=2)
        for c in range(chunks):
            z_ref[pl.ds(place_ref[first + t * chunks + c], 1), :] = jnp.sum(acc[c], axis=0, keepdims=True)
        part = slice(base, base + tall)
        stores.append(pltpu.make_async_copy(e_ref.at[:, part], e_hbm.at[:, part], sem.at[2 + count + t]))
        stores[-1].start()
    for copy in stores:
        copy.wait()


def self_first(own, mate, sources, half, weight, place, first):
    rows, width = 2 * own.shape[0], own.shape[1]
    count, tall = len(sources), sources[0].shape[0]
    cols = count * tall
    hbm = pl.BlockSpec(memory_space=pltpu.HBM)
    vmem = pl.BlockSpec(memory_space=pltpu.VMEM)
    return pl.pallas_call(
        functools.partial(self_first_kernel, count, first),
        in_specs=[hbm] * (2 + count) + [vmem, vmem, pl.BlockSpec(memory_space=pltpu.SMEM)],
        out_shape=(
            jax.ShapeDtypeStruct((rows, cols), F32),
            jax.ShapeDtypeStruct((place.shape[0], LANES), F32),
        ),
        out_specs=(hbm, vmem),
        scratch_shapes=[
            pltpu.VMEM((rows, width), jnp.bfloat16),
            pltpu.VMEM((cols, width), jnp.bfloat16),
            pltpu.VMEM((rows, cols), F32),
            pltpu.VMEM((rows, LANES), F32),
            pltpu.VMEM((rows, LANES), F32),
            pltpu.SemaphoreType.DMA((2 + 2 * count,)),
        ],
        compiler_params=pltpu.CompilerParams(vmem_limit_bytes=32 << 20),
        name=f"self_first_{first}",
    )(own, mate, *sources, half, weight, place)


def self_cols_kernel(count, *refs):
    w_ref, place_ref, z_ref, e_ref, ws_ref, sem = refs[count:]
    rows = e_ref.shape[0]
    chunks = 256 // LANES
    copies = load_tiles(refs[:count], e_ref, sem, 256)
    spread(w_ref, ws_ref, rows // LANES)
    zero = jnp.zeros((8, LANES), F32)
    for t, copy in enumerate(copies):
        copy.wait()

        def body(r, acc):
            at = pl.ds(pl.multiple_of(r * ROWS, ROWS), ROWS)
            ws = ws_ref[at, :]
            out = []
            for c in range(chunks):
                e = e_ref[at, t * 256 + c * LANES : t * 256 + (c + 1) * LANES] * ws
                out.append(acc[c] + jnp.sum(e.reshape(ROWS // 8, 8, LANES), axis=0))
            return tuple(out)

        acc = lax.fori_loop(0, rows // ROWS, body, (zero,) * chunks, unroll=4)
        for c in range(chunks):
            z_ref[pl.ds(place_ref[t * chunks + c], 1), :] = jnp.sum(acc[c], axis=0, keepdims=True)


def self_rows_kernel(count, *refs):
    w_ref, place_ref, y_ref, e_ref, rowacc_ref, sem = refs[count:]
    rows = e_ref.shape[0]
    chunks = 256 // LANES
    copies = load_tiles(refs[:count], e_ref, sem, 256)
    rowacc_ref[...] = jnp.zeros_like(rowacc_ref)
    for t, copy in enumerate(copies):
        copy.wait()
        w = [w_ref[pl.ds(place_ref[t * chunks + c], 1), :] for c in range(chunks)]

        def body(r, carry):
            at = pl.ds(pl.multiple_of(r * ROWS, ROWS), ROWS)
            acc = rowacc_ref[at, :]
            for c in range(chunks):
                acc = acc + e_ref[at, t * 256 + c * LANES : t * 256 + (c + 1) * LANES] * w[c]
            rowacc_ref[at, :] = acc
            return carry

        lax.fori_loop(0, rows // ROWS, body, 0, unroll=4)
    for q in range(rows // LANES):
        y_ref[q : q + 1, :] = lane_fold(rowacc_ref[q * LANES : (q + 1) * LANES, :], jnp.sum)


def self_apply(kernel, name, parts, w, place, out_rows):
    rows = parts[0].shape[0]
    cols = sum(part.shape[1] for part in parts)
    vmem = pl.BlockSpec(memory_space=pltpu.VMEM)
    return pl.pallas_call(
        functools.partial(kernel, len(parts)),
        in_specs=[pl.BlockSpec(memory_space=pltpu.HBM)] * len(parts)
        + [vmem, pl.BlockSpec(memory_space=pltpu.SMEM)],
        out_shape=jax.ShapeDtypeStruct((out_rows, LANES), F32),
        out_specs=vmem,
        scratch_shapes=[
            pltpu.VMEM((rows, cols), F32),
            pltpu.VMEM((rows, LANES), F32),
            pltpu.SemaphoreType.DMA((cols // 256,)),
        ],
        compiler_params=pltpu.CompilerParams(vmem_limit_bytes=32 << 20),
        name=name,
    )(*parts, w, place)


def log_add(parts):
    top = functools.reduce(jnp.maximum, parts)
    return top + jnp.log2(sum(jnp.exp2(part - top) for part in parts))


def build(n_z, n_y, n_core, n_ref):
    n_zy = n_z * n_y
    n_gen = n_zy * n_core
    assert n_z == n_y == n_ref == 4 and n_core == 2

    def place_of(g):
        return g // (n_y * n_core), (g // n_core) % n_y, g % n_core

    def gen_perm(move):
        out = []
        for g in range(n_gen):
            z, y, c = move(*place_of(g))
            out.append((g, ((z % n_z) * n_y + y % n_y) * n_core + c % n_core))
        return out

    core_stage = [gen_perm(lambda z, y, c: (z, y, c + 1))]
    y_stage = [gen_perm(lambda z, y, c: (z, y + k, c)) for k in (1, 2, 3)]
    z_stage = [gen_perm(lambda z, y, c: (z + k, y, c)) for k in (1, 2, 3)]
    ref_stage = [[(i, (i + k) % n_ref) for i in range(n_ref)] for k in (1, 2, 3)]
    first_axis = {k: gen_perm(lambda z, y, c: (z, y + k, c) if c == 0 else (z + k, y, c)) for k in (1, 2, 3)}
    second_axis = {k: gen_perm(lambda z, y, c: (z + k, y, c) if c == 0 else (z, y + k, c)) for k in (1, 3)}
    order = [(0, 0), (0, 1), (0, 2), (0, 3)]
    order += [(1, 0), (1, 1), (3, 2), (3, 3), (1, 2), (1, 3), (3, 0), (3, 1)]
    order += [(2, 0), (2, 1), (2, 2), (2, 3)]

    def shift(value, axis, perms):
        return [lax.ppermute(value, axis, perm) for perm in perms]

    def merge(parts, logs):
        top = log_add([part[:logs] for part in parts])
        if parts[0].shape[0] == logs:
            return top
        return jnp.concatenate([top, sum(part[logs:] for part in parts)], axis=0)

    def stage(value, axis, perms, logs):
        return merge([value] + shift(value, axis, perms), logs)

    def per_device(gen_features, gen_weight, ref_features, ref_weight, ref_self):
        gen_count = gen_features.shape[0]
        ref_count = ref_features.shape[0]
        nq, nc = gen_count // LANES, ref_count // LANES
        g = lax.axis_index("gen")
        x = lax.axis_index("ref")
        z, y, core = place_of(g)
        zy = z * n_y + y
        rows_of = lambda value, at, count: lax.dynamic_slice_in_dim(value, at, count, 0)
        place = []
        for b, a in order:
            mine = ((z - b) % n_z) * n_y + (y - a) % n_y
            other = ((z - a) % n_z) * n_y + (y - b) % n_y
            place.append(jnp.where(core == 0, mine, other))
        place = jnp.stack(place).astype(jnp.int32)

        with jax.named_scope("gather"):
            own = rows_of(gen_features, x * LANES, LANES)
            mate = lax.ppermute(gen_features, "gen", core_stage[0])
            got = [lax.ppermute(own, "gen", first_axis[k]) for k in (1, 2, 3)]
            low = jnp.concatenate([own, got[0]], axis=0)
            high = jnp.concatenate([got[1], got[2]], axis=0)
            low_up = lax.ppermute(low, "gen", second_axis[1])
            high_down = lax.ppermute(high, "gen", second_axis[3])
            high_up = lax.ppermute(high, "gen", second_axis[1])
            low_down = lax.ppermute(low, "gen", second_axis[3])
            low_far = lax.ppermute(low_up, "gen", second_axis[1])
            high_far = lax.ppermute(high_down, "gen", second_axis[3])

        wg = gen_weight.reshape(nq, LANES)
        wr = ref_weight.reshape(nc, LANES)
        glog = jnp.log2(wg)
        rlog = jnp.log2(wr)
        at_zy = lax.broadcasted_iota(jnp.int32, (n_zy, LANES), 0) == zy
        at_x = lax.broadcasted_iota(jnp.int32, (n_ref, LANES), 0) == x

        def to_cols(rows):
            return jnp.where(at_zy, rows_of(rows, x, 1), 0.0)

        def to_rows(cols):
            return jnp.where(at_x, rows_of(cols, zy, 1), 0.0)

        d0, lrow0, lcol0, hrow, hcol0 = first_pass(gen_features, ref_features, glog, rlog, 0, 2)
        d1, lrow1, lcol1, _, hcol1 = first_pass(gen_features, ref_features, glog, rlog, 1, 2)
        hcol = jnp.concatenate([hcol0, hcol1], axis=0)
        hw = jnp.concatenate([hrow, wg], axis=0)
        mate_hw = lax.ppermute(hw, "gen", core_stage[0])
        half = jnp.concatenate([hrow, mate_hw[:nq]], axis=0)
        weight = jnp.concatenate([wg, mate_hw[nq:]], axis=0)
        e0, z1_0 = self_first(gen_features, mate, [low, high], half, weight, place, 0)
        e1, z1_1 = self_first(
            gen_features, mate, [low_up, high_down, high_up, low_down], half, weight, place, 4
        )
        e2, z1_2 = self_first(gen_features, mate, [low_far, high_far], half, weight, place, 12)
        e = [e0, e1, e2]

        with jax.named_scope("round1"):
            row_part = jnp.concatenate([log_add([lrow0, lrow1]), jnp.full((nq, LANES), jnp.sum(wr))], axis=0)
            row_part = stage(row_part, "ref", ref_stage, nq)
            col_part = jnp.concatenate([lcol0, lcol1, jnp.full((8, LANES), jnp.sum(wg))], axis=0)
            col_part = stage(col_part, "gen", core_stage, nc)
            col_part = jnp.concatenate([col_part, to_cols(wg)], axis=0)
            col_part = stage(col_part, "gen", y_stage, nc)
            col_part = stage(col_part, "gen", z_stage, nc)
            gmass = col_part[nc : nc + 1]
            rmass = row_part[nq : nq + 1]
            wcols = col_part[nc + 8 :] / gmass
        gmass_log = jnp.log2(gmass)
        rmass_log = jnp.log2(rmass)
        f = hrow - (row_part[:nq] - rmass_log)
        c = hcol - (col_part[:nc] - gmass_log)
        ubase = rlog - rmass_log - hcol
        vbase = glog - gmass_log - hrow
        share = wg / gmass

        with jax.named_scope("round2"):
            lrow, lcol = next_pass([d0, d1], ubase + c, vbase + f, "cross_second")
            lrow = stage(lrow, "ref", ref_stage, nq)
            lcol = stage(lcol, "gen", core_stage, nc)
            col_part = jnp.concatenate([lcol, z1_0 + z1_1 + z1_2], axis=0)
            col_part = stage(col_part, "gen", y_stage, nc)
            col_part = stage(col_part, "gen", z_stage, nc)
            f = 0.5 * (f + (hrow - lrow))
            c = 0.5 * (c + (hcol - col_part[:nc]))
            y1 = col_part[nc:] / gmass

        with jax.named_scope("round3"):
            lrow, lcol = next_pass([d0, d1], ubase + c, vbase + f, "cross_third")
            y2 = self_apply(self_rows_kernel, "self_rows", e, wcols / y1, place, 2 * nq)
            row_part = jnp.concatenate([lrow, y2, to_rows(-jnp.log2(y1))], axis=0)
            row_part = stage(row_part, "ref", ref_stage, nq)
            f = 0.5 * (f + (hrow - row_part[:nq]))
            f_part = jnp.full((8, LANES), jnp.sum(share * f))
            mine = jnp.concatenate([lcol, f_part, row_part[nq:]], axis=0)
            theirs = shift(mine, "gen", core_stage)[0]
            lcol = log_add([lcol, theirs[:nc]])
            f_part = f_part + theirs[nc : nc + 8]
            y2, y2_mate, s1 = row_part[nq : 2 * nq], row_part[2 * nq : 3 * nq], row_part[3 * nq :]
            at = nc + 8
            y2 = y2 + theirs[at + nq : at + 2 * nq]
            y2_mate = y2_mate + theirs[at : at + nq]
            s2 = 0.5 * (jnp.concatenate([s1, theirs[at + 2 * nq :]], axis=0) - jnp.log2(jnp.concatenate([y2, y2_mate], axis=0)))
            w3 = weight / gmass * jnp.exp2(s2)
            z3 = self_apply(self_cols_kernel, "self_cols", e, w3, place, n_zy)
            col_part = jnp.concatenate([lcol, f_part, z3, to_cols(s2)], axis=0)
            col_part = stage(col_part, "gen", y_stage, nc)
            col_part = stage(col_part, "gen", z_stage, nc)
            c = 0.5 * (c + (hcol - col_part[:nc]))
            f_part = col_part[nc : nc + 8]
            z3, s2 = col_part[nc + 8 : nc + 8 + n_zy], col_part[nc + 8 + n_zy :]

        with jax.named_scope("last"):
            unit = EPS / LOG2E
            ref_gap = c * unit - ref_self.reshape(nc, LANES)
            s3 = 0.5 * (s2 - jnp.log2(z3))
            s_part = jnp.full((8, LANES), jnp.sum(wcols * s3))
            s_part = s_part + shift(s_part, "gen", core_stage)[0]
            part = jnp.sum((wr / rmass) * ref_gap) - unit * s_part
            row_part = jnp.concatenate([to_rows(s3), part], axis=0)
            row_part = row_part + sum(shift(row_part, "ref", ref_stage))
            gen_gap = (f - row_part[:nq]) * unit
            divergence = (unit * f_part + row_part[nq:])[0, 0]
        return gen_gap.reshape(gen_count), ref_gap.reshape(ref_count), divergence

    return per_device


def solution(mesh):
    n_gen, n_ref = mesh.shape["gen"], mesh.shape["ref"]
    n_core = 2
    n_y = 1
    while n_y * n_y * n_core < n_gen:
        n_y *= 2
    placed = (P("gen", None), P("gen"), P("ref", None), P("ref"), P("ref"))
    return jax.shard_map(
        build(n_gen // (n_y * n_core), n_y, n_core, n_ref),
        mesh=mesh,
        in_specs=placed,
        out_specs=(P("gen"), P("ref"), P()),
        check_vma=False,
    )
```

```python
import functools

import jax
import jax.numpy as jnp
from jax import lax
from jax.experimental import pallas as pl
from jax.experimental.pallas import tpu as pltpu
from jax.sharding import PartitionSpec as P


EPS = 0.1
LOG2E = 1.4426950408889634
F32 = jnp.float32
LANES = 128
TILE = 512
ROWS = 32
LOW = 2.0**-80
HIGH = 2.0**120


def vmem_array(x):
    return pltpu.with_memory_space_constraint(x, pltpu.VMEM)


def hbm_array(x):
    return pltpu.with_memory_space_constraint(x, pltpu.HBM)


def spread(vec_ref, out_ref, count, first=0, at=0):
    for q in range(count):
        block = jnp.broadcast_to(vec_ref[first + q : first + q + 1, :], (LANES, LANES))
        out_ref[(at + q) * LANES : (at + q + 1) * LANES, :] = block.T


def lane_fold(acc, op):
    return op(acc.T, axis=0, keepdims=True)


def norms(feat_ref, start, count, scale):
    width = feat_ref.shape[1]
    out = []
    for q in range(count):
        acc = jnp.zeros((LANES, LANES), F32)
        for c in range(width // LANES):
            x = feat_ref[start + q * LANES : start + (q + 1) * LANES, c * LANES : (c + 1) * LANES].astype(F32)
            acc = acc + x * x
        out.append(lane_fold(acc, jnp.sum) * scale)
    return out


def sweep(d_ref, base, chunks, u, vs_ref, rowacc_ref):
    rows = d_ref.shape[0]

    def body(r, cols):
        at = pl.ds(pl.multiple_of(r * ROWS, ROWS), ROWS)
        vs = vs_ref[at, :]
        racc = rowacc_ref[at, :]
        out = []
        for c in range(chunks):
            p = jnp.exp2((d_ref[at, pl.ds(base + c * LANES, LANES)] + u[c]) + vs)
            racc = racc + p
            out.append(cols[c] + jnp.sum(p.reshape(ROWS // 8, 8, LANES), axis=0))
        rowacc_ref[at, :] = racc
        return tuple(out)

    zero = jnp.zeros((8, LANES), F32)
    cols = lax.fori_loop(0, rows // ROWS, body, (zero,) * chunks, unroll=2)
    return [jnp.sum(c, axis=0, keepdims=True) for c in cols]


def tile_peak(d_ref, u, vs_ref):
    rows = d_ref.shape[0]
    best = jnp.full((8, LANES), -3.0e38, F32)

    def body(r, best):
        at = pl.ds(pl.multiple_of(r * ROWS, ROWS), ROWS)
        val = (d_ref[at, 0:LANES] + u) + vs_ref[at, :]
        return jnp.maximum(best, jnp.max(val.reshape(ROWS // 8, 8, LANES), axis=0))

    best = lax.fori_loop(0, rows // ROWS, body, best, unroll=2)
    return jnp.max(jnp.max(best, axis=0, keepdims=True), axis=1, keepdims=True)


def start_peak(d_ref, u0, v_ref, vs_ref, peak_ref, rowacc_ref):
    rows = d_ref.shape[0]
    spread(v_ref, vs_ref, rows // LANES)
    peak = jnp.broadcast_to(tile_peak(d_ref, u0, vs_ref), (8, LANES))
    peak_ref[...] = peak
    vs_ref[...] = vs_ref[...] - peak[0:1, :]
    rowacc_ref[...] = jnp.zeros_like(rowacc_ref)


def finish(d_refs, u_ref, v_ref, vs_ref, rowacc_ref, colsum_ref, peak_ref, lrow_ref, lcol_ref):
    rows = d_refs[0].shape[0]
    nq = rows // LANES
    rowsum = [lane_fold(rowacc_ref[q * LANES : (q + 1) * LANES, :], jnp.sum) for q in range(nq)]
    rowsum = jnp.concatenate(rowsum, axis=0)
    colsum = colsum_ref[...]
    low = jnp.minimum(jnp.min(rowsum), jnp.min(colsum))
    high = jnp.maximum(jnp.max(rowsum), jnp.max(colsum))
    good = jnp.logical_and(low >= LOW, high <= HIGH)
    peak = peak_ref[0:1, :]

    @pl.when(good)
    def _():
        lrow_ref[0:nq, :] = (jnp.log2(rowsum) + peak) - v_ref[...]
        lcol_ref[...] = (jnp.log2(colsum) + peak) - u_ref[...]

    @pl.when(jnp.logical_not(good))
    def _():
        spread(v_ref, vs_ref, nq)

        def row_block(q, carry):
            part = pl.ds(pl.multiple_of(q * LANES, LANES), LANES)

            def scores(d_ref, first, c):
                at = pl.ds(pl.multiple_of(c * LANES, LANES), LANES)
                return d_ref[part, at] + u_ref[pl.ds(first + c, 1), :]

            best = jnp.full((LANES, LANES), -3.0e38, F32)
            first = 0
            for d_ref in d_refs:
                count = d_ref.shape[1] // LANES
                best = lax.fori_loop(
                    0, count, lambda c, best: jnp.maximum(best, scores(d_ref, first, c)), best
                )
                first += count
            top = jnp.max(best, axis=1, keepdims=True)
            acc = jnp.zeros((LANES, LANES), F32)
            first = 0
            for d_ref in d_refs:
                count = d_ref.shape[1] // LANES
                acc = lax.fori_loop(
                    0, count, lambda c, acc: acc + jnp.exp2(scores(d_ref, first, c) - top), acc
                )
                first += count
            log_sum = jnp.log2(jnp.sum(acc, axis=1, keepdims=True)) + top
            lrow_ref[pl.ds(q, 1), :] = lane_fold(jnp.broadcast_to(log_sum, (LANES, LANES)), jnp.max)
            return carry

        lax.fori_loop(0, nq, row_block, 0)
        first = 0
        for d_ref in d_refs:
            count = d_ref.shape[1] // LANES

            def column(c, carry):
                at = pl.ds(pl.multiple_of(c * LANES, LANES), LANES)

                def block(r):
                    part = pl.ds(pl.multiple_of(r * ROWS, ROWS), ROWS)
                    return d_ref[part, at] + vs_ref[part, :]

                top = lax.fori_loop(
                    0,
                    rows // ROWS,
                    lambda r, best: jnp.maximum(best, jnp.max(block(r), axis=0, keepdims=True)),
                    jnp.full((1, LANES), -3.0e38, F32),
                )
                total = lax.fori_loop(
                    0,
                    rows // ROWS,
                    lambda r, acc: acc + jnp.sum(jnp.exp2(block(r) - top), axis=0, keepdims=True),
                    jnp.zeros((1, LANES), F32),
                )
                lcol_ref[pl.ds(first + c, 1), :] = top + jnp.log2(total)
                return carry

            lax.fori_loop(0, count, column, 0)
            first += count


def first_kernel(
    offset, gen_ref, ref_hbm, gweight_ref, rweight_ref, d_ref, lrow_ref, lcol_ref, hrow_ref, hcol_ref, mass_ref,
    tile_ref, u_ref, v_ref, vs_ref, rowacc_ref, colsum_ref, peak_ref, sem,
):
    rows, width = gen_ref.shape
    nq, nc = rows // LANES, d_ref.shape[1] // LANES
    chunks = TILE // LANES
    steps = d_ref.shape[1] // TILE
    half_scale = 0.5 * LOG2E / (EPS * width)
    dot_scale = LOG2E / (EPS * width)

    def load(j, slot):
        at = pl.ds(pl.multiple_of((offset * steps + j) * TILE, TILE), TILE)
        return pltpu.make_async_copy(ref_hbm.at[at, :], tile_ref.at[slot], sem.at[slot])

    load(0, 0).start()
    for q, part in enumerate(norms(gen_ref, 0, nq, half_scale)):
        hrow_ref[q : q + 1, :] = part
        v_ref[q : q + 1, :] = jnp.log2(gweight_ref[q : q + 1, :]) - part
        hrow_ref[nq + q : nq + q + 1, :] = gweight_ref[q : q + 1, :]
    lrow_ref[nq : 2 * nq, :] = jnp.broadcast_to(jnp.sum(rweight_ref[...]).reshape(1, 1), (nq, LANES))
    mass_ref[...] = jnp.broadcast_to(jnp.sum(gweight_ref[...]).reshape(1, 1), (8, LANES))

    def step(j, carry):
        slot = lax.rem(j, 2)

        @pl.when(j + 1 < steps)
        def _():
            load(j + 1, 1 - slot).start()

        load(j, slot).wait()
        tile = tile_ref.at[slot]
        half = norms(tile, 0, chunks, half_scale)
        u = []
        for c in range(chunks):
            row = pl.ds(j * chunks + c, 1)
            hcol_ref[row, :] = half[c]
            u.append(jnp.log2(rweight_ref[pl.ds(offset * nc + j * chunks + c, 1), :]) - half[c])
            u_ref[row, :] = u[c]
        base = pl.multiple_of(j * TILE, TILE)
        dots = lax.dot_general(
            gen_ref[...], tile[...], (((1,), (1,)), ((), ())), preferred_element_type=F32
        )
        d_ref[:, pl.ds(base, TILE)] = dots * dot_scale

        @pl.when(j == 0)
        def _():
            start_peak(d_ref, u[0], v_ref, vs_ref, peak_ref, rowacc_ref)

        for c, part in enumerate(sweep(d_ref, base, chunks, u, vs_ref, rowacc_ref)):
            colsum_ref[pl.ds(j * chunks + c, 1), :] = part
        return carry

    lax.fori_loop(0, steps, step, 0)
    finish([d_ref], u_ref, v_ref, vs_ref, rowacc_ref, colsum_ref, peak_ref, lrow_ref, lcol_ref)


def first_pass(gen, ref, gweight, rweight, piece, pieces):
    rows, width = gen.shape
    cols = ref.shape[0] // pieces
    nq, nc = rows // LANES, cols // LANES
    vmem = pl.BlockSpec(memory_space=pltpu.VMEM)
    vec = lambda n: jax.ShapeDtypeStruct((n, LANES), F32)
    return pl.pallas_call(
        functools.partial(first_kernel, piece),
        in_specs=[vmem, pl.BlockSpec(memory_space=pltpu.HBM), vmem, vmem],
        out_shape=(pltpu.VMEM((rows, cols), F32), vec(2 * nq), vec(nc), vec(2 * nq), vec(nc), vec(8)),
        out_specs=(vmem,) * 6,
        scratch_shapes=[
            pltpu.VMEM((2, TILE, width), jnp.bfloat16),
            pltpu.VMEM((nc, LANES), F32),
            pltpu.VMEM((nq, LANES), F32),
            pltpu.VMEM((rows, LANES), F32),
            pltpu.VMEM((rows, LANES), F32),
            pltpu.VMEM((nc, LANES), F32),
            pltpu.VMEM((8, LANES), F32),
            pltpu.SemaphoreType.DMA((2,)),
        ],
        compiler_params=pltpu.CompilerParams(vmem_limit_bytes=16 << 20),
    )(vmem_array(gen), hbm_array(ref), gweight, rweight)


def next_kernel(count, *refs):
    sources = refs[:count]
    u_ref, v_ref, lrow_ref, lcol_ref, vs_ref, rowacc_ref, colsum_ref, peak_ref = refs[count:]
    chunks = TILE // LANES
    start_peak(sources[0], u_ref[0:1, :], v_ref, vs_ref, peak_ref, rowacc_ref)
    first = 0
    for d_ref in sources:
        steps = d_ref.shape[1] // TILE

        def step(j, carry):
            u = [u_ref[pl.ds(first + j * chunks + c, 1), :] for c in range(chunks)]
            base = pl.multiple_of(j * TILE, TILE)
            for c, part in enumerate(sweep(d_ref, base, chunks, u, vs_ref, rowacc_ref)):
                colsum_ref[pl.ds(first + j * chunks + c, 1), :] = part
            return carry

        lax.fori_loop(0, steps, step, 0)
        first += steps * chunks
    finish(sources, u_ref, v_ref, vs_ref, rowacc_ref, colsum_ref, peak_ref, lrow_ref, lcol_ref)


def next_pass(parts, u, v):
    rows = parts[0].shape[0]
    cols = sum(part.shape[1] for part in parts)
    nq, nc = rows // LANES, cols // LANES
    vmem = pl.BlockSpec(memory_space=pltpu.VMEM)
    return pl.pallas_call(
        functools.partial(next_kernel, len(parts)),
        in_specs=[vmem] * (len(parts) + 2),
        out_shape=(jax.ShapeDtypeStruct((nq, LANES), F32), jax.ShapeDtypeStruct((nc, LANES), F32)),
        out_specs=(vmem, vmem),
        scratch_shapes=[
            pltpu.VMEM((rows, LANES), F32),
            pltpu.VMEM((rows, LANES), F32),
            pltpu.VMEM((nc, LANES), F32),
            pltpu.VMEM((8, LANES), F32),
        ],
        compiler_params=pltpu.CompilerParams(vmem_limit_bytes=8 << 20),
    )(*[vmem_array(part) for part in parts], u, v)


def self_first_kernel(count, first, *refs):
    own_ref, mate_ref = refs[:2]
    sources = refs[2 : 2 + count]
    mine_ref, theirs_ref, place_ref, e_ref, z_ref = refs[2 + count : 7 + count]
    piece_ref, hs_ref, ws_ref, sem = refs[7 + count :]
    half, width = own_ref.shape
    rows = 2 * half
    tall = piece_ref.shape[0] // count
    chunks = tall // LANES
    half_scale = 0.5 * LOG2E / (EPS * width)
    dot_scale = LOG2E / (EPS * width)

    def load(t, src):
        at = pl.ds(pl.multiple_of(t * tall, tall), tall)
        return pltpu.make_async_copy(src, piece_ref.at[at, :], sem.at[t])

    for t, src in enumerate(sources):
        load(t, src).start()
    nq = half // LANES
    for at, vec_ref in ((0, mine_ref), (nq, theirs_ref)):
        spread(vec_ref, hs_ref, nq, 0, at)
        spread(vec_ref, ws_ref, nq, nq, at)
    z_ref[...] = jnp.zeros_like(z_ref)
    zero = jnp.zeros((8, LANES), F32)

    def tile(t, carry):
        load(t, sources[0]).wait()
        base = pl.multiple_of(t * tall, tall)
        view = piece_ref.at[pl.ds(base, tall), :]
        piece_half = norms(view, 0, chunks, half_scale)
        for h, rows_ref in enumerate((own_ref, mate_ref)):
            e_ref[h * half : (h + 1) * half, pl.ds(base, tall)] = lax.dot_general(
                rows_ref[...], view[...], (((1,), (1,)), ((), ())), preferred_element_type=F32
            )

        def body(r, acc):
            at = pl.ds(pl.multiple_of(r * ROWS, ROWS), ROWS)
            hs = hs_ref[at, :]
            ws = ws_ref[at, :]
            out = []
            for c in range(chunks):
                part = pl.ds(base + c * LANES, LANES)
                e = jnp.exp2(e_ref[at, part] * dot_scale - (hs + piece_half[c]))
                e_ref[at, part] = e
                out.append(acc[c] + jnp.sum((e * ws).reshape(ROWS // 8, 8, LANES), axis=0))
            return tuple(out)

        acc = lax.fori_loop(0, rows // ROWS, body, (zero,) * chunks, unroll=2)
        for c in range(chunks):
            z_ref[pl.ds(place_ref[first + t * chunks + c], 1), :] = jnp.sum(acc[c], axis=0, keepdims=True)
        return carry

    lax.fori_loop(0, count, tile, 0)


def self_first(own, mate, sources, mine, theirs, place, first):
    rows, width = 2 * own.shape[0], own.shape[1]
    count, tall = len(sources), sources[0].shape[0]
    cols = count * tall
    vmem = pl.BlockSpec(memory_space=pltpu.VMEM)
    return pl.pallas_call(
        functools.partial(self_first_kernel, count, first),
        in_specs=[vmem, vmem]
        + [pl.BlockSpec(memory_space=pl.ANY)] * count
        + [vmem, vmem, pl.BlockSpec(memory_space=pltpu.SMEM)],
        out_shape=(pltpu.VMEM((rows, cols), F32), jax.ShapeDtypeStruct((place.shape[0], LANES), F32)),
        out_specs=(vmem, vmem),
        scratch_shapes=[
            pltpu.VMEM((cols, width), jnp.bfloat16),
            pltpu.VMEM((rows, LANES), F32),
            pltpu.VMEM((rows, LANES), F32),
            pltpu.SemaphoreType.DMA((count,)),
        ],
        compiler_params=pltpu.CompilerParams(vmem_limit_bytes=16 << 20),
    )(vmem_array(own), vmem_array(mate), *sources, mine, theirs, place)


def self_cols_kernel(count, *refs):
    w_ref, place_ref, z_ref, ws_ref = refs[count:]
    rows = refs[0].shape[0]
    chunks = 256 // LANES
    spread(w_ref, ws_ref, rows // LANES)
    zero = jnp.zeros((8, LANES), F32)
    first = 0
    for e_ref in refs[:count]:
        steps = e_ref.shape[1] // 256

        def tile(t, carry):
            base = pl.multiple_of(t * 256, 256)

            def body(r, acc):
                at = pl.ds(pl.multiple_of(r * ROWS, ROWS), ROWS)
                ws = ws_ref[at, :]
                out = []
                for c in range(chunks):
                    e = e_ref[at, pl.ds(base + c * LANES, LANES)] * ws
                    out.append(acc[c] + jnp.sum(e.reshape(ROWS // 8, 8, LANES), axis=0))
                return tuple(out)

            acc = lax.fori_loop(0, rows // ROWS, body, (zero,) * chunks, unroll=4)
            for c in range(chunks):
                z_ref[pl.ds(place_ref[first + t * chunks + c], 1), :] = jnp.sum(acc[c], axis=0, keepdims=True)
            return carry

        lax.fori_loop(0, steps, tile, 0)
        first += steps * chunks


def self_rows_kernel(count, *refs):
    w_ref, place_ref, y_ref, rowacc_ref = refs[count:]
    rows = refs[0].shape[0]
    chunks = 512 // LANES
    rowacc_ref[...] = jnp.zeros_like(rowacc_ref)
    first = 0
    for e_ref in refs[:count]:
        steps = e_ref.shape[1] // 512

        def tile(t, carry):
            base = pl.multiple_of(t * 512, 512)
            w = [w_ref[pl.ds(place_ref[first + t * chunks + c], 1), :] for c in range(chunks)]

            def body(r, carry):
                at = pl.ds(pl.multiple_of(r * ROWS, ROWS), ROWS)
                acc = rowacc_ref[at, :]
                for c in range(chunks):
                    acc = acc + e_ref[at, pl.ds(base + c * LANES, LANES)] * w[c]
                rowacc_ref[at, :] = acc
                return carry

            return lax.fori_loop(0, rows // ROWS, body, carry, unroll=4)

        lax.fori_loop(0, steps, tile, 0)
        first += steps * chunks
    for q in range(rows // LANES):
        y_ref[q : q + 1, :] = lane_fold(rowacc_ref[q * LANES : (q + 1) * LANES, :], jnp.sum)


def self_apply(kernel, parts, w, place, out_rows):
    rows = parts[0].shape[0]
    vmem = pl.BlockSpec(memory_space=pltpu.VMEM)
    return pl.pallas_call(
        functools.partial(kernel, len(parts)),
        in_specs=[vmem] * (len(parts) + 1) + [pl.BlockSpec(memory_space=pltpu.SMEM)],
        out_shape=jax.ShapeDtypeStruct((out_rows, LANES), F32),
        out_specs=vmem,
        scratch_shapes=[pltpu.VMEM((rows, LANES), F32)],
        compiler_params=pltpu.CompilerParams(vmem_limit_bytes=8 << 20),
    )(*[vmem_array(part) for part in parts], w, place)


def log_add(parts):
    top = functools.reduce(jnp.maximum, parts)
    return top + jnp.log2(sum(jnp.exp2(part - top) for part in parts))


def build(n_z, n_y, n_core, n_ref):
    n_zy = n_z * n_y
    n_gen = n_zy * n_core
    assert n_z == n_y == n_ref == 4 and n_core == 2

    def place_of(g):
        return g // (n_y * n_core), (g // n_core) % n_y, g % n_core

    def gen_perm(move):
        out = []
        for g in range(n_gen):
            z, y, c = move(*place_of(g))
            out.append((g, ((z % n_z) * n_y + y % n_y) * n_core + c % n_core))
        return out

    core_stage = [gen_perm(lambda z, y, c: (z, y, c + 1))]
    y_stage = [gen_perm(lambda z, y, c: (z, y + k, c)) for k in (1, 2, 3)]
    z_stage = [gen_perm(lambda z, y, c: (z + k, y, c)) for k in (1, 2, 3)]
    ref_stage = [[(i, (i + k) % n_ref) for i in range(n_ref)] for k in (1, 2, 3)]
    first_axis = {k: gen_perm(lambda z, y, c: (z, y + k, c) if c == 0 else (z + k, y, c)) for k in (1, 2, 3)}
    second_axis = {k: gen_perm(lambda z, y, c: (z + k, y, c) if c == 0 else (z, y + k, c)) for k in (1, 3)}
    order = [(0, 0), (0, 1), (0, 2), (0, 3)]
    order += [(1, 0), (1, 1), (1, 2), (1, 3), (3, 0), (3, 1), (3, 2), (3, 3)]
    order += [(2, 0), (2, 1), (2, 2), (2, 3)]

    def shift(value, axis, perms):
        return [lax.ppermute(value, axis, perm) for perm in perms]

    def merge(parts, logs):
        top = log_add([part[:logs] for part in parts])
        if parts[0].shape[0] == logs:
            return top
        return jnp.concatenate([top, sum(part[logs:] for part in parts)], axis=0)

    def stage(value, axis, perms, logs):
        return merge([value] + shift(value, axis, perms), logs)

    def run(gen_features, gen_weight, ref_features, ref_weight, ref_self):
        gen_count = gen_features.shape[0]
        ref_count = ref_features.shape[0]
        nq, nc = gen_count // LANES, ref_count // LANES
        g = lax.axis_index("gen")
        x = lax.axis_index("ref")
        z, y, core = place_of(g)
        zy = z * n_y + y
        b, a = (lax.broadcasted_iota(jnp.int32, (len(order),), 0) for _ in range(2))
        b = functools.reduce(lambda v, k: jnp.where(a == k, order[k][0], v), range(len(order)), b)
        a = a % 4
        mine = ((z - b + n_z) % n_z) * n_y + (y - a + n_y) % n_y
        other = ((z - a + n_z) % n_z) * n_y + (y - b + n_y) % n_y
        place = jnp.where(core == 0, mine, other)
        wg = gen_weight.reshape(nq, LANES)
        wr = ref_weight.reshape(nc, LANES)
        at_zy = (lax.broadcasted_iota(jnp.int32, (n_zy, LANES), 0) == zy).astype(F32)
        at_x = (lax.broadcasted_iota(jnp.int32, (n_ref, LANES), 0) == x).astype(F32)
        wg, place, at_zy, at_x = lax.optimization_barrier((wg, place, at_zy, at_x))

        def to_cols(rows):
            picked = jnp.sum(jnp.where(at_x > 0, rows, 0.0), axis=0, keepdims=True)
            return jnp.where(at_zy > 0, picked, 0.0)

        def to_rows(cols):
            picked = jnp.sum(jnp.where(at_zy > 0, cols, 0.0), axis=0, keepdims=True)
            return jnp.where(at_x > 0, picked, 0.0)

        own = lax.dynamic_slice_in_dim(gen_features, x * LANES, LANES, 0)
        got = [lax.ppermute(own, "gen", first_axis[k]) for k in (1, 2, 3)]
        mate = lax.ppermute(gen_features, "gen", core_stage[0])
        near = jnp.concatenate([own] + got, axis=0)
        up = lax.ppermute(near, "gen", second_axis[1])
        down = lax.ppermute(near, "gen", second_axis[3])
        low_far = lax.ppermute(up[: 2 * LANES], "gen", second_axis[1])
        high_far = lax.ppermute(down[2 * LANES :], "gen", second_axis[3])

        d0, row0, lcol0, mine, hcol0, gmass = first_pass(gen_features, ref_features, wg, wr, 0, 2)
        theirs = lax.ppermute(mine, "gen", core_stage[0])
        d1, row1, lcol1, _, hcol1, _ = first_pass(gen_features, ref_features, wg, wr, 1, 2)
        hcol = jnp.concatenate([hcol0, hcol1], axis=0)
        hrow = mine[:nq]
        weight = jnp.concatenate([wg, theirs[nq:]], axis=0)
        e0, z1_0 = self_first(gen_features, mate, [near], mine, theirs, place, 0)
        e1, z1_1 = self_first(gen_features, mate, [up, down], mine, theirs, place, 4)
        e2, z1_2 = self_first(gen_features, mate, [low_far, high_far], mine, theirs, place, 12)
        e = [e0, e1, e2]

        row_part = jnp.concatenate([log_add([row0[:nq], row1[:nq]]), row0[nq:]], axis=0)
        row_part = stage(row_part, "ref", ref_stage, nq)
        col_part = jnp.concatenate([lcol0, lcol1, gmass], axis=0)
        col_part = stage(col_part, "gen", core_stage, nc)
        col_part = jnp.concatenate([col_part, to_cols(wg)], axis=0)
        col_part = stage(col_part, "gen", y_stage, nc)
        col_part = stage(col_part, "gen", z_stage, nc)
        gmass = col_part[nc : nc + 1]
        rmass = row_part[nq : nq + 1]
        wcols = col_part[nc + 8 :] / gmass
        gmass_log = jnp.log2(gmass)
        rmass_log = jnp.log2(rmass)
        f = hrow - (row_part[:nq] - rmass_log)
        c = hcol - (col_part[:nc] - gmass_log)
        ubase = jnp.log2(wr) - rmass_log - hcol
        vbase = jnp.log2(wg) - gmass_log - hrow
        share = wg / gmass

        lrow, lcol = next_pass([d0, d1], ubase + c, vbase + f)
        lrow = stage(lrow, "ref", ref_stage, nq)
        lcol = stage(lcol, "gen", core_stage, nc)
        col_part = jnp.concatenate([lcol, z1_0 + z1_1 + z1_2], axis=0)
        col_part = stage(col_part, "gen", y_stage, nc)
        col_part = stage(col_part, "gen", z_stage, nc)
        f = 0.5 * (f + (hrow - lrow))
        c = 0.5 * (c + (hcol - col_part[:nc]))
        y1 = col_part[nc:] / gmass

        lrow, lcol = next_pass([d0, d1], ubase + c, vbase + f)
        y2 = self_apply(self_rows_kernel, e, wcols / y1, place, 2 * nq)
        row_part = jnp.concatenate([lrow, y2, to_rows(-jnp.log2(y1))], axis=0)
        row_part = stage(row_part, "ref", ref_stage, nq)
        f = 0.5 * (f + (hrow - row_part[:nq]))
        f_part = share * f
        f_part = jnp.concatenate([f_part, f_part], axis=0)
        mine = jnp.concatenate([lcol, f_part, row_part[nq:]], axis=0)
        theirs = shift(mine, "gen", core_stage)[0]
        lcol = log_add([lcol, theirs[:nc]])
        f_part = f_part + theirs[nc : nc + 8]
        y2, y2_mate, s1 = row_part[nq : 2 * nq], row_part[2 * nq : 3 * nq], row_part[3 * nq :]
        at = nc + 8
        y2 = y2 + theirs[at + nq : at + 2 * nq]
        y2_mate = y2_mate + theirs[at : at + nq]
        s1 = jnp.concatenate([s1, theirs[at + 2 * nq :]], axis=0)
        s2 = 0.5 * (s1 - jnp.log2(jnp.concatenate([y2, y2_mate], axis=0)))
        w3 = weight / gmass * jnp.exp2(s2)
        z3 = self_apply(self_cols_kernel, e, w3, place, n_zy)
        col_part = jnp.concatenate([lcol, f_part, z3, to_cols(s2[:nq])], axis=0)
        col_part = stage(col_part, "gen", y_stage, nc)
        col_part = stage(col_part, "gen", z_stage, nc)
        c = 0.5 * (c + (hcol - col_part[:nc]))
        f_part = col_part[nc : nc + nq]
        z3, s2 = col_part[nc + 8 : nc + 8 + n_zy], col_part[nc + 8 + n_zy :]

        unit = EPS / LOG2E
        ref_gap = c * unit - ref_self.reshape(nc, LANES)
        s3 = 0.5 * (s2 - jnp.log2(z3))
        s_part = jnp.sum((wcols * s3).reshape(2, 8, LANES), axis=0)
        s_part = s_part + shift(s_part, "gen", core_stage)[0]
        part = jnp.sum(((wr / rmass) * ref_gap).reshape(nc // 8, 8, LANES), axis=0) - unit * s_part
        row_part = jnp.concatenate([to_rows(s3), part], axis=0)
        row_part = row_part + sum(shift(row_part, "ref", ref_stage))
        gen_gap = (f - row_part[:nq]) * unit
        divergence = unit * jnp.sum(f_part) + jnp.sum(row_part[nq:])
        return gen_gap.reshape(gen_count), ref_gap.reshape(ref_count), divergence

    return run


def solution(mesh):
    n_gen, n_ref = mesh.shape["gen"], mesh.shape["ref"]
    n_core = 2
    n_y = 1
    while n_y * n_y * n_core < n_gen:
        n_y *= 2
    placed = (P("gen", None), P("gen"), P("ref", None), P("ref"), P("ref"))
    return jax.shard_map(
        build(n_gen // (n_y * n_core), n_y, n_core, n_ref),
        mesh=mesh,
        in_specs=placed,
        out_specs=(P("gen"), P("ref"), P()),
        check_vma=False,
    )
```

```python
import functools

import jax
import jax.numpy as jnp
from jax import lax
from jax.experimental import pallas as pl
from jax.experimental.pallas import tpu as pltpu
from jax.sharding import PartitionSpec as P


EPS = 0.1
LOG2E = 1.4426950408889634
F32 = jnp.float32
LANES = 128
TILE = 512
ROWS = 32
LOW = 2.0**-80
HIGH = 2.0**120


def vmem_array(x):
    return pltpu.with_memory_space_constraint(x, pltpu.VMEM)


def hbm_array(x):
    return pltpu.with_memory_space_constraint(x, pltpu.HBM)


def spread(vec_ref, out_ref, count, first=0, at=0):
    for q in range(count):
        block = jnp.broadcast_to(vec_ref[first + q : first + q + 1, :], (LANES, LANES))
        out_ref[(at + q) * LANES : (at + q + 1) * LANES, :] = block.T


def lane_fold(acc, op):
    return op(acc.T, axis=0, keepdims=True)


def norms(feat_ref, start, count, scale):
    width = feat_ref.shape[1]
    out = []
    for q in range(count):
        acc = jnp.zeros((LANES, LANES), F32)
        for c in range(width // LANES):
            x = feat_ref[start + q * LANES : start + (q + 1) * LANES, c * LANES : (c + 1) * LANES].astype(F32)
            acc = acc + x * x
        out.append(lane_fold(acc, jnp.sum) * scale)
    return out


def row_block(r):
    if isinstance(r, int):
        return slice(r * ROWS, (r + 1) * ROWS)
    return pl.ds(pl.multiple_of(r * ROWS, ROWS), ROWS)


def sweep(d_ref, base, chunks, u, vs_ref, rowacc_ref, straight=False, keep=None):
    rows = d_ref.shape[0]

    def body(r, cols):
        at = row_block(r)
        vs = vs_ref[at, :]
        racc = rowacc_ref[at, :]
        out = []
        for c in range(chunks):
            d = d_ref[at, pl.ds(base + c * LANES, LANES)]
            if keep is not None:
                keep[0][at, pl.ds(pl.multiple_of(keep[1] + c * LANES, LANES), LANES)] = d
            p = jnp.exp2((d + u[c]) + vs)
            racc = racc + p
            out.append(cols[c] + jnp.sum(p.reshape(ROWS // 8, 8, LANES), axis=0))
        rowacc_ref[at, :] = racc
        return tuple(out)

    cols = (jnp.zeros((8, LANES), F32),) * chunks
    if straight:
        for r in range(rows // ROWS):
            cols = body(r, cols)
    else:
        cols = lax.fori_loop(0, rows // ROWS, body, cols, unroll=2)
    return [jnp.sum(c, axis=0, keepdims=True) for c in cols]


def tile_peak(d_ref, u, vs_ref):
    rows = d_ref.shape[0]
    best = jnp.full((8, LANES), -3.0e38, F32)

    def body(r, best):
        at = pl.ds(pl.multiple_of(r * ROWS, ROWS), ROWS)
        val = (d_ref[at, 0:LANES] + u) + vs_ref[at, :]
        return jnp.maximum(best, jnp.max(val.reshape(ROWS // 8, 8, LANES), axis=0))

    best = lax.fori_loop(0, rows // ROWS, body, best, unroll=2)
    return jnp.max(jnp.max(best, axis=0, keepdims=True), axis=1, keepdims=True)


def start_peak(d_ref, u0, v_ref, vs_ref, peak_ref, rowacc_ref):
    rows = d_ref.shape[0]
    spread(v_ref, vs_ref, rows // LANES)
    peak = jnp.broadcast_to(tile_peak(d_ref, u0, vs_ref), (8, LANES))
    peak_ref[...] = peak
    vs_ref[...] = vs_ref[...] - peak[0:1, :]
    rowacc_ref[...] = jnp.zeros_like(rowacc_ref)


def finish(d_refs, u_ref, v_ref, vs_ref, rowacc_ref, colsum_ref, peak_ref, lrow_ref, lcol_ref):
    rows = d_refs[0].shape[0]
    nq = rows // LANES
    rowsum = [lane_fold(rowacc_ref[q * LANES : (q + 1) * LANES, :], jnp.sum) for q in range(nq)]
    rowsum = jnp.concatenate(rowsum, axis=0)
    colsum = colsum_ref[...]
    low = jnp.minimum(jnp.min(rowsum), jnp.min(colsum))
    high = jnp.maximum(jnp.max(rowsum), jnp.max(colsum))
    good = jnp.logical_and(low >= LOW, high <= HIGH)
    peak = peak_ref[0:1, :]

    @pl.when(good)
    def _():
        lrow_ref[0:nq, :] = (jnp.log2(rowsum) + peak) - v_ref[...]
        lcol_ref[...] = (jnp.log2(colsum) + peak) - u_ref[...]

    @pl.when(jnp.logical_not(good))
    def _():
        spread(v_ref, vs_ref, nq)

        def row_block(q, carry):
            part = pl.ds(pl.multiple_of(q * LANES, LANES), LANES)

            def scores(d_ref, first, c):
                at = pl.ds(pl.multiple_of(c * LANES, LANES), LANES)
                return d_ref[part, at] + u_ref[pl.ds(first + c, 1), :]

            best = jnp.full((LANES, LANES), -3.0e38, F32)
            first = 0
            for d_ref in d_refs:
                count = d_ref.shape[1] // LANES
                best = lax.fori_loop(
                    0, count, lambda c, best: jnp.maximum(best, scores(d_ref, first, c)), best
                )
                first += count
            top = jnp.max(best, axis=1, keepdims=True)
            acc = jnp.zeros((LANES, LANES), F32)
            first = 0
            for d_ref in d_refs:
                count = d_ref.shape[1] // LANES
                acc = lax.fori_loop(
                    0, count, lambda c, acc: acc + jnp.exp2(scores(d_ref, first, c) - top), acc
                )
                first += count
            log_sum = jnp.log2(jnp.sum(acc, axis=1, keepdims=True)) + top
            lrow_ref[pl.ds(q, 1), :] = lane_fold(jnp.broadcast_to(log_sum, (LANES, LANES)), jnp.max)
            return carry

        lax.fori_loop(0, nq, row_block, 0)
        first = 0
        for d_ref in d_refs:
            count = d_ref.shape[1] // LANES

            def column(c, carry):
                at = pl.ds(pl.multiple_of(c * LANES, LANES), LANES)

                def block(r):
                    part = pl.ds(pl.multiple_of(r * ROWS, ROWS), ROWS)
                    return d_ref[part, at] + vs_ref[part, :]

                top = lax.fori_loop(
                    0,
                    rows // ROWS,
                    lambda r, best: jnp.maximum(best, jnp.max(block(r), axis=0, keepdims=True)),
                    jnp.full((1, LANES), -3.0e38, F32),
                )
                total = lax.fori_loop(
                    0,
                    rows // ROWS,
                    lambda r, acc: acc + jnp.sum(jnp.exp2(block(r) - top), axis=0, keepdims=True),
                    jnp.zeros((1, LANES), F32),
                )
                lcol_ref[pl.ds(first + c, 1), :] = top + jnp.log2(total)
                return carry

            lax.fori_loop(0, count, column, 0)
            first += count


def first_kernel(
    offset, gen_ref, ref_hbm, gweight_hbm, rweight_hbm,
    d_ref, lrow_ref, lcol_ref, hrow_ref, hcol_ref, mass_ref, *refs,
):
    if offset == 0:
        held_ref, *refs = refs
    tile_ref, stage_ref, gweight_ref, rweight_ref, u_ref, v_ref, vs_ref, rowacc_ref, colsum_ref, peak_ref, sem = refs
    rows, width = gen_ref.shape
    nq, nc = rows // LANES, d_ref.shape[1] // LANES
    chunks = TILE // LANES
    steps = d_ref.shape[1] // TILE
    half_scale = 0.5 * LOG2E / (EPS * width)
    dot_scale = LOG2E / (EPS * width)
    loads = []
    if offset == 0:
        loads.append(pltpu.make_async_copy(gen_ref, held_ref, sem.at[steps + 2]))
        gen_ref = held_ref
    loads.append(pltpu.make_async_copy(gweight_hbm, gweight_ref, sem.at[steps]))
    loads.append(pltpu.make_async_copy(rweight_hbm, rweight_ref, sem.at[steps + 1]))

    def load(j):
        at = pl.ds(pl.multiple_of((offset * steps + j) * TILE, TILE), TILE)
        return pltpu.make_async_copy(ref_hbm.at[at, :], tile_ref.at[j], sem.at[j])

    tiles = [load(j) for j in range(steps)]
    for copy in loads[:1] + tiles[:1] + loads[1:] + tiles[1:]:
        copy.start()
    for copy in loads:
        copy.wait()
    for q, part in enumerate(norms(gen_ref, 0, nq, half_scale)):
        hrow_ref[q : q + 1, :] = part
        v_ref[q : q + 1, :] = jnp.log2(gweight_ref[q : q + 1, :]) - part
        hrow_ref[nq + q : nq + q + 1, :] = gweight_ref[q : q + 1, :]
    lrow_ref[nq : 2 * nq, :] = jnp.broadcast_to(jnp.sum(rweight_ref[...]).reshape(1, 1), (nq, LANES))
    mass_ref[...] = jnp.broadcast_to(jnp.sum(gweight_ref[...]).reshape(1, 1), (8, LANES))

    def product(j):
        for c, half in enumerate(norms(tile_ref.at[j], 0, chunks, half_scale)):
            row = pl.ds(j * chunks + c, 1)
            hcol_ref[row, :] = half
            u_ref[row, :] = jnp.log2(rweight_ref[pl.ds(offset * nc + j * chunks + c, 1), :]) - half
        dots = lax.dot_general(
            gen_ref[...], tile_ref[j], (((1,), (1,)), ((), ())), preferred_element_type=F32
        )
        stage_ref[...] = dots * dot_scale

    def sums(j, straight):
        mine = [u_ref[pl.ds(j * chunks + c, 1), :] for c in range(chunks)]
        found = sweep(stage_ref, 0, chunks, mine, vs_ref, rowacc_ref, straight, (d_ref, j * TILE))
        for c, part in enumerate(found):
            colsum_ref[pl.ds(j * chunks + c, 1), :] = part

    tiles[0].wait()
    product(0)
    start_peak(stage_ref, u_ref[0:1, :], v_ref, vs_ref, peak_ref, rowacc_ref)

    def step(j, carry):
        load(j).wait()
        sums(j - 1, True)
        product(j)
        return carry

    lax.fori_loop(1, steps, step, 0)
    sums(steps - 1, False)
    finish([d_ref], u_ref, v_ref, vs_ref, rowacc_ref, colsum_ref, peak_ref, lrow_ref, lcol_ref)


def first_pass(gen, ref, gweight, rweight, piece, pieces):
    rows, width = gen.shape
    cols = ref.shape[0] // pieces
    nq, nc = rows // LANES, cols // LANES
    vmem = pl.BlockSpec(memory_space=pltpu.VMEM)
    hbm = pl.BlockSpec(memory_space=pltpu.HBM)
    vec = lambda n: jax.ShapeDtypeStruct((n, LANES), F32)
    held = () if piece else (pltpu.VMEM((rows, width), gen.dtype),)
    return pl.pallas_call(
        functools.partial(first_kernel, piece),
        in_specs=[vmem if piece else hbm, hbm, hbm, hbm],
        out_shape=(pltpu.VMEM((rows, cols), F32), vec(2 * nq), vec(nc), vec(2 * nq), vec(nc), vec(8)) + held,
        out_specs=(vmem,) * (6 + len(held)),
        scratch_shapes=[
            pltpu.VMEM((cols // TILE, TILE, width), jnp.bfloat16),
            pltpu.VMEM((rows, TILE), F32),
            pltpu.VMEM((nq, LANES), F32),
            pltpu.VMEM(rweight.shape, F32),
            pltpu.VMEM((nc, LANES), F32),
            pltpu.VMEM((nq, LANES), F32),
            pltpu.VMEM((rows, LANES), F32),
            pltpu.VMEM((rows, LANES), F32),
            pltpu.VMEM((nc, LANES), F32),
            pltpu.VMEM((8, LANES), F32),
            pltpu.SemaphoreType.DMA((cols // TILE + 3,)),
        ],
        compiler_params=pltpu.CompilerParams(vmem_limit_bytes=16 << 20),
    )(vmem_array(gen) if piece else hbm_array(gen), hbm_array(ref), gweight, rweight)


def next_kernel(count, *refs):
    sources = refs[:count]
    u_ref, v_ref, lrow_ref, lcol_ref, vs_ref, rowacc_ref, colsum_ref, peak_ref = refs[count:]
    chunks = TILE // LANES
    start_peak(sources[0], u_ref[0:1, :], v_ref, vs_ref, peak_ref, rowacc_ref)
    first = 0
    for d_ref in sources:
        steps = d_ref.shape[1] // TILE

        def step(j, carry):
            u = [u_ref[pl.ds(first + j * chunks + c, 1), :] for c in range(chunks)]
            base = pl.multiple_of(j * TILE, TILE)
            for c, part in enumerate(sweep(d_ref, base, chunks, u, vs_ref, rowacc_ref)):
                colsum_ref[pl.ds(first + j * chunks + c, 1), :] = part
            return carry

        lax.fori_loop(0, steps, step, 0)
        first += steps * chunks
    finish(sources, u_ref, v_ref, vs_ref, rowacc_ref, colsum_ref, peak_ref, lrow_ref, lcol_ref)


def next_pass(parts, u, v):
    rows = parts[0].shape[0]
    cols = sum(part.shape[1] for part in parts)
    nq, nc = rows // LANES, cols // LANES
    vmem = pl.BlockSpec(memory_space=pltpu.VMEM)
    return pl.pallas_call(
        functools.partial(next_kernel, len(parts)),
        in_specs=[vmem] * (len(parts) + 2),
        out_shape=(jax.ShapeDtypeStruct((nq, LANES), F32), jax.ShapeDtypeStruct((nc, LANES), F32)),
        out_specs=(vmem, vmem),
        scratch_shapes=[
            pltpu.VMEM((rows, LANES), F32),
            pltpu.VMEM((rows, LANES), F32),
            pltpu.VMEM((nc, LANES), F32),
            pltpu.VMEM((8, LANES), F32),
        ],
        compiler_params=pltpu.CompilerParams(vmem_limit_bytes=8 << 20),
    )(*[vmem_array(part) for part in parts], u, v)


def self_first_kernel(count, first, *refs):
    own_ref, mate_ref = refs[:2]
    sources = refs[2 : 2 + count]
    rest = refs[2 + count :]
    half, width = own_ref.shape
    nq = half // LANES
    if first == 0:
        mine_ref, theirs_ref, place_ref, e_ref, z_ref, hs_ref, ws_ref = rest
        for at, vec_ref in ((0, mine_ref), (nq, theirs_ref)):
            spread(vec_ref, hs_ref, nq, 0, at)
            spread(vec_ref, ws_ref, nq, nq, at)
    else:
        hs_ref, ws_ref, place_ref, e_ref, z_ref = rest
    wide = 256
    chunks = wide // LANES
    half_scale = 0.5 * LOG2E / (EPS * width)
    dot_scale = LOG2E / (EPS * width)
    z_ref[...] = jnp.zeros_like(z_ref)
    tiles = [(src, k) for src in sources for k in range(src.shape[0] // wide)]
    piece_half = {}

    def product(t):
        src, k = tiles[t]
        view = src.at[k * wide : (k + 1) * wide, :]
        piece_half[t] = norms(view, 0, chunks, half_scale)
        for h, rows_ref in enumerate((own_ref, mate_ref)):
            e_ref[h * half : (h + 1) * half, t * wide : (t + 1) * wide] = lax.dot_general(
                rows_ref[...], view[...], (((1,), (1,)), ((), ())), preferred_element_type=F32
            )

    def sums(t, straight):
        def body(r, acc):
            at = row_block(r)
            hs = hs_ref[at, :]
            ws = ws_ref[at, :]
            out = []
            for c in range(chunks):
                part = slice(t * wide + c * LANES, t * wide + (c + 1) * LANES)
                e = jnp.exp2(e_ref[at, part] * dot_scale - (hs + piece_half[t][c]))
                e_ref[at, part] = e
                out.append(acc[c] + jnp.sum((e * ws).reshape(ROWS // 8, 8, LANES), axis=0))
            return tuple(out)

        acc = (jnp.zeros((8, LANES), F32),) * chunks
        if straight:
            for r in range(2 * half // ROWS):
                acc = body(r, acc)
        else:
            acc = lax.fori_loop(0, 2 * half // ROWS, body, acc, unroll=2)
        for c in range(chunks):
            z_ref[pl.ds(place_ref[first + t * chunks + c], 1), :] = jnp.sum(acc[c], axis=0, keepdims=True)

    product(0)
    for t in range(1, len(tiles)):
        sums(t - 1, True)
        product(t)
    sums(len(tiles) - 1, False)


def self_first(own, mate, sources, left, right, place, first):
    rows = 2 * own.shape[0]
    cols = sum(src.shape[0] for src in sources)
    vmem = pl.BlockSpec(memory_space=pltpu.VMEM)
    lanes = () if first else (pltpu.VMEM((rows, LANES), F32),) * 2
    if first:
        left, right = vmem_array(left), vmem_array(right)
    return pl.pallas_call(
        functools.partial(self_first_kernel, len(sources), first),
        in_specs=[vmem] * (4 + len(sources)) + [pl.BlockSpec(memory_space=pltpu.SMEM)],
        out_shape=(pltpu.VMEM((rows, cols), F32), jax.ShapeDtypeStruct((place.shape[0], LANES), F32)) + lanes,
        out_specs=(vmem,) * (2 + len(lanes)),
        compiler_params=pltpu.CompilerParams(vmem_limit_bytes=8 << 20),
    )(vmem_array(own), vmem_array(mate), *[vmem_array(src) for src in sources], left, right, place)


def self_cols_kernel(count, *refs):
    w_ref, place_ref, z_ref, ws_ref = refs[count:]
    rows = refs[0].shape[0]
    chunks = 256 // LANES
    spread(w_ref, ws_ref, rows // LANES)
    zero = jnp.zeros((8, LANES), F32)
    first = 0
    for e_ref in refs[:count]:
        steps = e_ref.shape[1] // 256

        def tile(t, carry):
            base = pl.multiple_of(t * 256, 256)

            def body(r, acc):
                at = pl.ds(pl.multiple_of(r * ROWS, ROWS), ROWS)
                ws = ws_ref[at, :]
                out = []
                for c in range(chunks):
                    e = e_ref[at, pl.ds(base + c * LANES, LANES)] * ws
                    out.append(acc[c] + jnp.sum(e.reshape(ROWS // 8, 8, LANES), axis=0))
                return tuple(out)

            acc = lax.fori_loop(0, rows // ROWS, body, (zero,) * chunks, unroll=4)
            for c in range(chunks):
                z_ref[pl.ds(place_ref[first + t * chunks + c], 1), :] = jnp.sum(acc[c], axis=0, keepdims=True)
            return carry

        lax.fori_loop(0, steps, tile, 0)
        first += steps * chunks


def self_rows_kernel(count, *refs):
    w_ref, place_ref, y_ref, rowacc_ref = refs[count:]
    rows = refs[0].shape[0]
    chunks = 512 // LANES
    rowacc_ref[...] = jnp.zeros_like(rowacc_ref)
    first = 0
    for e_ref in refs[:count]:
        steps = e_ref.shape[1] // 512

        def tile(t, carry):
            base = pl.multiple_of(t * 512, 512)
            w = [w_ref[pl.ds(place_ref[first + t * chunks + c], 1), :] for c in range(chunks)]

            def body(r, carry):
                at = pl.ds(pl.multiple_of(r * ROWS, ROWS), ROWS)
                acc = rowacc_ref[at, :]
                for c in range(chunks):
                    acc = acc + e_ref[at, pl.ds(base + c * LANES, LANES)] * w[c]
                rowacc_ref[at, :] = acc
                return carry

            return lax.fori_loop(0, rows // ROWS, body, carry, unroll=4)

        lax.fori_loop(0, steps, tile, 0)
        first += steps * chunks
    for q in range(rows // LANES):
        y_ref[q : q + 1, :] = lane_fold(rowacc_ref[q * LANES : (q + 1) * LANES, :], jnp.sum)


def self_apply(kernel, parts, w, place, out_rows):
    rows = parts[0].shape[0]
    vmem = pl.BlockSpec(memory_space=pltpu.VMEM)
    return pl.pallas_call(
        functools.partial(kernel, len(parts)),
        in_specs=[vmem] * (len(parts) + 1) + [pl.BlockSpec(memory_space=pltpu.SMEM)],
        out_shape=jax.ShapeDtypeStruct((out_rows, LANES), F32),
        out_specs=vmem,
        scratch_shapes=[pltpu.VMEM((rows, LANES), F32)],
        compiler_params=pltpu.CompilerParams(vmem_limit_bytes=8 << 20),
    )(*[vmem_array(part) for part in parts], w, place)


def log_add(parts):
    top = functools.reduce(jnp.maximum, parts)
    return top + jnp.log2(sum(jnp.exp2(part - top) for part in parts))


def build(n_z, n_y, n_core, n_ref):
    n_zy = n_z * n_y
    n_gen = n_zy * n_core
    assert n_z == n_y == n_ref == 4 and n_core == 2

    def place_of(g):
        return g // (n_y * n_core), (g // n_core) % n_y, g % n_core

    def gen_perm(move):
        out = []
        for g in range(n_gen):
            z, y, c = move(*place_of(g))
            out.append((g, ((z % n_z) * n_y + y % n_y) * n_core + c % n_core))
        return out

    core_stage = [gen_perm(lambda z, y, c: (z, y, c + 1))]
    y_stage = [gen_perm(lambda z, y, c: (z, y + k, c)) for k in (1, 2, 3)]
    z_stage = [gen_perm(lambda z, y, c: (z + k, y, c)) for k in (1, 2, 3)]
    ref_stage = [[(i, (i + k) % n_ref) for i in range(n_ref)] for k in (1, 2, 3)]
    first_axis = {k: gen_perm(lambda z, y, c: (z, y + k, c) if c == 0 else (z + k, y, c)) for k in (1, 2, 3)}
    second_axis = {k: gen_perm(lambda z, y, c: (z + k, y, c) if c == 0 else (z, y + k, c)) for k in (1, 3)}
    order = [(0, 0), (0, 1), (0, 2), (0, 3)]
    order += [(1, 0), (1, 1), (1, 2), (1, 3), (3, 0), (3, 1), (3, 2), (3, 3)]
    order += [(2, 0), (2, 1), (2, 2), (2, 3)]

    def shift(value, axis, perms):
        return [lax.ppermute(value, axis, perm) for perm in perms]

    def merge(parts, logs):
        top = log_add([part[:logs] for part in parts])
        if parts[0].shape[0] == logs:
            return top
        return jnp.concatenate([top, sum(part[logs:] for part in parts)], axis=0)

    def stage(value, axis, perms, logs):
        return merge([value] + shift(value, axis, perms), logs)

    def doubled(value, logs):
        for bit in (1, 2):
            value = merge([value, lax.ppermute(value, "ref", [(i, i ^ bit) for i in range(n_ref)])], logs)
        return value

    def run(gen_features, gen_weight, ref_features, ref_weight, ref_self):
        gen_count = gen_features.shape[0]
        ref_count = ref_features.shape[0]
        nq, nc = gen_count // LANES, ref_count // LANES
        g = lax.axis_index("gen")
        x = lax.axis_index("ref")
        z, y, core = place_of(g)
        zy = z * n_y + y
        b, a = (lax.broadcasted_iota(jnp.int32, (len(order),), 0) for _ in range(2))
        b = functools.reduce(lambda v, k: jnp.where(a == k, order[k][0], v), range(len(order)), b)
        a = a % 4
        mine = ((z - b + n_z) % n_z) * n_y + (y - a + n_y) % n_y
        other = ((z - a + n_z) % n_z) * n_y + (y - b + n_y) % n_y
        place = jnp.where(core == 0, mine, other)
        wg = gen_weight.reshape(nq, LANES)
        wr = ref_weight.reshape(nc, LANES)
        at_zy = (lax.broadcasted_iota(jnp.int32, (n_zy, LANES), 0) == zy).astype(F32)
        at_x = (lax.broadcasted_iota(jnp.int32, (n_ref, LANES), 0) == x).astype(F32)
        wg, place, at_zy, at_x = lax.optimization_barrier((wg, place, at_zy, at_x))

        def to_cols(rows):
            picked = jnp.sum(jnp.where(at_x > 0, rows, 0.0), axis=0, keepdims=True)
            return jnp.where(at_zy > 0, picked, 0.0)

        def to_rows(cols):
            picked = jnp.sum(jnp.where(at_zy > 0, cols, 0.0), axis=0, keepdims=True)
            return jnp.where(at_x > 0, picked, 0.0)

        own = lax.dynamic_slice_in_dim(gen_features, x * LANES, LANES, 0)
        got = [lax.ppermute(own, "gen", first_axis[k]) for k in (1, 2, 3)]
        mate = lax.ppermute(gen_features, "gen", core_stage[0])
        near = jnp.concatenate([own] + got, axis=0)
        up = lax.ppermute(near, "gen", second_axis[1])
        down = lax.ppermute(near, "gen", second_axis[3])
        low_far = lax.ppermute(up[: 2 * LANES], "gen", second_axis[1])
        high_far = lax.ppermute(down[2 * LANES :], "gen", second_axis[3])

        d0, row0, lcol0, mine, hcol0, gmass, held = first_pass(gen_features, ref_features, wg, wr, 0, 2)
        theirs = lax.ppermute(mine, "gen", core_stage[0])
        d1, row1, lcol1, _, hcol1, _ = first_pass(held, ref_features, wg, wr, 1, 2)
        hcol = jnp.concatenate([hcol0, hcol1], axis=0)
        hrow = mine[:nq]
        weight = jnp.concatenate([wg, theirs[nq:]], axis=0)
        e0, z1_0, hs, ws = self_first(held, mate, [near], mine, theirs, place, 0)
        e1, z1_1 = self_first(held, mate, [up, down], hs, ws, place, 4)
        e2, z1_2 = self_first(held, mate, [low_far, high_far], hs, ws, place, 12)
        e = [e0, e1, e2]

        row_part = jnp.concatenate([log_add([row0[:nq], row1[:nq]]), row0[nq:]], axis=0)
        row_part = doubled(row_part, nq)
        col_part = jnp.concatenate([lcol0, lcol1, gmass], axis=0)
        col_part = stage(col_part, "gen", core_stage, nc)
        col_part = jnp.concatenate([col_part, to_cols(wg)], axis=0)
        col_part = stage(col_part, "gen", y_stage, nc)
        col_part = stage(col_part, "gen", z_stage, nc)
        gmass = col_part[nc : nc + 1]
        rmass = row_part[nq : nq + 1]
        wcols = col_part[nc + 8 :] / gmass
        gmass_log = jnp.log2(gmass)
        rmass_log = jnp.log2(rmass)
        f = hrow - (row_part[:nq] - rmass_log)
        c = hcol - (col_part[:nc] - gmass_log)
        ubase = jnp.log2(wr) - rmass_log - hcol
        vbase = jnp.log2(wg) - gmass_log - hrow
        share = wg / gmass

        lrow, lcol = next_pass([d0, d1], ubase + c, vbase + f)
        lrow = doubled(lrow, nq)
        lcol = stage(lcol, "gen", core_stage, nc)
        col_part = jnp.concatenate([lcol, z1_0 + z1_1 + z1_2], axis=0)
        col_part = stage(col_part, "gen", y_stage, nc)
        col_part = stage(col_part, "gen", z_stage, nc)
        f = 0.5 * (f + (hrow - lrow))
        c = 0.5 * (c + (hcol - col_part[:nc]))
        y1 = col_part[nc:] / gmass

        lrow, lcol = next_pass([d0, d1], ubase + c, vbase + f)
        y2 = self_apply(self_rows_kernel, e, wcols / y1, place, 2 * nq)
        row_part = jnp.concatenate([lrow, y2, to_rows(-jnp.log2(y1))], axis=0)
        row_part = stage(row_part, "ref", ref_stage, nq)
        f = 0.5 * (f + (hrow - row_part[:nq]))
        f_part = share * f
        f_part = jnp.concatenate([f_part, f_part], axis=0)
        mine = jnp.concatenate([lcol, f_part, row_part[nq:]], axis=0)
        theirs = shift(mine, "gen", core_stage)[0]
        lcol = log_add([lcol, theirs[:nc]])
        f_part = f_part + theirs[nc : nc + 8]
        y2, y2_mate, s1 = row_part[nq : 2 * nq], row_part[2 * nq : 3 * nq], row_part[3 * nq :]
        at = nc + 8
        y2 = y2 + theirs[at + nq : at + 2 * nq]
        y2_mate = y2_mate + theirs[at : at + nq]
        s1 = jnp.concatenate([s1, theirs[at + 2 * nq :]], axis=0)
        s2 = 0.5 * (s1 - jnp.log2(jnp.concatenate([y2, y2_mate], axis=0)))
        w3 = weight / gmass * jnp.exp2(s2)
        z3 = self_apply(self_cols_kernel, e, w3, place, n_zy)
        col_part = jnp.concatenate([lcol, f_part, z3, to_cols(s2[:nq])], axis=0)
        col_part = stage(col_part, "gen", y_stage, nc)
        col_part = stage(col_part, "gen", z_stage, nc)
        c = 0.5 * (c + (hcol - col_part[:nc]))
        f_part = col_part[nc : nc + nq]
        z3, s2 = col_part[nc + 8 : nc + 8 + n_zy], col_part[nc + 8 + n_zy :]

        unit = EPS / LOG2E
        ref_gap = c * unit - ref_self.reshape(nc, LANES)
        s3 = 0.5 * (s2 - jnp.log2(z3))
        s_part = jnp.sum((wcols * s3).reshape(2, 8, LANES), axis=0)
        s_part = s_part + shift(s_part, "gen", core_stage)[0]
        part = jnp.sum(((wr / rmass) * ref_gap).reshape(nc // 8, 8, LANES), axis=0) - unit * s_part
        row_part = jnp.concatenate([to_rows(s3), part], axis=0)
        row_part = row_part + sum(shift(row_part, "ref", ref_stage))
        gen_gap = (f - row_part[:nq]) * unit
        divergence = jnp.sum(unit * f_part + row_part[nq : 2 * nq] + row_part[2 * nq :])
        return gen_gap.reshape(gen_count), ref_gap.reshape(ref_count), divergence

    return run


def solution(mesh):
    n_gen, n_ref = mesh.shape["gen"], mesh.shape["ref"]
    n_core = 2
    n_y = 1
    while n_y * n_y * n_core < n_gen:
        n_y *= 2
    placed = (P("gen", None), P("gen"), P("ref", None), P("ref"), P("ref"))
    return jax.shard_map(
        build(n_gen // (n_y * n_core), n_y, n_core, n_ref),
        mesh=mesh,
        in_specs=placed,
        out_specs=(P("gen"), P("ref"), P()),
        check_vma=False,
    )
```

```python
import functools

import jax
import jax.numpy as jnp
from jax import lax
from jax.experimental import pallas as pl
from jax.experimental.pallas import tpu as pltpu
from jax.sharding import PartitionSpec as P


EPS = 0.1
LOG2E = 1.4426950408889634
F32 = jnp.float32
LANES = 128
TILE = 512
ROWS = 32
LOW = 2.0**-80
HIGH = 2.0**120


def vmem_array(x):
    return pltpu.with_memory_space_constraint(x, pltpu.VMEM)


def hbm_array(x):
    return pltpu.with_memory_space_constraint(x, pltpu.HBM)


def spread(vec_ref, out_ref, count, first=0, at=0):
    for q in range(count):
        block = jnp.broadcast_to(vec_ref[first + q : first + q + 1, :], (LANES, LANES))
        out_ref[(at + q) * LANES : (at + q + 1) * LANES, :] = block.T


def lane_fold(acc, op):
    return op(acc.T, axis=0, keepdims=True)


def norms(feat_ref, start, count, scale):
    width = feat_ref.shape[1]
    out = []
    for q in range(count):
        acc = jnp.zeros((LANES, LANES), F32)
        for c in range(width // LANES):
            x = feat_ref[start + q * LANES : start + (q + 1) * LANES, c * LANES : (c + 1) * LANES].astype(F32)
            acc = acc + x * x
        out.append(lane_fold(acc, jnp.sum) * scale)
    return out


def row_block(r):
    if isinstance(r, int):
        return slice(r * ROWS, (r + 1) * ROWS)
    return pl.ds(pl.multiple_of(r * ROWS, ROWS), ROWS)


def sweep(d_ref, base, chunks, u, vs_ref, rowacc_ref, straight=False, keep=None):
    rows = d_ref.shape[0]

    def body(r, cols):
        at = row_block(r)
        vs = vs_ref[at, :]
        racc = rowacc_ref[at, :]
        out = []
        for c in range(chunks):
            d = d_ref[at, pl.ds(base + c * LANES, LANES)]
            if keep is not None:
                keep[0][at, pl.ds(pl.multiple_of(keep[1] + c * LANES, LANES), LANES)] = d
            p = jnp.exp2((d + u[c]) + vs)
            racc = racc + p
            out.append(cols[c] + jnp.sum(p.reshape(ROWS // 8, 8, LANES), axis=0))
        rowacc_ref[at, :] = racc
        return tuple(out)

    cols = (jnp.zeros((8, LANES), F32),) * chunks
    if straight:
        for r in range(rows // ROWS):
            cols = body(r, cols)
    else:
        cols = lax.fori_loop(0, rows // ROWS, body, cols, unroll=4)
    return [jnp.sum(c, axis=0, keepdims=True) for c in cols]


def tile_peak(d_ref, u, vs_ref):
    rows = d_ref.shape[0]
    best = jnp.full((8, LANES), -3.0e38, F32)

    def body(r, best):
        at = pl.ds(pl.multiple_of(r * ROWS, ROWS), ROWS)
        val = (d_ref[at, 0:LANES] + u) + vs_ref[at, :]
        return jnp.maximum(best, jnp.max(val.reshape(ROWS // 8, 8, LANES), axis=0))

    best = lax.fori_loop(0, rows // ROWS, body, best, unroll=2)
    return jnp.max(jnp.max(best, axis=0, keepdims=True), axis=1, keepdims=True)


def start_peak(d_ref, u0, v_ref, vs_ref, peak_ref, rowacc_ref):
    rows = d_ref.shape[0]
    spread(v_ref, vs_ref, rows // LANES)
    peak = jnp.broadcast_to(tile_peak(d_ref, u0, vs_ref), (8, LANES))
    peak_ref[...] = peak
    vs_ref[...] = vs_ref[...] - peak[0:1, :]
    rowacc_ref[...] = jnp.zeros_like(rowacc_ref)


def finish(d_refs, u_ref, v_ref, vs_ref, rowacc_ref, colsum_ref, peak_ref, lrow_ref, lcol_ref):
    rows = d_refs[0].shape[0]
    nq = rows // LANES
    rowsum = [lane_fold(rowacc_ref[q * LANES : (q + 1) * LANES, :], jnp.sum) for q in range(nq)]
    rowsum = jnp.concatenate(rowsum, axis=0)
    colsum = colsum_ref[...]
    low = jnp.minimum(jnp.min(rowsum), jnp.min(colsum))
    high = jnp.maximum(jnp.max(rowsum), jnp.max(colsum))
    good = jnp.logical_and(low >= LOW, high <= HIGH)
    peak = peak_ref[0:1, :]

    @pl.when(good)
    def _():
        lrow_ref[0:nq, :] = (jnp.log2(rowsum) + peak) - v_ref[...]
        lcol_ref[...] = (jnp.log2(colsum) + peak) - u_ref[...]

    @pl.when(jnp.logical_not(good))
    def _():
        spread(v_ref, vs_ref, nq)

        def row_block(q, carry):
            part = pl.ds(pl.multiple_of(q * LANES, LANES), LANES)

            def scores(d_ref, first, c):
                at = pl.ds(pl.multiple_of(c * LANES, LANES), LANES)
                return d_ref[part, at] + u_ref[pl.ds(first + c, 1), :]

            best = jnp.full((LANES, LANES), -3.0e38, F32)
            first = 0
            for d_ref in d_refs:
                count = d_ref.shape[1] // LANES
                best = lax.fori_loop(
                    0, count, lambda c, best: jnp.maximum(best, scores(d_ref, first, c)), best
                )
                first += count
            top = jnp.max(best, axis=1, keepdims=True)
            acc = jnp.zeros((LANES, LANES), F32)
            first = 0
            for d_ref in d_refs:
                count = d_ref.shape[1] // LANES
                acc = lax.fori_loop(
                    0, count, lambda c, acc: acc + jnp.exp2(scores(d_ref, first, c) - top), acc
                )
                first += count
            log_sum = jnp.log2(jnp.sum(acc, axis=1, keepdims=True)) + top
            lrow_ref[pl.ds(q, 1), :] = lane_fold(jnp.broadcast_to(log_sum, (LANES, LANES)), jnp.max)
            return carry

        lax.fori_loop(0, nq, row_block, 0)
        first = 0
        for d_ref in d_refs:
            count = d_ref.shape[1] // LANES

            def column(c, carry):
                at = pl.ds(pl.multiple_of(c * LANES, LANES), LANES)

                def block(r):
                    part = pl.ds(pl.multiple_of(r * ROWS, ROWS), ROWS)
                    return d_ref[part, at] + vs_ref[part, :]

                top = lax.fori_loop(
                    0,
                    rows // ROWS,
                    lambda r, best: jnp.maximum(best, jnp.max(block(r), axis=0, keepdims=True)),
                    jnp.full((1, LANES), -3.0e38, F32),
                )
                total = lax.fori_loop(
                    0,
                    rows // ROWS,
                    lambda r, acc: acc + jnp.sum(jnp.exp2(block(r) - top), axis=0, keepdims=True),
                    jnp.zeros((1, LANES), F32),
                )
                lcol_ref[pl.ds(first + c, 1), :] = top + jnp.log2(total)
                return carry

            lax.fori_loop(0, count, column, 0)
            first += count


def first_kernel(offset, steps, *refs):
    if offset == 0:
        gen_hbm, ref_hbm, gweight_hbm, rweight_hbm, *refs = refs
        d_ref, lrow_ref, lcol_ref, hcol_ref, hrow_ref, mass_ref, gen_ref, ahead_ref, *refs = refs
        gweight_ref, *refs = refs
    else:
        gen_ref, ref_hbm, rweight_hbm, hrow_ref, first_ref, d_ref, lrow_ref, lcol_ref, hcol_ref, *refs = refs
    tile_ref, stage_ref, rweight_ref, u_ref, v_ref, vs_ref, rowacc_ref, colsum_ref, peak_ref, sem = refs
    rows, width = gen_ref.shape
    nq, nc = rows // LANES, d_ref.shape[1] // LANES
    chunks = TILE // LANES
    half_scale = 0.5 * LOG2E / (EPS * width)
    dot_scale = LOG2E / (EPS * width)
    first_tile = offset * steps

    def load(j):
        at = pl.ds(pl.multiple_of((first_tile + j) * TILE, TILE), TILE)
        return pltpu.make_async_copy(ref_hbm.at[at, :], tile_ref.at[j], sem.at[j])

    rload = pltpu.make_async_copy(rweight_hbm, rweight_ref, sem.at[steps])
    if offset == 0:
        own = pltpu.make_async_copy(gen_hbm, gen_ref, sem.at[steps + 1])
        gload = pltpu.make_async_copy(gweight_hbm, gweight_ref, sem.at[steps + 2])
        ahead = pltpu.make_async_copy(
            ref_hbm.at[steps * TILE : (steps + 1) * TILE, :], ahead_ref, sem.at[steps + 3]
        )
        for copy in (own, load(0), gload, rload):
            copy.start()
        own.wait()
        load(1).start()
        gload.wait()
        rload.wait()
        for q, part in enumerate(norms(gen_ref, 0, nq, half_scale)):
            hrow_ref[q : q + 1, :] = part
            v_ref[q : q + 1, :] = jnp.log2(gweight_ref[q : q + 1, :]) - part
            hrow_ref[nq + q : nq + q + 1, :] = gweight_ref[q : q + 1, :]
        lrow_ref[nq : 2 * nq, :] = jnp.broadcast_to(jnp.sum(rweight_ref[...]).reshape(1, 1), (nq, LANES))
        mass_ref[...] = jnp.broadcast_to(jnp.sum(gweight_ref[...]).reshape(1, 1), (8, LANES))
        load(0).wait()
        tile0_ref = tile_ref.at[0]
    else:
        rload.start()
        load(1).start()
        v_ref[...] = jnp.log2(hrow_ref[nq : 2 * nq, :]) - hrow_ref[0:nq, :]
        rload.wait()
        tile0_ref = first_ref

    def product(j, tile):
        for c, half in enumerate(norms(tile, 0, chunks, half_scale)):
            row = pl.ds(j * chunks + c, 1)
            hcol_ref[row, :] = half
            u_ref[row, :] = jnp.log2(rweight_ref[pl.ds(offset * nc + j * chunks + c, 1), :]) - half
        dots = lax.dot_general(gen_ref[...], tile[...], (((1,), (1,)), ((), ())), preferred_element_type=F32)
        stage_ref[...] = dots * dot_scale

    def sums(j, straight):
        mine = [u_ref[pl.ds(j * chunks + c, 1), :] for c in range(chunks)]
        found = sweep(stage_ref, 0, chunks, mine, vs_ref, rowacc_ref, straight, (d_ref, j * TILE))
        for c, part in enumerate(found):
            colsum_ref[pl.ds(j * chunks + c, 1), :] = part

    product(0, tile0_ref)
    start_peak(stage_ref, u_ref[0:1, :], v_ref, vs_ref, peak_ref, rowacc_ref)

    def step(j, carry):
        load(j).wait()

        @pl.when(j + 1 < steps)
        def _():
            load(j + 1).start()

        if offset == 0:

            @pl.when(j + 1 == steps)
            def _():
                ahead.start()

        sums(j - 1, True)
        product(j, tile_ref.at[j])
        return carry

    lax.fori_loop(1, steps, step, 0)
    sums(steps - 1, False)
    finish([d_ref], u_ref, v_ref, vs_ref, rowacc_ref, colsum_ref, peak_ref, lrow_ref, lcol_ref)
    if offset == 0:
        ahead.wait()


def first_pass(offset, pieces, gen, ref, rweight, *more):
    rows, width = gen.shape
    cols = ref.shape[0] // pieces
    steps = cols // TILE
    nq, nc = rows // LANES, cols // LANES
    vmem = pl.BlockSpec(memory_space=pltpu.VMEM)
    hbm = pl.BlockSpec(memory_space=pltpu.HBM)
    vec = lambda n: jax.ShapeDtypeStruct((n, LANES), F32)
    outs = (pltpu.VMEM((rows, cols), F32), vec(nq if offset else 2 * nq), vec(nc), vec(nc))
    if offset == 0:
        (gweight,) = more
        outs += (vec(2 * nq), vec(8), pltpu.VMEM((rows, width), gen.dtype), pltpu.VMEM((TILE, width), ref.dtype))
        specs = [hbm] * 4
        operands = [hbm_array(gen), hbm_array(ref), hbm_array(gweight), hbm_array(rweight)]
        weights = [pltpu.VMEM((nq, LANES), F32)]
    else:
        hrow, first = more
        specs = [vmem, hbm, hbm, vmem, vmem]
        operands = [vmem_array(gen), hbm_array(ref), hbm_array(rweight), hrow, vmem_array(first)]
        weights = []
    return pl.pallas_call(
        functools.partial(first_kernel, offset, steps),
        in_specs=specs,
        out_shape=outs,
        out_specs=(vmem,) * len(outs),
        scratch_shapes=weights
        + [
            pltpu.VMEM((steps, TILE, width), jnp.bfloat16),
            pltpu.VMEM((rows, TILE), F32),
            pltpu.VMEM(rweight.shape, F32),
            pltpu.VMEM((nc, LANES), F32),
            pltpu.VMEM((nq, LANES), F32),
            pltpu.VMEM((rows, LANES), F32),
            pltpu.VMEM((rows, LANES), F32),
            pltpu.VMEM((nc, LANES), F32),
            pltpu.VMEM((8, LANES), F32),
            pltpu.SemaphoreType.DMA((steps + 4,)),
        ],
        compiler_params=pltpu.CompilerParams(vmem_limit_bytes=16 << 20),
    )(*operands)


def next_kernel(count, *refs):
    sources = refs[:count]
    u_ref, v_ref, lrow_ref, lcol_ref, vs_ref, rowacc_ref, colsum_ref, peak_ref = refs[count:]
    chunks = TILE // LANES
    start_peak(sources[0], u_ref[0:1, :], v_ref, vs_ref, peak_ref, rowacc_ref)
    first = 0
    for d_ref in sources:
        steps = d_ref.shape[1] // TILE

        def step(j, carry):
            u = [u_ref[pl.ds(first + j * chunks + c, 1), :] for c in range(chunks)]
            base = pl.multiple_of(j * TILE, TILE)
            for c, part in enumerate(sweep(d_ref, base, chunks, u, vs_ref, rowacc_ref)):
                colsum_ref[pl.ds(first + j * chunks + c, 1), :] = part
            return carry

        lax.fori_loop(0, steps, step, 0)
        first += steps * chunks
    finish(sources, u_ref, v_ref, vs_ref, rowacc_ref, colsum_ref, peak_ref, lrow_ref, lcol_ref)


def next_pass(parts, u, v):
    rows = parts[0].shape[0]
    cols = sum(part.shape[1] for part in parts)
    nq, nc = rows // LANES, cols // LANES
    vmem = pl.BlockSpec(memory_space=pltpu.VMEM)
    return pl.pallas_call(
        functools.partial(next_kernel, len(parts)),
        in_specs=[vmem] * (len(parts) + 2),
        out_shape=(jax.ShapeDtypeStruct((nq, LANES), F32), jax.ShapeDtypeStruct((nc, LANES), F32)),
        out_specs=(vmem, vmem),
        scratch_shapes=[
            pltpu.VMEM((rows, LANES), F32),
            pltpu.VMEM((rows, LANES), F32),
            pltpu.VMEM((nc, LANES), F32),
            pltpu.VMEM((8, LANES), F32),
        ],
        compiler_params=pltpu.CompilerParams(vmem_limit_bytes=8 << 20),
    )(*[vmem_array(part) for part in parts], u, v)


def self_first_kernel(count, first, *refs):
    own_ref, mate_ref = refs[:2]
    sources = refs[2 : 2 + count]
    rest = refs[2 + count :]
    half, width = own_ref.shape
    nq = half // LANES
    if first == 0:
        mine_ref, theirs_ref, place_ref, e_ref, z_ref, hs_ref, ws_ref = rest
        for at, vec_ref in ((0, mine_ref), (nq, theirs_ref)):
            spread(vec_ref, hs_ref, nq, 0, at)
            spread(vec_ref, ws_ref, nq, nq, at)
    else:
        hs_ref, ws_ref, place_ref, e_ref, z_ref = rest
    wide = 256
    chunks = wide // LANES
    half_scale = 0.5 * LOG2E / (EPS * width)
    dot_scale = LOG2E / (EPS * width)
    z_ref[...] = jnp.zeros_like(z_ref)
    tiles = [(src, k) for src in sources for k in range(src.shape[0] // wide)]
    piece_half = {}

    def product(t):
        src, k = tiles[t]
        view = src.at[k * wide : (k + 1) * wide, :]
        piece_half[t] = norms(view, 0, chunks, half_scale)
        for h, rows_ref in enumerate((own_ref, mate_ref)):
            e_ref[h * half : (h + 1) * half, t * wide : (t + 1) * wide] = lax.dot_general(
                rows_ref[...], view[...], (((1,), (1,)), ((), ())), preferred_element_type=F32
            )

    def sums(t, straight):
        def body(r, acc):
            at = row_block(r)
            hs = hs_ref[at, :]
            ws = ws_ref[at, :]
            out = []
            for c in range(chunks):
                part = slice(t * wide + c * LANES, t * wide + (c + 1) * LANES)
                e = jnp.exp2(e_ref[at, part] * dot_scale - (hs + piece_half[t][c]))
                e_ref[at, part] = e
                out.append(acc[c] + jnp.sum((e * ws).reshape(ROWS // 8, 8, LANES), axis=0))
            return tuple(out)

        acc = (jnp.zeros((8, LANES), F32),) * chunks
        if straight:
            for r in range(2 * half // ROWS):
                acc = body(r, acc)
        else:
            acc = lax.fori_loop(0, 2 * half // ROWS, body, acc, unroll=2)
        for c in range(chunks):
            z_ref[pl.ds(place_ref[first + t * chunks + c], 1), :] = jnp.sum(acc[c], axis=0, keepdims=True)

    product(0)
    for t in range(1, len(tiles)):
        sums(t - 1, True)
        product(t)
    sums(len(tiles) - 1, False)


def self_first(own, mate, sources, left, right, place, first):
    rows = 2 * own.shape[0]
    cols = sum(src.shape[0] for src in sources)
    vmem = pl.BlockSpec(memory_space=pltpu.VMEM)
    lanes = () if first else (pltpu.VMEM((rows, LANES), F32),) * 2
    if first:
        left, right = vmem_array(left), vmem_array(right)
    return pl.pallas_call(
        functools.partial(self_first_kernel, len(sources), first),
        in_specs=[vmem] * (4 + len(sources)) + [pl.BlockSpec(memory_space=pltpu.SMEM)],
        out_shape=(pltpu.VMEM((rows, cols), F32), jax.ShapeDtypeStruct((place.shape[0], LANES), F32)) + lanes,
        out_specs=(vmem,) * (2 + len(lanes)),
        compiler_params=pltpu.CompilerParams(vmem_limit_bytes=8 << 20),
    )(vmem_array(own), vmem_array(mate), *[vmem_array(src) for src in sources], left, right, place)


def self_cols_kernel(count, *refs):
    w_ref, place_ref, z_ref, ws_ref = refs[count:]
    rows = refs[0].shape[0]
    chunks = 256 // LANES
    spread(w_ref, ws_ref, rows // LANES)
    zero = jnp.zeros((8, LANES), F32)
    first = 0
    for e_ref in refs[:count]:
        steps = e_ref.shape[1] // 256

        def tile(t, carry):
            base = pl.multiple_of(t * 256, 256)

            def body(r, acc):
                at = pl.ds(pl.multiple_of(r * ROWS, ROWS), ROWS)
                ws = ws_ref[at, :]
                out = []
                for c in range(chunks):
                    e = e_ref[at, pl.ds(base + c * LANES, LANES)] * ws
                    out.append(acc[c] + jnp.sum(e.reshape(ROWS // 8, 8, LANES), axis=0))
                return tuple(out)

            acc = lax.fori_loop(0, rows // ROWS, body, (zero,) * chunks, unroll=4)
            for c in range(chunks):
                z_ref[pl.ds(place_ref[first + t * chunks + c], 1), :] = jnp.sum(acc[c], axis=0, keepdims=True)
            return carry

        lax.fori_loop(0, steps, tile, 0)
        first += steps * chunks


def self_rows_kernel(count, *refs):
    w_ref, place_ref, y_ref, rowacc_ref = refs[count:]
    rows = refs[0].shape[0]
    chunks = 512 // LANES
    rowacc_ref[...] = jnp.zeros_like(rowacc_ref)
    first = 0
    for e_ref in refs[:count]:
        steps = e_ref.shape[1] // 512

        def tile(t, carry):
            base = pl.multiple_of(t * 512, 512)
            w = [w_ref[pl.ds(place_ref[first + t * chunks + c], 1), :] for c in range(chunks)]

            def body(r, carry):
                at = pl.ds(pl.multiple_of(r * ROWS, ROWS), ROWS)
                acc = rowacc_ref[at, :]
                for c in range(chunks):
                    acc = acc + e_ref[at, pl.ds(base + c * LANES, LANES)] * w[c]
                rowacc_ref[at, :] = acc
                return carry

            return lax.fori_loop(0, rows // ROWS, body, carry, unroll=4)

        lax.fori_loop(0, steps, tile, 0)
        first += steps * chunks
    for q in range(rows // LANES):
        y_ref[q : q + 1, :] = lane_fold(rowacc_ref[q * LANES : (q + 1) * LANES, :], jnp.sum)


def self_apply(kernel, parts, w, place, out_rows):
    rows = parts[0].shape[0]
    vmem = pl.BlockSpec(memory_space=pltpu.VMEM)
    return pl.pallas_call(
        functools.partial(kernel, len(parts)),
        in_specs=[vmem] * (len(parts) + 1) + [pl.BlockSpec(memory_space=pltpu.SMEM)],
        out_shape=jax.ShapeDtypeStruct((out_rows, LANES), F32),
        out_specs=vmem,
        scratch_shapes=[pltpu.VMEM((rows, LANES), F32)],
        compiler_params=pltpu.CompilerParams(vmem_limit_bytes=8 << 20),
    )(*[vmem_array(part) for part in parts], w, place)


def log_add(parts):
    top = functools.reduce(jnp.maximum, parts)
    return top + jnp.log2(sum(jnp.exp2(part - top) for part in parts))


def build(n_z, n_y, n_core, n_ref):
    n_zy = n_z * n_y
    n_gen = n_zy * n_core
    assert n_z == n_y == n_ref == 4 and n_core == 2

    def place_of(g):
        return g // (n_y * n_core), (g // n_core) % n_y, g % n_core

    def gen_perm(move):
        out = []
        for g in range(n_gen):
            z, y, c = move(*place_of(g))
            out.append((g, ((z % n_z) * n_y + y % n_y) * n_core + c % n_core))
        return out

    core_stage = [gen_perm(lambda z, y, c: (z, y, c + 1))]
    y_stage = [gen_perm(lambda z, y, c: (z, y + k, c)) for k in (1, 2, 3)]
    z_stage = [gen_perm(lambda z, y, c: (z + k, y, c)) for k in (1, 2, 3)]
    ref_stage = [[(i, (i + k) % n_ref) for i in range(n_ref)] for k in (1, 2, 3)]
    first_axis = {k: gen_perm(lambda z, y, c: (z, y + k, c) if c == 0 else (z + k, y, c)) for k in (1, 2, 3)}
    second_axis = {k: gen_perm(lambda z, y, c: (z + k, y, c) if c == 0 else (z, y + k, c)) for k in (1, 3)}
    order = [(0, 0), (0, 1), (0, 2), (0, 3)]
    order += [(1, 0), (1, 1), (1, 2), (1, 3), (3, 0), (3, 1), (3, 2), (3, 3)]
    order += [(2, 0), (2, 1), (2, 2), (2, 3)]

    def shift(value, axis, perms):
        return [lax.ppermute(value, axis, perm) for perm in perms]

    def merge(parts, logs):
        top = log_add([part[:logs] for part in parts])
        if parts[0].shape[0] == logs:
            return top
        return jnp.concatenate([top, sum(part[logs:] for part in parts)], axis=0)

    def stage(value, axis, perms, logs):
        return merge([value] + shift(value, axis, perms), logs)

    def doubled(value, logs):
        for bit in (1, 2):
            value = merge([value, lax.ppermute(value, "ref", [(i, i ^ bit) for i in range(n_ref)])], logs)
        return value

    def run(gen_features, gen_weight, ref_features, ref_weight, ref_self):
        gen_count = gen_features.shape[0]
        ref_count = ref_features.shape[0]
        nq, nc = gen_count // LANES, ref_count // LANES
        g = lax.axis_index("gen")
        x = lax.axis_index("ref")
        z, y, core = place_of(g)
        zy = z * n_y + y
        b, a = (lax.broadcasted_iota(jnp.int32, (len(order),), 0) for _ in range(2))
        b = functools.reduce(lambda v, k: jnp.where(a == k, order[k][0], v), range(len(order)), b)
        a = a % 4
        mine = ((z - b + n_z) % n_z) * n_y + (y - a + n_y) % n_y
        other = ((z - a + n_z) % n_z) * n_y + (y - b + n_y) % n_y
        place = jnp.where(core == 0, mine, other)
        wg = gen_weight.reshape(nq, LANES)
        wr = ref_weight.reshape(nc, LANES)
        at_zy = (lax.broadcasted_iota(jnp.int32, (n_zy, LANES), 0) == zy).astype(F32)
        at_x = (lax.broadcasted_iota(jnp.int32, (n_ref, LANES), 0) == x).astype(F32)
        wg, place, at_zy, at_x = lax.optimization_barrier((wg, place, at_zy, at_x))

        def to_cols(rows):
            picked = jnp.sum(jnp.where(at_x > 0, rows, 0.0), axis=0, keepdims=True)
            return jnp.where(at_zy > 0, picked, 0.0)

        def to_rows(cols):
            picked = jnp.sum(jnp.where(at_zy > 0, cols, 0.0), axis=0, keepdims=True)
            return jnp.where(at_x > 0, picked, 0.0)

        own = lax.dynamic_slice_in_dim(gen_features, x * LANES, LANES, 0)
        got = [lax.ppermute(own, "gen", first_axis[k]) for k in (1, 2, 3)]
        mate = lax.ppermute(gen_features, "gen", core_stage[0])
        near = jnp.concatenate([own] + got, axis=0)
        up = lax.ppermute(near, "gen", second_axis[1])
        down = lax.ppermute(near, "gen", second_axis[3])
        low_far = lax.ppermute(up[: 2 * LANES], "gen", second_axis[1])
        high_far = lax.ppermute(down[2 * LANES :], "gen", second_axis[3])

        d0, row0, lcol0, hcol0, mine, gmass, held, ahead = first_pass(0, 2, gen_features, ref_features, wr, wg)
        theirs = lax.ppermute(mine, "gen", core_stage[0])
        d1, row1, lcol1, hcol1 = first_pass(1, 2, held, ref_features, wr, mine, ahead)
        hcol = jnp.concatenate([hcol0, hcol1], axis=0)
        hrow = mine[:nq]
        weight = jnp.concatenate([wg, theirs[nq:]], axis=0)
        e0, z1_0, hs, ws = self_first(held, mate, [near], mine, theirs, place, 0)
        e1, z1_1 = self_first(held, mate, [up, down], hs, ws, place, 4)
        e2, z1_2 = self_first(held, mate, [low_far, high_far], hs, ws, place, 12)
        e = [e0, e1, e2]

        row_part = jnp.concatenate([log_add([row0[:nq], row1]), row0[nq:]], axis=0)
        row_part = doubled(row_part, nq)
        col_part = jnp.concatenate([lcol0, lcol1, gmass], axis=0)
        col_part = stage(col_part, "gen", core_stage, nc)
        col_part = jnp.concatenate([col_part, to_cols(wg)], axis=0)
        col_part = stage(col_part, "gen", y_stage, nc)
        col_part = stage(col_part, "gen", z_stage, nc)
        gmass = col_part[nc : nc + 1]
        rmass = row_part[nq : nq + 1]
        wcols = col_part[nc + 8 :] / gmass
        gmass_log = jnp.log2(gmass)
        rmass_log = jnp.log2(rmass)
        f = hrow - (row_part[:nq] - rmass_log)
        c = hcol - (col_part[:nc] - gmass_log)
        ubase = jnp.log2(wr) - rmass_log - hcol
        vbase = jnp.log2(wg) - gmass_log - hrow
        share = wg / gmass

        lrow, lcol = next_pass([d0, d1], ubase + c, vbase + f)
        lrow = doubled(lrow, nq)
        lcol = stage(lcol, "gen", core_stage, nc)
        col_part = jnp.concatenate([lcol, z1_0 + z1_1 + z1_2], axis=0)
        col_part = stage(col_part, "gen", y_stage, nc)
        col_part = stage(col_part, "gen", z_stage, nc)
        f = 0.5 * (f + (hrow - lrow))
        c = 0.5 * (c + (hcol - col_part[:nc]))
        y1 = col_part[nc:] / gmass

        lrow, lcol = next_pass([d0, d1], ubase + c, vbase + f)
        y2 = self_apply(self_rows_kernel, e, wcols / y1, place, 2 * nq)
        row_part = jnp.concatenate([lrow, y2, to_rows(-jnp.log2(y1))], axis=0)
        row_part = stage(row_part, "ref", ref_stage, nq)
        f = 0.5 * (f + (hrow - row_part[:nq]))
        f_part = share * f
        f_part = jnp.concatenate([f_part, f_part], axis=0)
        mine = jnp.concatenate([lcol, f_part, row_part[nq:]], axis=0)
        theirs = shift(mine, "gen", core_stage)[0]
        lcol = log_add([lcol, theirs[:nc]])
        f_part = f_part + theirs[nc : nc + 8]
        y2, y2_mate, s1 = row_part[nq : 2 * nq], row_part[2 * nq : 3 * nq], row_part[3 * nq :]
        at = nc + 8
        y2 = y2 + theirs[at + nq : at + 2 * nq]
        y2_mate = y2_mate + theirs[at : at + nq]
        s1 = jnp.concatenate([s1, theirs[at + 2 * nq :]], axis=0)
        s2 = 0.5 * (s1 - jnp.log2(jnp.concatenate([y2, y2_mate], axis=0)))
        w3 = weight / gmass * jnp.exp2(s2)
        z3 = self_apply(self_cols_kernel, e, w3, place, n_zy)
        col_part = jnp.concatenate([lcol, f_part, z3, to_cols(s2[:nq])], axis=0)
        col_part = stage(col_part, "gen", y_stage, nc)
        col_part = stage(col_part, "gen", z_stage, nc)
        c = 0.5 * (c + (hcol - col_part[:nc]))
        f_part = col_part[nc : nc + nq]
        z3, s2 = col_part[nc + 8 : nc + 8 + n_zy], col_part[nc + 8 + n_zy :]

        unit = EPS / LOG2E
        ref_gap = c * unit - ref_self.reshape(nc, LANES)
        s3 = 0.5 * (s2 - jnp.log2(z3))
        s_part = jnp.sum((wcols * s3).reshape(2, 8, LANES), axis=0)
        s_part = s_part + shift(s_part, "gen", core_stage)[0]
        part = jnp.sum(((wr / rmass) * ref_gap).reshape(nc // 8, 8, LANES), axis=0) - unit * s_part
        row_part = jnp.concatenate([to_rows(s3), part], axis=0)
        row_part = row_part + sum(shift(row_part, "ref", ref_stage))
        gen_gap = (f - row_part[:nq]) * unit
        divergence = jnp.sum(unit * f_part + row_part[nq : 2 * nq] + row_part[2 * nq :])
        return gen_gap.reshape(gen_count), ref_gap.reshape(ref_count), divergence

    return run


def solution(mesh):
    n_gen, n_ref = mesh.shape["gen"], mesh.shape["ref"]
    n_core = 2
    n_y = 1
    while n_y * n_y * n_core < n_gen:
        n_y *= 2
    placed = (P("gen", None), P("gen"), P("ref", None), P("ref"), P("ref"))
    return jax.shard_map(
        build(n_gen // (n_y * n_core), n_y, n_core, n_ref),
        mesh=mesh,
        in_specs=placed,
        out_specs=(P("gen"), P("ref"), P()),
        check_vma=False,
    )
```

```python
import functools

import jax
import jax.numpy as jnp
from jax import lax
from jax.experimental import pallas as pl
from jax.experimental.pallas import tpu as pltpu
from jax.sharding import PartitionSpec as P


EPS = 0.1
LOG2E = 1.4426950408889634
F32 = jnp.float32
LANES = 128
TILE = 512
ROWS = 32
LOW = 2.0**-80
HIGH = 2.0**120


def vmem_array(x):
    return pltpu.with_memory_space_constraint(x, pltpu.VMEM)


def hbm_array(x):
    return pltpu.with_memory_space_constraint(x, pltpu.HBM)


def spread(vec_ref, out_ref, count, first=0, at=0):
    for q in range(count):
        block = jnp.broadcast_to(vec_ref[first + q : first + q + 1, :], (LANES, LANES))
        out_ref[(at + q) * LANES : (at + q + 1) * LANES, :] = block.T


def lane_fold(acc, op):
    return op(acc.T, axis=0, keepdims=True)


def norms(feat_ref, start, count, scale):
    width = feat_ref.shape[1]
    out = []
    for q in range(count):
        acc = jnp.zeros((LANES, LANES), F32)
        for c in range(width // LANES):
            x = feat_ref[start + q * LANES : start + (q + 1) * LANES, c * LANES : (c + 1) * LANES].astype(F32)
            acc = acc + x * x
        out.append(lane_fold(acc, jnp.sum) * scale)
    return out


def row_block(r):
    if isinstance(r, int):
        return slice(r * ROWS, (r + 1) * ROWS)
    return pl.ds(pl.multiple_of(r * ROWS, ROWS), ROWS)


def sweep(d_ref, base, chunks, u, vs_ref, rowacc_ref, straight=False, keep=None):
    rows = d_ref.shape[0]

    def body(r, cols):
        at = row_block(r)
        vs = vs_ref[at, :]
        racc = rowacc_ref[at, :]
        out = []
        for c in range(chunks):
            d = d_ref[at, pl.ds(base + c * LANES, LANES)]
            if keep is not None:
                keep[0][at, pl.ds(pl.multiple_of(keep[1] + c * LANES, LANES), LANES)] = d
            p = jnp.exp2((d + u[c]) + vs)
            racc = racc + p
            out.append(cols[c] + jnp.sum(p.reshape(ROWS // 8, 8, LANES), axis=0))
        rowacc_ref[at, :] = racc
        return tuple(out)

    cols = (jnp.zeros((8, LANES), F32),) * chunks
    if straight:
        for r in range(rows // ROWS):
            cols = body(r, cols)
    else:
        cols = lax.fori_loop(0, rows // ROWS, body, cols, unroll=4)
    return [jnp.sum(c, axis=0, keepdims=True) for c in cols]


def tile_peak(d_ref, u, vs_ref):
    rows = d_ref.shape[0]
    best = jnp.full((8, LANES), -3.0e38, F32)

    def body(r, best):
        at = pl.ds(pl.multiple_of(r * ROWS, ROWS), ROWS)
        val = (d_ref[at, 0:LANES] + u) + vs_ref[at, :]
        return jnp.maximum(best, jnp.max(val.reshape(ROWS // 8, 8, LANES), axis=0))

    best = lax.fori_loop(0, rows // ROWS, body, best, unroll=2)
    return jnp.max(jnp.max(best, axis=0, keepdims=True), axis=1, keepdims=True)


def start_peak(d_ref, u0, v_ref, vs_ref, peak_ref, rowacc_ref):
    rows = d_ref.shape[0]
    spread(v_ref, vs_ref, rows // LANES)
    peak = jnp.broadcast_to(tile_peak(d_ref, u0, vs_ref), (8, LANES))
    peak_ref[...] = peak
    vs_ref[...] = vs_ref[...] - peak[0:1, :]
    rowacc_ref[...] = jnp.zeros_like(rowacc_ref)


def finish(d_refs, u_ref, v_ref, vs_ref, rowacc_ref, colsum_ref, peak_ref, lrow_ref, lcol_ref):
    rows = d_refs[0].shape[0]
    nq = rows // LANES
    rowsum = [lane_fold(rowacc_ref[q * LANES : (q + 1) * LANES, :], jnp.sum) for q in range(nq)]
    rowsum = jnp.concatenate(rowsum, axis=0)
    colsum = colsum_ref[...]
    low = jnp.minimum(jnp.min(rowsum), jnp.min(colsum))
    high = jnp.maximum(jnp.max(rowsum), jnp.max(colsum))
    good = jnp.logical_and(low >= LOW, high <= HIGH)
    peak = peak_ref[0:1, :]

    @pl.when(good)
    def _():
        lrow_ref[0:nq, :] = (jnp.log2(rowsum) + peak) - v_ref[...]
        lcol_ref[...] = (jnp.log2(colsum) + peak) - u_ref[...]

    @pl.when(jnp.logical_not(good))
    def _():
        spread(v_ref, vs_ref, nq)

        def row_block(q, carry):
            part = pl.ds(pl.multiple_of(q * LANES, LANES), LANES)

            def scores(d_ref, first, c):
                at = pl.ds(pl.multiple_of(c * LANES, LANES), LANES)
                return d_ref[part, at] + u_ref[pl.ds(first + c, 1), :]

            best = jnp.full((LANES, LANES), -3.0e38, F32)
            first = 0
            for d_ref in d_refs:
                count = d_ref.shape[1] // LANES
                best = lax.fori_loop(
                    0, count, lambda c, best: jnp.maximum(best, scores(d_ref, first, c)), best
                )
                first += count
            top = jnp.max(best, axis=1, keepdims=True)
            acc = jnp.zeros((LANES, LANES), F32)
            first = 0
            for d_ref in d_refs:
                count = d_ref.shape[1] // LANES
                acc = lax.fori_loop(
                    0, count, lambda c, acc: acc + jnp.exp2(scores(d_ref, first, c) - top), acc
                )
                first += count
            log_sum = jnp.log2(jnp.sum(acc, axis=1, keepdims=True)) + top
            lrow_ref[pl.ds(q, 1), :] = lane_fold(jnp.broadcast_to(log_sum, (LANES, LANES)), jnp.max)
            return carry

        lax.fori_loop(0, nq, row_block, 0)
        first = 0
        for d_ref in d_refs:
            count = d_ref.shape[1] // LANES

            def column(c, carry):
                at = pl.ds(pl.multiple_of(c * LANES, LANES), LANES)

                def block(r):
                    part = pl.ds(pl.multiple_of(r * ROWS, ROWS), ROWS)
                    return d_ref[part, at] + vs_ref[part, :]

                top = lax.fori_loop(
                    0,
                    rows // ROWS,
                    lambda r, best: jnp.maximum(best, jnp.max(block(r), axis=0, keepdims=True)),
                    jnp.full((1, LANES), -3.0e38, F32),
                )
                total = lax.fori_loop(
                    0,
                    rows // ROWS,
                    lambda r, acc: acc + jnp.sum(jnp.exp2(block(r) - top), axis=0, keepdims=True),
                    jnp.zeros((1, LANES), F32),
                )
                lcol_ref[pl.ds(first + c, 1), :] = top + jnp.log2(total)
                return carry

            lax.fori_loop(0, count, column, 0)
            first += count


def entry_kernel(gen_hbm, ref_hbm, gweight_hbm, rweight_hbm, own_ref, gen_ref, tile_ref, gweight_ref, rweight_ref, sem):
    count = own_ref.shape[0]
    at = pl.ds(pl.multiple_of(lax.axis_index("ref") * count, count), count)
    pairs = (
        (gen_hbm.at[at, :], own_ref),
        (gweight_hbm, gweight_ref),
        (rweight_hbm, rweight_ref),
        (gen_hbm, gen_ref),
        (ref_hbm.at[: tile_ref.shape[0], :], tile_ref),
    )
    copies = [pltpu.make_async_copy(src, dst, sem.at[k]) for k, (src, dst) in enumerate(pairs)]
    for copy in copies:
        copy.start()
    for copy in copies:
        copy.wait()


def entry(gen, ref, gweight, rweight):
    vmem = pl.BlockSpec(memory_space=pltpu.VMEM)
    hbm = pl.BlockSpec(memory_space=pltpu.HBM)
    width = gen.shape[1]
    return pl.pallas_call(
        entry_kernel,
        in_specs=[hbm] * 4,
        out_shape=(
            pltpu.VMEM((LANES, width), gen.dtype),
            pltpu.VMEM(gen.shape, gen.dtype),
            pltpu.VMEM((TILE, width), ref.dtype),
            pltpu.VMEM(gweight.shape, F32),
            pltpu.VMEM(rweight.shape, F32),
        ),
        out_specs=(vmem,) * 5,
        scratch_shapes=[pltpu.SemaphoreType.DMA((5,))],
        compiler_params=pltpu.CompilerParams(vmem_limit_bytes=4 << 20),
        name="entry",
    )(*[hbm_array(x) for x in (gen, ref, gweight, rweight)])


def total(x):
    return jnp.sum(jnp.sum(x, axis=0, keepdims=True), axis=1, keepdims=True)


def first_kernel(offset, steps, *refs):
    if offset == 0:
        gen_ref, first_ref, gweight_ref, rweight_ref, ref_hbm, *refs = refs
        d_ref, hcol_ref, hrow_ref, mass_ref, ahead_ref, vs_ref, rowacc_ref, u_ref, colsum_ref, peak_ref, *refs = refs
        tile_ref, stage_ref, v_ref, sem = refs
    else:
        gen_ref, first_ref, rweight_ref, hrow_ref, ref_hbm, before_ref, *refs = refs
        hcol0_ref, vs_ref, rowacc0_ref, u0_ref, colsum0_ref, peak_ref, *refs = refs
        d_ref, lrow_ref, lcol_ref, hcol_ref, tile_ref, stage_ref, v_ref, rowacc_ref, u_ref, colsum_ref, sem = refs
    rows, width = gen_ref.shape
    nq, nc = rows // LANES, d_ref.shape[1] // LANES
    chunks = TILE // LANES
    half_scale = 0.5 * LOG2E / (EPS * width)
    dot_scale = LOG2E / (EPS * width)
    first_tile = offset * steps

    def load(j):
        at = pl.ds(pl.multiple_of((first_tile + j) * TILE, TILE), TILE)
        return pltpu.make_async_copy(ref_hbm.at[at, :], tile_ref.at[j], sem.at[j])

    def product(j, tile, out_ref, columns):
        for c, half in enumerate(norms(tile, 0, chunks, half_scale)):
            row = pl.ds((first_tile + j) * chunks + c, 1)
            hcol_ref[row, :] = half
            u_ref[row, :] = jnp.log2(rweight_ref[row, :]) - half
        dots = lax.dot_general(gen_ref[...], tile[...], (((1,), (1,)), ((), ())), preferred_element_type=F32)
        out_ref[:, columns] = dots * dot_scale

    def sums(j, straight, src_ref, base, keep):
        mine = [u_ref[pl.ds(j * chunks + c, 1), :] for c in range(chunks)]
        for c, part in enumerate(sweep(src_ref, base, chunks, mine, vs_ref, rowacc_ref, straight, keep)):
            colsum_ref[pl.ds(j * chunks + c, 1), :] = part

    whole = slice(0, TILE)
    load(1).start()
    if offset == 0:
        ahead = pltpu.make_async_copy(ref_hbm.at[steps * TILE : (steps + 1) * TILE, :], ahead_ref, sem.at[steps])
        for q, part in enumerate(norms(gen_ref, 0, nq, half_scale)):
            hrow_ref[q : q + 1, :] = part
            v_ref[q : q + 1, :] = jnp.log2(gweight_ref[q : q + 1, :]) - part
            hrow_ref[nq + q : nq + q + 1, :] = gweight_ref[q : q + 1, :]
        mass_ref[...] = jnp.broadcast_to(total(gweight_ref[...]), (8, LANES))
        product(0, first_ref, stage_ref, whole)
        start_peak(stage_ref, u_ref[0:1, :], v_ref, vs_ref, peak_ref, rowacc_ref)
    else:
        v_ref[...] = jnp.log2(hrow_ref[nq : 2 * nq, :]) - hrow_ref[0:nq, :]
        lrow_ref[nq : 2 * nq, :] = jnp.broadcast_to(total(rweight_ref[...]), (nq, LANES))
        hcol_ref[0:nc, :] = hcol0_ref[...]
        rowacc_ref[...] = rowacc0_ref[...]
        u_ref[0:nc, :] = u0_ref[...]
        colsum_ref[0:nc, :] = colsum0_ref[...]
        sums(steps - 1, True, before_ref, (steps - 1) * TILE, None)
        product(0, first_ref, stage_ref, whole)

    def step(j, carry):
        load(j).wait()

        @pl.when(j + 1 < steps)
        def _():
            load(j + 1).start()

        sums(first_tile + j - 1, True, stage_ref, 0, (d_ref, (j - 1) * TILE))
        product(j, tile_ref.at[j], stage_ref, whole)
        return carry

    if offset == 0:
        lax.fori_loop(1, steps - 1, step, 0)
        load(steps - 1).wait()
        ahead.start()
        sums(steps - 2, True, stage_ref, 0, (d_ref, (steps - 2) * TILE))
        product(steps - 1, tile_ref.at[steps - 1], d_ref, slice((steps - 1) * TILE, steps * TILE))
        colsum_ref[(steps - 1) * chunks : steps * chunks, :] = jnp.zeros((chunks, LANES), F32)
        ahead.wait()
    else:
        lax.fori_loop(1, steps, step, 0)
        sums(first_tile + steps - 1, False, stage_ref, 0, (d_ref, (steps - 1) * TILE))
        finish([before_ref, d_ref], u_ref, v_ref, vs_ref, rowacc_ref, colsum_ref, peak_ref, lrow_ref, lcol_ref)


def first_pass(offset, pieces, gen, first, ref, *more):
    rows, width = gen.shape
    cols = ref.shape[0] // pieces
    steps = cols // TILE
    nq, nc = rows // LANES, cols // LANES
    vmem = pl.BlockSpec(memory_space=pltpu.VMEM)
    hbm = pl.BlockSpec(memory_space=pltpu.HBM)
    vec = lambda n: jax.ShapeDtypeStruct((n, LANES), F32)
    lanes = pltpu.VMEM((rows, LANES), F32)
    scratch = [
        pltpu.VMEM((steps, TILE, width), jnp.bfloat16),
        pltpu.VMEM((rows, TILE), F32),
        pltpu.VMEM((nq, LANES), F32),
    ]
    if offset == 0:
        gweight, rweight = more
        operands = [vmem_array(gen), vmem_array(first), gweight, rweight, hbm_array(ref)]
        outs = (
            pltpu.VMEM((rows, cols), F32), vec(nc), vec(2 * nq), vec(8), pltpu.VMEM((TILE, width), ref.dtype),
            lanes, lanes, vec(nc), vec(nc), vec(8),
        )
        specs = [vmem] * 4 + [hbm]
    else:
        rweight, hrow, before, hcol, vs, rowacc, u, colsum, peak = more
        operands = [vmem_array(gen), vmem_array(first), rweight, hrow, hbm_array(ref), vmem_array(before)]
        operands += [hcol, vmem_array(vs), vmem_array(rowacc), u, colsum, peak]
        outs = (pltpu.VMEM((rows, cols), F32), vec(2 * nq), vec(2 * nc), vec(2 * nc))
        specs = [vmem] * 4 + [hbm] + [vmem] * 7
        scratch += [
            pltpu.VMEM((rows, LANES), F32),
            pltpu.VMEM((2 * nc, LANES), F32),
            pltpu.VMEM((2 * nc, LANES), F32),
        ]
    return pl.pallas_call(
        functools.partial(first_kernel, offset, steps),
        in_specs=specs,
        out_shape=outs,
        out_specs=(vmem,) * len(outs),
        scratch_shapes=scratch + [pltpu.SemaphoreType.DMA((steps + 1,))],
        compiler_params=pltpu.CompilerParams(vmem_limit_bytes=16 << 20),
    )(*operands)


def next_kernel(count, *refs):
    sources = refs[:count]
    u_ref, v_ref, lrow_ref, lcol_ref, vs_ref, rowacc_ref, colsum_ref, peak_ref = refs[count:]
    chunks = TILE // LANES
    start_peak(sources[0], u_ref[0:1, :], v_ref, vs_ref, peak_ref, rowacc_ref)
    first = 0
    for d_ref in sources:
        steps = d_ref.shape[1] // TILE

        def step(j, carry):
            u = [u_ref[pl.ds(first + j * chunks + c, 1), :] for c in range(chunks)]
            base = pl.multiple_of(j * TILE, TILE)
            for c, part in enumerate(sweep(d_ref, base, chunks, u, vs_ref, rowacc_ref)):
                colsum_ref[pl.ds(first + j * chunks + c, 1), :] = part
            return carry

        lax.fori_loop(0, steps, step, 0)
        first += steps * chunks
    finish(sources, u_ref, v_ref, vs_ref, rowacc_ref, colsum_ref, peak_ref, lrow_ref, lcol_ref)


def next_pass(parts, u, v):
    rows = parts[0].shape[0]
    cols = sum(part.shape[1] for part in parts)
    nq, nc = rows // LANES, cols // LANES
    vmem = pl.BlockSpec(memory_space=pltpu.VMEM)
    return pl.pallas_call(
        functools.partial(next_kernel, len(parts)),
        in_specs=[vmem] * (len(parts) + 2),
        out_shape=(jax.ShapeDtypeStruct((nq, LANES), F32), jax.ShapeDtypeStruct((nc, LANES), F32)),
        out_specs=(vmem, vmem),
        scratch_shapes=[
            pltpu.VMEM((rows, LANES), F32),
            pltpu.VMEM((rows, LANES), F32),
            pltpu.VMEM((nc, LANES), F32),
            pltpu.VMEM((8, LANES), F32),
        ],
        compiler_params=pltpu.CompilerParams(vmem_limit_bytes=8 << 20),
    )(*[vmem_array(part) for part in parts], u, v)


def self_first_kernel(count, first, *refs):
    own_ref, mate_ref = refs[:2]
    sources = refs[2 : 2 + count]
    rest = refs[2 + count :]
    half, width = own_ref.shape
    nq = half // LANES
    if first == 0:
        mine_ref, theirs_ref, place_ref, e_ref, z_ref, hs_ref, ws_ref = rest
        for at, vec_ref in ((0, mine_ref), (nq, theirs_ref)):
            spread(vec_ref, hs_ref, nq, 0, at)
            spread(vec_ref, ws_ref, nq, nq, at)
    else:
        hs_ref, ws_ref, place_ref, e_ref, z_ref = rest
    wide = 256
    chunks = wide // LANES
    half_scale = 0.5 * LOG2E / (EPS * width)
    dot_scale = LOG2E / (EPS * width)
    z_ref[...] = jnp.zeros_like(z_ref)
    tiles = [(src, k) for src in sources for k in range(src.shape[0] // wide)]
    piece_half = {}

    def product(t):
        src, k = tiles[t]
        view = src.at[k * wide : (k + 1) * wide, :]
        piece_half[t] = norms(view, 0, chunks, half_scale)
        for h, rows_ref in enumerate((own_ref, mate_ref)):
            e_ref[h * half : (h + 1) * half, t * wide : (t + 1) * wide] = lax.dot_general(
                rows_ref[...], view[...], (((1,), (1,)), ((), ())), preferred_element_type=F32
            )

    def sums(t, straight):
        def body(r, acc):
            at = row_block(r)
            hs = hs_ref[at, :]
            ws = ws_ref[at, :]
            out = []
            for c in range(chunks):
                part = slice(t * wide + c * LANES, t * wide + (c + 1) * LANES)
                e = jnp.exp2(e_ref[at, part] * dot_scale - (hs + piece_half[t][c]))
                e_ref[at, part] = e
                out.append(acc[c] + jnp.sum((e * ws).reshape(ROWS // 8, 8, LANES), axis=0))
            return tuple(out)

        acc = (jnp.zeros((8, LANES), F32),) * chunks
        if straight:
            for r in range(2 * half // ROWS):
                acc = body(r, acc)
        else:
            acc = lax.fori_loop(0, 2 * half // ROWS, body, acc, unroll=2)
        for c in range(chunks):
            z_ref[pl.ds(place_ref[first + t * chunks + c], 1), :] = jnp.sum(acc[c], axis=0, keepdims=True)

    product(0)
    for t in range(1, len(tiles)):
        sums(t - 1, True)
        product(t)
    sums(len(tiles) - 1, False)


def self_first(own, mate, sources, left, right, place, first):
    rows = 2 * own.shape[0]
    cols = sum(src.shape[0] for src in sources)
    vmem = pl.BlockSpec(memory_space=pltpu.VMEM)
    lanes = () if first else (pltpu.VMEM((rows, LANES), F32),) * 2
    if first:
        left, right = vmem_array(left), vmem_array(right)
    return pl.pallas_call(
        functools.partial(self_first_kernel, len(sources), first),
        in_specs=[vmem] * (4 + len(sources)) + [pl.BlockSpec(memory_space=pltpu.SMEM)],
        out_shape=(pltpu.VMEM((rows, cols), F32), jax.ShapeDtypeStruct((place.shape[0], LANES), F32)) + lanes,
        out_specs=(vmem,) * (2 + len(lanes)),
        compiler_params=pltpu.CompilerParams(vmem_limit_bytes=8 << 20),
    )(vmem_array(own), vmem_array(mate), *[vmem_array(src) for src in sources], left, right, place)


def self_cols_kernel(count, *refs):
    w_ref, place_ref, z_ref, ws_ref = refs[count:]
    rows = refs[0].shape[0]
    chunks = 256 // LANES
    spread(w_ref, ws_ref, rows // LANES)
    zero = jnp.zeros((8, LANES), F32)
    first = 0
    for e_ref in refs[:count]:
        steps = e_ref.shape[1] // 256

        def tile(t, carry):
            base = pl.multiple_of(t * 256, 256)

            def body(r, acc):
                at = pl.ds(pl.multiple_of(r * ROWS, ROWS), ROWS)
                ws = ws_ref[at, :]
                out = []
                for c in range(chunks):
                    e = e_ref[at, pl.ds(base + c * LANES, LANES)] * ws
                    out.append(acc[c] + jnp.sum(e.reshape(ROWS // 8, 8, LANES), axis=0))
                return tuple(out)

            acc = lax.fori_loop(0, rows // ROWS, body, (zero,) * chunks, unroll=4)
            for c in range(chunks):
                z_ref[pl.ds(place_ref[first + t * chunks + c], 1), :] = jnp.sum(acc[c], axis=0, keepdims=True)
            return carry

        lax.fori_loop(0, steps, tile, 0)
        first += steps * chunks


def self_rows_kernel(count, *refs):
    w_ref, place_ref, y_ref, rowacc_ref = refs[count:]
    rows = refs[0].shape[0]
    chunks = 512 // LANES
    rowacc_ref[...] = jnp.zeros_like(rowacc_ref)
    first = 0
    for e_ref in refs[:count]:
        steps = e_ref.shape[1] // 512

        def tile(t, carry):
            base = pl.multiple_of(t * 512, 512)
            w = [w_ref[pl.ds(place_ref[first + t * chunks + c], 1), :] for c in range(chunks)]

            def body(r, carry):
                at = pl.ds(pl.multiple_of(r * ROWS, ROWS), ROWS)
                acc = rowacc_ref[at, :]
                for c in range(chunks):
                    acc = acc + e_ref[at, pl.ds(base + c * LANES, LANES)] * w[c]
                rowacc_ref[at, :] = acc
                return carry

            return lax.fori_loop(0, rows // ROWS, body, carry, unroll=4)

        lax.fori_loop(0, steps, tile, 0)
        first += steps * chunks
    for q in range(rows // LANES):
        y_ref[q : q + 1, :] = lane_fold(rowacc_ref[q * LANES : (q + 1) * LANES, :], jnp.sum)


def self_apply(kernel, parts, w, place, out_rows):
    rows = parts[0].shape[0]
    vmem = pl.BlockSpec(memory_space=pltpu.VMEM)
    return pl.pallas_call(
        functools.partial(kernel, len(parts)),
        in_specs=[vmem] * (len(parts) + 1) + [pl.BlockSpec(memory_space=pltpu.SMEM)],
        out_shape=jax.ShapeDtypeStruct((out_rows, LANES), F32),
        out_specs=vmem,
        scratch_shapes=[pltpu.VMEM((rows, LANES), F32)],
        compiler_params=pltpu.CompilerParams(vmem_limit_bytes=8 << 20),
    )(*[vmem_array(part) for part in parts], w, place)


def log_add(parts):
    top = functools.reduce(jnp.maximum, parts)
    return top + jnp.log2(sum(jnp.exp2(part - top) for part in parts))


def build(n_z, n_y, n_core, n_ref):
    n_zy = n_z * n_y
    n_gen = n_zy * n_core
    assert n_z == n_y == n_ref == 4 and n_core == 2

    def place_of(g):
        return g // (n_y * n_core), (g // n_core) % n_y, g % n_core

    def gen_perm(move):
        out = []
        for g in range(n_gen):
            z, y, c = move(*place_of(g))
            out.append((g, ((z % n_z) * n_y + y % n_y) * n_core + c % n_core))
        return out

    core_stage = [gen_perm(lambda z, y, c: (z, y, c + 1))]
    y_stage = [gen_perm(lambda z, y, c: (z, y + k, c)) for k in (1, 2, 3)]
    z_stage = [gen_perm(lambda z, y, c: (z + k, y, c)) for k in (1, 2, 3)]
    ref_stage = [[(i, (i + k) % n_ref) for i in range(n_ref)] for k in (1, 2, 3)]
    first_axis = {k: gen_perm(lambda z, y, c: (z, y + k, c) if c == 0 else (z + k, y, c)) for k in (1, 2, 3)}
    second_axis = {k: gen_perm(lambda z, y, c: (z + k, y, c) if c == 0 else (z, y + k, c)) for k in (1, 3)}
    order = [(0, 0), (0, 1), (0, 2), (0, 3)]
    order += [(1, 0), (1, 1), (1, 2), (1, 3), (3, 0), (3, 1), (3, 2), (3, 3)]
    order += [(2, 0), (2, 1), (2, 2), (2, 3)]

    def shift(value, axis, perms):
        return [lax.ppermute(value, axis, perm) for perm in perms]

    def merge(parts, logs):
        top = log_add([part[:logs] for part in parts])
        if parts[0].shape[0] == logs:
            return top
        return jnp.concatenate([top, sum(part[logs:] for part in parts)], axis=0)

    def stage(value, axis, perms, logs):
        return merge([value] + shift(value, axis, perms), logs)

    def doubled(value, logs):
        for flip in (1, n_ref - 1):
            value = merge([value, lax.ppermute(value, "ref", [(i, i ^ flip) for i in range(n_ref)])], logs)
        return value

    def run(gen_features, gen_weight, ref_features, ref_weight, ref_self):
        gen_count = gen_features.shape[0]
        ref_count = ref_features.shape[0]
        nq, nc = gen_count // LANES, ref_count // LANES
        g = lax.axis_index("gen")
        x = lax.axis_index("ref")
        z, y, core = place_of(g)
        zy = z * n_y + y
        b, a = (lax.broadcasted_iota(jnp.int32, (len(order),), 0) for _ in range(2))
        b = functools.reduce(lambda v, k: jnp.where(a == k, order[k][0], v), range(len(order)), b)
        a = a % 4
        mine = ((z - b + n_z) % n_z) * n_y + (y - a + n_y) % n_y
        other = ((z - a + n_z) % n_z) * n_y + (y - b + n_y) % n_y
        place = jnp.where(core == 0, mine, other)
        at_zy = (lax.broadcasted_iota(jnp.int32, (n_zy, LANES), 0) == zy).astype(F32)
        at_x = (lax.broadcasted_iota(jnp.int32, (n_ref, LANES), 0) == x).astype(F32)
        wg = gen_weight.reshape(nq, LANES)
        wg, place, at_zy, at_x = lax.optimization_barrier((wg, place, at_zy, at_x))
        own, held, tile0, wg, wr = entry(
            gen_features, ref_features, wg, ref_weight.reshape(nc, LANES)
        )

        def to_cols(rows):
            picked = jnp.sum(jnp.where(at_x > 0, rows, 0.0), axis=0, keepdims=True)
            return jnp.where(at_zy > 0, picked, 0.0)

        def to_rows(cols):
            picked = jnp.sum(jnp.where(at_zy > 0, cols, 0.0), axis=0, keepdims=True)
            return jnp.where(at_x > 0, picked, 0.0)

        got = [lax.ppermute(own, "gen", first_axis[k]) for k in (1, 2, 3)]
        mate = lax.ppermute(held, "gen", core_stage[0])
        near = jnp.concatenate([own] + got, axis=0)
        up = lax.ppermute(near, "gen", second_axis[1])
        down = lax.ppermute(near, "gen", second_axis[3])
        low_far = lax.ppermute(up[: 2 * LANES], "gen", second_axis[1])
        high_far = lax.ppermute(down[2 * LANES :], "gen", second_axis[3])

        d0, hcol, mine, gmass, ahead, *carried = first_pass(0, 2, held, tile0, ref_features, wg, wr)
        theirs = lax.ppermute(mine, "gen", core_stage[0])
        d1, row_part, lcol, hcol = first_pass(1, 2, held, ahead, ref_features, wr, mine, d0, hcol, *carried)
        hrow = mine[:nq]
        weight = jnp.concatenate([wg, theirs[nq:]], axis=0)
        e0, z1_0, hs, ws = self_first(held, mate, [near], mine, theirs, place, 0)
        e1, z1_1 = self_first(held, mate, [up, down], hs, ws, place, 4)
        e2, z1_2 = self_first(held, mate, [low_far, high_far], hs, ws, place, 12)
        e = [e0, e1, e2]

        row_part = doubled(row_part, nq)
        col_part = jnp.concatenate([lcol, gmass], axis=0)
        col_part = stage(col_part, "gen", core_stage, nc)
        col_part = jnp.concatenate([col_part, to_cols(wg)], axis=0)
        col_part = stage(col_part, "gen", y_stage, nc)
        col_part = stage(col_part, "gen", z_stage, nc)
        gmass = col_part[nc : nc + 1]
        rmass = row_part[nq : nq + 1]
        wcols = col_part[nc + 8 :] / gmass
        gmass_log = jnp.log2(gmass)
        rmass_log = jnp.log2(rmass)
        f = hrow - (row_part[:nq] - rmass_log)
        c = hcol - (col_part[:nc] - gmass_log)
        ubase = jnp.log2(wr) - rmass_log - hcol
        vbase = jnp.log2(wg) - gmass_log - hrow
        share = wg / gmass

        lrow, lcol = next_pass([d0, d1], ubase + c, vbase + f)
        lrow = doubled(lrow, nq)
        lcol = stage(lcol, "gen", core_stage, nc)
        col_part = jnp.concatenate([lcol, z1_0 + z1_1 + z1_2], axis=0)
        col_part = stage(col_part, "gen", y_stage, nc)
        col_part = stage(col_part, "gen", z_stage, nc)
        f = 0.5 * (f + (hrow - lrow))
        c = 0.5 * (c + (hcol - col_part[:nc]))
        y1 = col_part[nc:] / gmass

        lrow, lcol = next_pass([d0, d1], ubase + c, vbase + f)
        y2 = self_apply(self_rows_kernel, e, wcols / y1, place, 2 * nq)
        row_part = jnp.concatenate([lrow, y2, to_rows(-jnp.log2(y1))], axis=0)
        row_part = stage(row_part, "ref", ref_stage, nq)
        f = 0.5 * (f + (hrow - row_part[:nq]))
        f_part = share * f
        f_part = jnp.concatenate([f_part, f_part], axis=0)
        mine = jnp.concatenate([lcol, f_part, row_part[nq:]], axis=0)
        theirs = shift(mine, "gen", core_stage)[0]
        lcol = log_add([lcol, theirs[:nc]])
        f_part = f_part + theirs[nc : nc + 8]
        y2, y2_mate, s1 = row_part[nq : 2 * nq], row_part[2 * nq : 3 * nq], row_part[3 * nq :]
        at = nc + 8
        y2 = y2 + theirs[at + nq : at + 2 * nq]
        y2_mate = y2_mate + theirs[at : at + nq]
        s1 = jnp.concatenate([s1, theirs[at + 2 * nq :]], axis=0)
        s2 = 0.5 * (s1 - jnp.log2(jnp.concatenate([y2, y2_mate], axis=0)))
        w3 = weight / gmass * jnp.exp2(s2)
        z3 = self_apply(self_cols_kernel, e, w3, place, n_zy)
        col_part = jnp.concatenate([lcol, f_part, z3, to_cols(s2[:nq])], axis=0)
        col_part = stage(col_part, "gen", y_stage, nc)
        col_part = stage(col_part, "gen", z_stage, nc)
        c = 0.5 * (c + (hcol - col_part[:nc]))
        f_part = col_part[nc : nc + nq]
        z3, s2 = col_part[nc + 8 : nc + 8 + n_zy], col_part[nc + 8 + n_zy :]

        unit = EPS / LOG2E
        ref_gap = c * unit - ref_self.reshape(nc, LANES)
        s3 = 0.5 * (s2 - jnp.log2(z3))
        s_part = jnp.sum((wcols * s3).reshape(2, 8, LANES), axis=0)
        s_part = s_part + shift(s_part, "gen", core_stage)[0]
        part = jnp.sum(((wr / rmass) * ref_gap).reshape(nc // 8, 8, LANES), axis=0) - unit * s_part
        row_part = jnp.concatenate([to_rows(s3), part], axis=0)
        row_part = row_part + sum(shift(row_part, "ref", ref_stage))
        gen_gap = (f - row_part[:nq]) * unit
        divergence = jnp.sum(unit * f_part + row_part[nq : 2 * nq] + row_part[2 * nq :])
        return gen_gap.reshape(gen_count), ref_gap.reshape(ref_count), divergence

    return run


def solution(mesh):
    n_gen, n_ref = mesh.shape["gen"], mesh.shape["ref"]
    n_core = 2
    n_y = 1
    while n_y * n_y * n_core < n_gen:
        n_y *= 2
    placed = (P("gen", None), P("gen"), P("ref", None), P("ref"), P("ref"))
    return jax.shard_map(
        build(n_gen // (n_y * n_core), n_y, n_core, n_ref),
        mesh=mesh,
        in_specs=placed,
        out_specs=(P("gen"), P("ref"), P()),
        check_vma=False,
    )
```

```python
import functools

import jax
import jax.numpy as jnp
from jax import lax
from jax.experimental import pallas as pl
from jax.experimental.pallas import tpu as pltpu
from jax.sharding import PartitionSpec as P


EPS = 0.1
LOG2E = 1.4426950408889634
F32 = jnp.float32
LANES = 128
TILE = 512
ROWS = 32
LEAD = 5
LOW = 2.0**-80
HIGH = 2.0**120


def vmem_array(x):
    return pltpu.with_memory_space_constraint(x, pltpu.VMEM)


def hbm_array(x):
    return pltpu.with_memory_space_constraint(x, pltpu.HBM)


def spread(vec_ref, out_ref, count, first=0, at=0):
    for q in range(count):
        block = jnp.broadcast_to(vec_ref[first + q : first + q + 1, :], (LANES, LANES))
        out_ref[(at + q) * LANES : (at + q + 1) * LANES, :] = block.T


def lane_fold(acc, op):
    return op(acc.T, axis=0, keepdims=True)


def norms(feat_ref, start, count, scale):
    width = feat_ref.shape[1]
    out = []
    for q in range(count):
        acc = jnp.zeros((LANES, LANES), F32)
        for c in range(width // LANES):
            x = feat_ref[start + q * LANES : start + (q + 1) * LANES, c * LANES : (c + 1) * LANES].astype(F32)
            acc = acc + x * x
        out.append(lane_fold(acc, jnp.sum) * scale)
    return out


def row_block(r):
    if isinstance(r, int):
        return slice(r * ROWS, (r + 1) * ROWS)
    return pl.ds(pl.multiple_of(r * ROWS, ROWS), ROWS)


def sweep(d_ref, base, chunks, u, vs_ref, rowacc_ref, straight=False, keep=None):
    rows = d_ref.shape[0]

    def body(r, cols):
        at = row_block(r)
        vs = vs_ref[at, :]
        racc = rowacc_ref[at, :]
        out = []
        for c in range(chunks):
            d = d_ref[at, pl.ds(base + c * LANES, LANES)]
            if keep is not None:
                keep[0][at, pl.ds(pl.multiple_of(keep[1] + c * LANES, LANES), LANES)] = d
            p = jnp.exp2((d + u[c]) + vs)
            racc = racc + p
            out.append(cols[c] + jnp.sum(p.reshape(ROWS // 8, 8, LANES), axis=0))
        rowacc_ref[at, :] = racc
        return tuple(out)

    cols = (jnp.zeros((8, LANES), F32),) * chunks
    if straight:
        for r in range(rows // ROWS):
            cols = body(r, cols)
    else:
        cols = lax.fori_loop(0, rows // ROWS, body, cols, unroll=4)
    return [jnp.sum(c, axis=0, keepdims=True) for c in cols]


def tile_peak(d_ref, u, vs_ref):
    rows = d_ref.shape[0]
    best = jnp.full((8, LANES), -3.0e38, F32)

    def body(r, best):
        at = pl.ds(pl.multiple_of(r * ROWS, ROWS), ROWS)
        val = (d_ref[at, 0:LANES] + u) + vs_ref[at, :]
        return jnp.maximum(best, jnp.max(val.reshape(ROWS // 8, 8, LANES), axis=0))

    best = lax.fori_loop(0, rows // ROWS, body, best, unroll=2)
    return jnp.max(jnp.max(best, axis=0, keepdims=True), axis=1, keepdims=True)


def start_peak(d_ref, u0, v_ref, vs_ref, peak_ref, rowacc_ref):
    rows = d_ref.shape[0]
    spread(v_ref, vs_ref, rows // LANES)
    peak = jnp.broadcast_to(tile_peak(d_ref, u0, vs_ref), (8, LANES))
    peak_ref[...] = peak
    vs_ref[...] = vs_ref[...] - peak[0:1, :]
    rowacc_ref[...] = jnp.zeros_like(rowacc_ref)


def finish(d_refs, u_ref, v_ref, vs_ref, rowacc_ref, colsum_ref, peak_ref, lrow_ref, lcol_ref):
    rows = d_refs[0].shape[0]
    nq = rows // LANES
    rowsum = [lane_fold(rowacc_ref[q * LANES : (q + 1) * LANES, :], jnp.sum) for q in range(nq)]
    rowsum = jnp.concatenate(rowsum, axis=0)
    colsum = colsum_ref[...]
    low = jnp.minimum(jnp.min(rowsum), jnp.min(colsum))
    high = jnp.maximum(jnp.max(rowsum), jnp.max(colsum))
    good = jnp.logical_and(low >= LOW, high <= HIGH)
    peak = peak_ref[0:1, :]

    @pl.when(good)
    def _():
        lrow_ref[0:nq, :] = (jnp.log2(rowsum) + peak) - v_ref[...]
        lcol_ref[...] = (jnp.log2(colsum) + peak) - u_ref[...]

    @pl.when(jnp.logical_not(good))
    def _():
        spread(v_ref, vs_ref, nq)

        def row_block(q, carry):
            part = pl.ds(pl.multiple_of(q * LANES, LANES), LANES)

            def scores(d_ref, first, c):
                at = pl.ds(pl.multiple_of(c * LANES, LANES), LANES)
                return d_ref[part, at] + u_ref[pl.ds(first + c, 1), :]

            best = jnp.full((LANES, LANES), -3.0e38, F32)
            first = 0
            for d_ref in d_refs:
                count = d_ref.shape[1] // LANES
                best = lax.fori_loop(
                    0, count, lambda c, best: jnp.maximum(best, scores(d_ref, first, c)), best
                )
                first += count
            top = jnp.max(best, axis=1, keepdims=True)
            acc = jnp.zeros((LANES, LANES), F32)
            first = 0
            for d_ref in d_refs:
                count = d_ref.shape[1] // LANES
                acc = lax.fori_loop(
                    0, count, lambda c, acc: acc + jnp.exp2(scores(d_ref, first, c) - top), acc
                )
                first += count
            log_sum = jnp.log2(jnp.sum(acc, axis=1, keepdims=True)) + top
            lrow_ref[pl.ds(q, 1), :] = lane_fold(jnp.broadcast_to(log_sum, (LANES, LANES)), jnp.max)
            return carry

        lax.fori_loop(0, nq, row_block, 0)
        first = 0
        for d_ref in d_refs:
            count = d_ref.shape[1] // LANES

            def column(c, carry):
                at = pl.ds(pl.multiple_of(c * LANES, LANES), LANES)

                def block(r):
                    part = pl.ds(pl.multiple_of(r * ROWS, ROWS), ROWS)
                    return d_ref[part, at] + vs_ref[part, :]

                top = lax.fori_loop(
                    0,
                    rows // ROWS,
                    lambda r, best: jnp.maximum(best, jnp.max(block(r), axis=0, keepdims=True)),
                    jnp.full((1, LANES), -3.0e38, F32),
                )
                total = lax.fori_loop(
                    0,
                    rows // ROWS,
                    lambda r, acc: acc + jnp.sum(jnp.exp2(block(r) - top), axis=0, keepdims=True),
                    jnp.zeros((1, LANES), F32),
                )
                lcol_ref[pl.ds(first + c, 1), :] = top + jnp.log2(total)
                return carry

            lax.fori_loop(0, count, column, 0)
            first += count


def entry_kernel(gen_hbm, ref_hbm, gweight_hbm, rweight_hbm, own_ref, gen_ref, tile_ref, gweight_ref, rweight_ref, sem):
    count = own_ref.shape[0]
    at = pl.ds(pl.multiple_of(lax.axis_index("ref") * count, count), count)
    pairs = (
        (gen_hbm.at[at, :], own_ref),
        (gweight_hbm, gweight_ref),
        (rweight_hbm, rweight_ref),
        (gen_hbm, gen_ref),
        (ref_hbm.at[: tile_ref.shape[0], :], tile_ref),
    )
    copies = [pltpu.make_async_copy(src, dst, sem.at[k]) for k, (src, dst) in enumerate(pairs)]
    for copy in copies:
        copy.start()
    for copy in copies:
        copy.wait()


def entry(gen, ref, gweight, rweight):
    vmem = pl.BlockSpec(memory_space=pltpu.VMEM)
    hbm = pl.BlockSpec(memory_space=pltpu.HBM)
    width = gen.shape[1]
    return pl.pallas_call(
        entry_kernel,
        in_specs=[hbm] * 4,
        out_shape=(
            pltpu.VMEM((LANES, width), gen.dtype),
            pltpu.VMEM(gen.shape, gen.dtype),
            pltpu.VMEM((TILE, width), ref.dtype),
            pltpu.VMEM(gweight.shape, F32),
            pltpu.VMEM(rweight.shape, F32),
        ),
        out_specs=(vmem,) * 5,
        scratch_shapes=[pltpu.SemaphoreType.DMA((5,))],
        compiler_params=pltpu.CompilerParams(vmem_limit_bytes=4 << 20),
        name="entry",
    )(*[hbm_array(x) for x in (gen, ref, gweight, rweight)])


def total(x):
    return jnp.sum(jnp.sum(x, axis=0, keepdims=True), axis=1, keepdims=True)


def first_kernel(first_tile, steps, *refs):
    leading = first_tile == 0
    if leading:
        gen_ref, first_ref, gweight_ref, rweight_ref, ref_hbm, *refs = refs
        d_ref, hcol_ref, hrow_ref, mass_ref, ahead_ref, vs_ref, rowacc_ref, u_ref, colsum_ref, peak_ref, *refs = refs
        tile_ref, stage_ref, v_ref, sem = refs
    else:
        gen_ref, first_ref, rweight_ref, hrow_ref, ref_hbm, before_ref, *refs = refs
        hcol0_ref, vs_ref, rowacc0_ref, u0_ref, colsum0_ref, peak_ref, *refs = refs
        d_ref, lrow_ref, lcol_ref, hcol_ref, tile_ref, stage_ref, v_ref, rowacc_ref, u_ref, colsum_ref, sem = refs
    rows, width = gen_ref.shape
    nq = rows // LANES
    chunks = TILE // LANES
    half_scale = 0.5 * LOG2E / (EPS * width)
    dot_scale = LOG2E / (EPS * width)

    def load(j):
        at = pl.ds(pl.multiple_of((first_tile + j) * TILE, TILE), TILE)
        return pltpu.make_async_copy(ref_hbm.at[at, :], tile_ref.at[j], sem.at[j])

    def product(j, tile, out_ref, columns):
        for c, half in enumerate(norms(tile, 0, chunks, half_scale)):
            row = pl.ds((first_tile + j) * chunks + c, 1)
            hcol_ref[row, :] = half
            u_ref[row, :] = jnp.log2(rweight_ref[row, :]) - half
        dots = lax.dot_general(gen_ref[...], tile[...], (((1,), (1,)), ((), ())), preferred_element_type=F32)
        out_ref[:, columns] = dots * dot_scale

    def sums(j, straight, src_ref, base, keep):
        mine = [u_ref[pl.ds(j * chunks + c, 1), :] for c in range(chunks)]
        for c, part in enumerate(sweep(src_ref, base, chunks, mine, vs_ref, rowacc_ref, straight, keep)):
            colsum_ref[pl.ds(j * chunks + c, 1), :] = part

    whole = slice(0, TILE)
    load(1).start()
    if leading:
        ahead = pltpu.make_async_copy(ref_hbm.at[steps * TILE : (steps + 1) * TILE, :], ahead_ref, sem.at[steps])
        for q, part in enumerate(norms(gen_ref, 0, nq, half_scale)):
            hrow_ref[q : q + 1, :] = part
            v_ref[q : q + 1, :] = jnp.log2(gweight_ref[q : q + 1, :]) - part
            hrow_ref[nq + q : nq + q + 1, :] = gweight_ref[q : q + 1, :]
        mass_ref[...] = jnp.broadcast_to(total(gweight_ref[...]), (8, LANES))
        product(0, first_ref, stage_ref, whole)
        start_peak(stage_ref, u_ref[0:1, :], v_ref, vs_ref, peak_ref, rowacc_ref)
    else:
        v_ref[...] = jnp.log2(hrow_ref[nq : 2 * nq, :]) - hrow_ref[0:nq, :]
        lrow_ref[nq : 2 * nq, :] = jnp.broadcast_to(total(rweight_ref[...]), (nq, LANES))
        done = first_tile * chunks
        hcol_ref[0:done, :] = hcol0_ref[...]
        rowacc_ref[...] = rowacc0_ref[...]
        u_ref[0:done, :] = u0_ref[...]
        colsum_ref[0:done, :] = colsum0_ref[...]
        sums(first_tile - 1, True, before_ref, (first_tile - 1) * TILE, None)
        product(0, first_ref, stage_ref, whole)

    def step(j, carry):
        load(j).wait()

        @pl.when(j + 1 < steps)
        def _():
            load(j + 1).start()

        sums(first_tile + j - 1, True, stage_ref, 0, (d_ref, (j - 1) * TILE))
        product(j, tile_ref.at[j], stage_ref, whole)
        return carry

    if leading:
        lax.fori_loop(1, steps - 1, step, 0)
        load(steps - 1).wait()
        ahead.start()
        sums(steps - 2, True, stage_ref, 0, (d_ref, (steps - 2) * TILE))
        product(steps - 1, tile_ref.at[steps - 1], d_ref, slice((steps - 1) * TILE, steps * TILE))
        colsum_ref[(steps - 1) * chunks : steps * chunks, :] = jnp.zeros((chunks, LANES), F32)
        ahead.wait()
    else:
        lax.fori_loop(1, steps, step, 0)
        sums(first_tile + steps - 1, False, stage_ref, 0, (d_ref, (steps - 1) * TILE))
        finish([before_ref, d_ref], u_ref, v_ref, vs_ref, rowacc_ref, colsum_ref, peak_ref, lrow_ref, lcol_ref)


def first_pass(gen, first, ref, *more):
    rows, width = gen.shape
    nq, tiles = rows // LANES, ref.shape[0] // TILE
    leading = len(more) == 2
    first_tile, steps = (0, LEAD) if leading else (LEAD, tiles - LEAD)
    cols = steps * TILE
    nc, all_nc = cols // LANES, ref.shape[0] // LANES
    vmem = pl.BlockSpec(memory_space=pltpu.VMEM)
    hbm = pl.BlockSpec(memory_space=pltpu.HBM)
    vec = lambda n: jax.ShapeDtypeStruct((n, LANES), F32)
    lanes = pltpu.VMEM((rows, LANES), F32)
    scratch = [
        pltpu.VMEM((steps, TILE, width), jnp.bfloat16),
        pltpu.VMEM((rows, TILE), F32),
        pltpu.VMEM((nq, LANES), F32),
    ]
    if leading:
        gweight, rweight = more
        operands = [vmem_array(gen), vmem_array(first), gweight, rweight, hbm_array(ref)]
        outs = (
            pltpu.VMEM((rows, cols), F32), vec(nc), vec(2 * nq), vec(8), pltpu.VMEM((TILE, width), ref.dtype),
            lanes, lanes, vec(nc), vec(nc), vec(8),
        )
        specs = [vmem] * 4 + [hbm]
    else:
        rweight, hrow, before, hcol, vs, rowacc, u, colsum, peak = more
        operands = [vmem_array(gen), vmem_array(first), rweight, hrow, hbm_array(ref), vmem_array(before)]
        operands += [hcol, vmem_array(vs), vmem_array(rowacc), u, colsum, peak]
        outs = (pltpu.VMEM((rows, cols), F32), vec(2 * nq), vec(all_nc), vec(all_nc))
        specs = [vmem] * 4 + [hbm] + [vmem] * 7
        scratch += [
            pltpu.VMEM((rows, LANES), F32),
            pltpu.VMEM((all_nc, LANES), F32),
            pltpu.VMEM((all_nc, LANES), F32),
        ]
    return pl.pallas_call(
        functools.partial(first_kernel, first_tile, steps),
        in_specs=specs,
        out_shape=outs,
        out_specs=(vmem,) * len(outs),
        scratch_shapes=scratch + [pltpu.SemaphoreType.DMA((steps + 1,))],
        compiler_params=pltpu.CompilerParams(vmem_limit_bytes=20 << 20),
        name="cross_first_0" if leading else "cross_first_1",
    )(*operands)


def next_kernel(count, *refs):
    sources = refs[:count]
    u_ref, v_ref, lrow_ref, lcol_ref, vs_ref, rowacc_ref, colsum_ref, peak_ref = refs[count:]
    chunks = TILE // LANES
    start_peak(sources[0], u_ref[0:1, :], v_ref, vs_ref, peak_ref, rowacc_ref)
    first = 0
    for d_ref in sources:
        steps = d_ref.shape[1] // TILE

        def step(j, carry):
            u = [u_ref[pl.ds(first + j * chunks + c, 1), :] for c in range(chunks)]
            base = pl.multiple_of(j * TILE, TILE)
            for c, part in enumerate(sweep(d_ref, base, chunks, u, vs_ref, rowacc_ref)):
                colsum_ref[pl.ds(first + j * chunks + c, 1), :] = part
            return carry

        lax.fori_loop(0, steps, step, 0)
        first += steps * chunks
    finish(sources, u_ref, v_ref, vs_ref, rowacc_ref, colsum_ref, peak_ref, lrow_ref, lcol_ref)


def next_pass(parts, u, v):
    rows = parts[0].shape[0]
    cols = sum(part.shape[1] for part in parts)
    nq, nc = rows // LANES, cols // LANES
    vmem = pl.BlockSpec(memory_space=pltpu.VMEM)
    return pl.pallas_call(
        functools.partial(next_kernel, len(parts)),
        in_specs=[vmem] * (len(parts) + 2),
        out_shape=(jax.ShapeDtypeStruct((nq, LANES), F32), jax.ShapeDtypeStruct((nc, LANES), F32)),
        out_specs=(vmem, vmem),
        scratch_shapes=[
            pltpu.VMEM((rows, LANES), F32),
            pltpu.VMEM((rows, LANES), F32),
            pltpu.VMEM((nc, LANES), F32),
            pltpu.VMEM((8, LANES), F32),
        ],
        compiler_params=pltpu.CompilerParams(vmem_limit_bytes=8 << 20),
    )(*[vmem_array(part) for part in parts], u, v)


def self_first_kernel(count, first, *refs):
    own_ref, mate_ref = refs[:2]
    sources = refs[2 : 2 + count]
    rest = refs[2 + count :]
    half, width = own_ref.shape
    nq = half // LANES
    if first == 0:
        mine_ref, theirs_ref, place_ref, e_ref, z_ref, hs_ref, ws_ref = rest
        for at, vec_ref in ((0, mine_ref), (nq, theirs_ref)):
            spread(vec_ref, hs_ref, nq, 0, at)
            spread(vec_ref, ws_ref, nq, nq, at)
    else:
        hs_ref, ws_ref, place_ref, e_ref, z_ref = rest
    wide = 256
    chunks = wide // LANES
    half_scale = 0.5 * LOG2E / (EPS * width)
    dot_scale = LOG2E / (EPS * width)
    z_ref[...] = jnp.zeros_like(z_ref)
    tiles = [(src, k) for src in sources for k in range(src.shape[0] // wide)]
    piece_half = {}

    def product(t):
        src, k = tiles[t]
        view = src.at[k * wide : (k + 1) * wide, :]
        piece_half[t] = norms(view, 0, chunks, half_scale)
        for h, rows_ref in enumerate((own_ref, mate_ref)):
            e_ref[h * half : (h + 1) * half, t * wide : (t + 1) * wide] = lax.dot_general(
                rows_ref[...], view[...], (((1,), (1,)), ((), ())), preferred_element_type=F32
            )

    def sums(t, straight):
        def body(r, acc):
            at = row_block(r)
            hs = hs_ref[at, :]
            ws = ws_ref[at, :]
            out = []
            for c in range(chunks):
                part = slice(t * wide + c * LANES, t * wide + (c + 1) * LANES)
                e = jnp.exp2(e_ref[at, part] * dot_scale - (hs + piece_half[t][c]))
                e_ref[at, part] = e
                out.append(acc[c] + jnp.sum((e * ws).reshape(ROWS // 8, 8, LANES), axis=0))
            return tuple(out)

        acc = (jnp.zeros((8, LANES), F32),) * chunks
        if straight:
            for r in range(2 * half // ROWS):
                acc = body(r, acc)
        else:
            acc = lax.fori_loop(0, 2 * half // ROWS, body, acc, unroll=2)
        for c in range(chunks):
            z_ref[pl.ds(place_ref[first + t * chunks + c], 1), :] = jnp.sum(acc[c], axis=0, keepdims=True)

    product(0)
    for t in range(1, len(tiles)):
        sums(t - 1, True)
        product(t)
    sums(len(tiles) - 1, False)


def self_first(own, mate, sources, left, right, place, first):
    rows = 2 * own.shape[0]
    cols = sum(src.shape[0] for src in sources)
    vmem = pl.BlockSpec(memory_space=pltpu.VMEM)
    lanes = () if first else (pltpu.VMEM((rows, LANES), F32),) * 2
    if first:
        left, right = vmem_array(left), vmem_array(right)
    return pl.pallas_call(
        functools.partial(self_first_kernel, len(sources), first),
        in_specs=[vmem] * (4 + len(sources)) + [pl.BlockSpec(memory_space=pltpu.SMEM)],
        out_shape=(pltpu.VMEM((rows, cols), F32), jax.ShapeDtypeStruct((place.shape[0], LANES), F32)) + lanes,
        out_specs=(vmem,) * (2 + len(lanes)),
        compiler_params=pltpu.CompilerParams(vmem_limit_bytes=8 << 20),
    )(vmem_array(own), vmem_array(mate), *[vmem_array(src) for src in sources], left, right, place)


def self_cols_kernel(count, *refs):
    w_ref, place_ref, z_ref, ws_ref = refs[count:]
    rows = refs[0].shape[0]
    chunks = 256 // LANES
    spread(w_ref, ws_ref, rows // LANES)
    zero = jnp.zeros((8, LANES), F32)
    first = 0
    for e_ref in refs[:count]:
        steps = e_ref.shape[1] // 256

        def tile(t, carry):
            base = pl.multiple_of(t * 256, 256)

            def body(r, acc):
                at = pl.ds(pl.multiple_of(r * ROWS, ROWS), ROWS)
                ws = ws_ref[at, :]
                out = []
                for c in range(chunks):
                    e = e_ref[at, pl.ds(base + c * LANES, LANES)] * ws
                    out.append(acc[c] + jnp.sum(e.reshape(ROWS // 8, 8, LANES), axis=0))
                return tuple(out)

            acc = lax.fori_loop(0, rows // ROWS, body, (zero,) * chunks, unroll=4)
            for c in range(chunks):
                z_ref[pl.ds(place_ref[first + t * chunks + c], 1), :] = jnp.sum(acc[c], axis=0, keepdims=True)
            return carry

        lax.fori_loop(0, steps, tile, 0)
        first += steps * chunks


def self_rows_kernel(count, *refs):
    w_ref, place_ref, y_ref, rowacc_ref = refs[count:]
    rows = refs[0].shape[0]
    chunks = 512 // LANES
    rowacc_ref[...] = jnp.zeros_like(rowacc_ref)
    first = 0
    for e_ref in refs[:count]:
        steps = e_ref.shape[1] // 512

        def tile(t, carry):
            base = pl.multiple_of(t * 512, 512)
            w = [w_ref[pl.ds(place_ref[first + t * chunks + c], 1), :] for c in range(chunks)]

            def body(r, carry):
                at = pl.ds(pl.multiple_of(r * ROWS, ROWS), ROWS)
                acc = rowacc_ref[at, :]
                for c in range(chunks):
                    acc = acc + e_ref[at, pl.ds(base + c * LANES, LANES)] * w[c]
                rowacc_ref[at, :] = acc
                return carry

            return lax.fori_loop(0, rows // ROWS, body, carry, unroll=4)

        lax.fori_loop(0, steps, tile, 0)
        first += steps * chunks
    for q in range(rows // LANES):
        y_ref[q : q + 1, :] = lane_fold(rowacc_ref[q * LANES : (q + 1) * LANES, :], jnp.sum)


def self_apply(kernel, parts, w, place, out_rows):
    rows = parts[0].shape[0]
    vmem = pl.BlockSpec(memory_space=pltpu.VMEM)
    return pl.pallas_call(
        functools.partial(kernel, len(parts)),
        in_specs=[vmem] * (len(parts) + 1) + [pl.BlockSpec(memory_space=pltpu.SMEM)],
        out_shape=jax.ShapeDtypeStruct((out_rows, LANES), F32),
        out_specs=vmem,
        scratch_shapes=[pltpu.VMEM((rows, LANES), F32)],
        compiler_params=pltpu.CompilerParams(vmem_limit_bytes=8 << 20),
    )(*[vmem_array(part) for part in parts], w, place)


def log_add(parts):
    top = functools.reduce(jnp.maximum, parts)
    return top + jnp.log2(sum(jnp.exp2(part - top) for part in parts))


def build(n_z, n_y, n_core, n_ref):
    n_zy = n_z * n_y
    n_gen = n_zy * n_core
    assert n_z == n_y == n_ref == 4 and n_core == 2

    def place_of(g):
        return g // (n_y * n_core), (g // n_core) % n_y, g % n_core

    def gen_perm(move):
        out = []
        for g in range(n_gen):
            z, y, c = move(*place_of(g))
            out.append((g, ((z % n_z) * n_y + y % n_y) * n_core + c % n_core))
        return out

    core_stage = [gen_perm(lambda z, y, c: (z, y, c + 1))]
    y_stage = [gen_perm(lambda z, y, c: (z, y + k, c)) for k in (2, 1, 3)]
    z_stage = [gen_perm(lambda z, y, c: (z + k, y, c)) for k in (2, 1, 3)]
    ref_stage = [[(i, (i + k) % n_ref) for i in range(n_ref)] for k in (2, 1, 3)]
    first_axis = {k: gen_perm(lambda z, y, c: (z, y + k, c) if c == 0 else (z + k, y, c)) for k in (1, 2, 3)}
    second_axis = {k: gen_perm(lambda z, y, c: (z + k, y, c) if c == 0 else (z, y + k, c)) for k in (1, 3)}
    order = [(0, 0), (0, 1), (0, 2), (0, 3)]
    order += [(1, 0), (1, 1), (1, 2), (1, 3), (3, 0), (3, 1), (3, 2), (3, 3)]
    order += [(2, 0), (2, 1), (2, 2), (2, 3)]

    def shift(value, axis, perms):
        return [lax.ppermute(value, axis, perm) for perm in perms]

    def merge(parts, logs):
        top = log_add([part[:logs] for part in parts])
        if parts[0].shape[0] == logs:
            return top
        return jnp.concatenate([top, sum(part[logs:] for part in parts)], axis=0)

    def stage(value, axis, perms, logs):
        return merge([value] + shift(value, axis, perms), logs)

    def doubled(value, logs):
        for flip in (1, n_ref - 1):
            value = merge([value, lax.ppermute(value, "ref", [(i, i ^ flip) for i in range(n_ref)])], logs)
        return value

    def run(gen_features, gen_weight, ref_features, ref_weight, ref_self):
        gen_count = gen_features.shape[0]
        ref_count = ref_features.shape[0]
        nq, nc = gen_count // LANES, ref_count // LANES
        g = lax.axis_index("gen")
        x = lax.axis_index("ref")
        z, y, core = place_of(g)
        zy = z * n_y + y
        b, a = (lax.broadcasted_iota(jnp.int32, (len(order),), 0) for _ in range(2))
        b = functools.reduce(lambda v, k: jnp.where(a == k, order[k][0], v), range(len(order)), b)
        a = a % 4
        mine = ((z - b + n_z) % n_z) * n_y + (y - a + n_y) % n_y
        other = ((z - a + n_z) % n_z) * n_y + (y - b + n_y) % n_y
        place = jnp.where(core == 0, mine, other)
        at_zy = (lax.broadcasted_iota(jnp.int32, (n_zy, LANES), 0) == zy).astype(F32)
        at_x = (lax.broadcasted_iota(jnp.int32, (n_ref, LANES), 0) == x).astype(F32)
        wg = gen_weight.reshape(nq, LANES)
        wg, place, at_zy, at_x = lax.optimization_barrier((wg, place, at_zy, at_x))
        own, held, tile0, wg, wr = entry(
            gen_features, ref_features, wg, ref_weight.reshape(nc, LANES)
        )

        def to_cols(rows):
            picked = jnp.sum(jnp.where(at_x > 0, rows, 0.0), axis=0, keepdims=True)
            return jnp.where(at_zy > 0, picked, 0.0)

        def to_rows(cols):
            picked = jnp.sum(jnp.where(at_zy > 0, cols, 0.0), axis=0, keepdims=True)
            return jnp.where(at_x > 0, picked, 0.0)

        got = {}
        for k in (1, 3, 2):
            got[k] = lax.ppermute(own, "gen", first_axis[k])
        mate = lax.ppermute(held, "gen", core_stage[0])
        near = jnp.concatenate([own, got[1], got[2], got[3]], axis=0)
        up = lax.ppermute(near, "gen", second_axis[1])
        down = lax.ppermute(near, "gen", second_axis[3])
        low_far = lax.ppermute(up[: 2 * LANES], "gen", second_axis[1])
        high_far = lax.ppermute(down[2 * LANES :], "gen", second_axis[3])

        d0, hcol, mine, gmass, ahead, *carried = first_pass(held, tile0, ref_features, wg, wr)
        theirs = lax.ppermute(mine, "gen", core_stage[0])
        d1, row_part, lcol, hcol = first_pass(held, ahead, ref_features, wr, mine, d0, hcol, *carried)
        hrow = mine[:nq]
        weight = jnp.concatenate([wg, theirs[nq:]], axis=0)
        e0, z1_0, hs, ws = self_first(held, mate, [near], mine, theirs, place, 0)
        e1, z1_1 = self_first(held, mate, [up, down], hs, ws, place, 4)
        e2, z1_2 = self_first(held, mate, [low_far, high_far], hs, ws, place, 12)
        e = [e0, e1, e2]

        row_part = doubled(row_part, nq)
        col_part = jnp.concatenate([lcol, gmass], axis=0)
        col_part = stage(col_part, "gen", core_stage, nc)
        col_part = jnp.concatenate([col_part, to_cols(wg)], axis=0)
        col_part = stage(col_part, "gen", y_stage, nc)
        col_part = stage(col_part, "gen", z_stage, nc)
        gmass = col_part[nc : nc + 1]
        rmass = row_part[nq : nq + 1]
        wcols = col_part[nc + 8 :] / gmass
        gmass_log = jnp.log2(gmass)
        rmass_log = jnp.log2(rmass)
        f = hrow - (row_part[:nq] - rmass_log)
        c = hcol - (col_part[:nc] - gmass_log)
        ubase = jnp.log2(wr) - rmass_log - hcol
        vbase = jnp.log2(wg) - gmass_log - hrow
        share = wg / gmass

        lrow, lcol = next_pass([d0, d1], ubase + c, vbase + f)
        lrow = doubled(lrow, nq)
        lcol = stage(lcol, "gen", core_stage, nc)
        col_part = jnp.concatenate([lcol, z1_0 + z1_1 + z1_2], axis=0)
        col_part = stage(col_part, "gen", y_stage, nc)
        col_part = stage(col_part, "gen", z_stage, nc)
        f = 0.5 * (f + (hrow - lrow))
        c = 0.5 * (c + (hcol - col_part[:nc]))
        y1 = col_part[nc:] / gmass

        lrow, lcol = next_pass([d0, d1], ubase + c, vbase + f)
        y2 = self_apply(self_rows_kernel, e, wcols / y1, place, 2 * nq)
        row_part = jnp.concatenate([lrow, y2, to_rows(-jnp.log2(y1))], axis=0)
        row_part = stage(row_part, "ref", ref_stage, nq)
        f = 0.5 * (f + (hrow - row_part[:nq]))
        f_part = share * f
        f_part = jnp.concatenate([f_part, f_part], axis=0)
        mine = jnp.concatenate([lcol, f_part, row_part[nq:]], axis=0)
        theirs = shift(mine, "gen", core_stage)[0]
        lcol = log_add([lcol, theirs[:nc]])
        f_part = f_part + theirs[nc : nc + 8]
        y2, y2_mate, s1 = row_part[nq : 2 * nq], row_part[2 * nq : 3 * nq], row_part[3 * nq :]
        at = nc + 8
        y2 = y2 + theirs[at + nq : at + 2 * nq]
        y2_mate = y2_mate + theirs[at : at + nq]
        s1 = jnp.concatenate([s1, theirs[at + 2 * nq :]], axis=0)
        s2 = 0.5 * (s1 - jnp.log2(jnp.concatenate([y2, y2_mate], axis=0)))
        w3 = weight / gmass * jnp.exp2(s2)
        z3 = self_apply(self_cols_kernel, e, w3, place, n_zy)
        col_part = jnp.concatenate([lcol, f_part, z3, to_cols(s2[:nq])], axis=0)
        col_part = stage(col_part, "gen", y_stage, nc)
        col_part = stage(col_part, "gen", z_stage, nc)
        c = 0.5 * (c + (hcol - col_part[:nc]))
        f_part = col_part[nc : nc + nq]
        z3, s2 = col_part[nc + 8 : nc + 8 + n_zy], col_part[nc + 8 + n_zy :]

        unit = EPS / LOG2E
        ref_gap = c * unit - ref_self.reshape(nc, LANES)
        s3 = 0.5 * (s2 - jnp.log2(z3))
        s_part = jnp.sum((wcols * s3).reshape(2, 8, LANES), axis=0)
        s_part = s_part + shift(s_part, "gen", core_stage)[0]
        part = jnp.sum(((wr / rmass) * ref_gap).reshape(nc // 8, 8, LANES), axis=0) - unit * s_part
        row_part = jnp.concatenate([to_rows(s3), part], axis=0)
        row_part = row_part + sum(shift(row_part, "ref", ref_stage))
        gen_gap = (f - row_part[:nq]) * unit
        divergence = jnp.sum(unit * f_part + row_part[nq : 2 * nq] + row_part[2 * nq :])
        return gen_gap.reshape(gen_count), ref_gap.reshape(ref_count), divergence

    return run


def solution(mesh):
    n_gen, n_ref = mesh.shape["gen"], mesh.shape["ref"]
    n_core = 2
    n_y = 1
    while n_y * n_y * n_core < n_gen:
        n_y *= 2
    placed = (P("gen", None), P("gen"), P("ref", None), P("ref"), P("ref"))
    return jax.shard_map(
        build(n_gen // (n_y * n_core), n_y, n_core, n_ref),
        mesh=mesh,
        in_specs=placed,
        out_specs=(P("gen"), P("ref"), P()),
        check_vma=False,
    )
```

```python
import functools

import jax
import jax.numpy as jnp
from jax import lax
from jax.experimental import pallas as pl
from jax.experimental.pallas import tpu as pltpu
from jax.sharding import PartitionSpec as P


EPS = 0.1
LOG2E = 1.4426950408889634
F32 = jnp.float32
LANES = 128
TILE = 512
ROWS = 32
LEAD = 6
LOW = 2.0**-80
HIGH = 2.0**120


def vmem_array(x):
    return pltpu.with_memory_space_constraint(x, pltpu.VMEM)


def hbm_array(x):
    return pltpu.with_memory_space_constraint(x, pltpu.HBM)


def spread(vec_ref, out_ref, count, first=0, at=0):
    for q in range(count):
        block = jnp.broadcast_to(vec_ref[first + q : first + q + 1, :], (LANES, LANES))
        out_ref[(at + q) * LANES : (at + q + 1) * LANES, :] = block.T


def lane_fold(acc, op):
    return op(acc.T, axis=0, keepdims=True)


def norms(feat_ref, start, count, scale):
    width = feat_ref.shape[1]
    out = []
    for q in range(count):
        acc = jnp.zeros((LANES, LANES), F32)
        for c in range(width // LANES):
            x = feat_ref[start + q * LANES : start + (q + 1) * LANES, c * LANES : (c + 1) * LANES].astype(F32)
            acc = acc + x * x
        out.append(lane_fold(acc, jnp.sum) * scale)
    return out


def row_block(r):
    if isinstance(r, int):
        return slice(r * ROWS, (r + 1) * ROWS)
    return pl.ds(pl.multiple_of(r * ROWS, ROWS), ROWS)


def sweep(d_ref, base, chunks, u, vs_ref, rowacc_ref, straight=False, keep=None):
    rows = d_ref.shape[0]
    u = [jnp.broadcast_to(part, (8, LANES))[None] for part in u]

    def body(r, cols):
        at = row_block(r)
        vs = vs_ref[at, :].reshape(ROWS // 8, 8, LANES)
        racc = rowacc_ref[at, :].reshape(ROWS // 8, 8, LANES)
        out = []
        for c in range(chunks):
            d = d_ref[at, pl.ds(base + c * LANES, LANES)]
            if keep is not None:
                keep[0][at, pl.ds(pl.multiple_of(keep[1] + c * LANES, LANES), LANES)] = d
            p = jnp.exp2((d.reshape(ROWS // 8, 8, LANES) + u[c]) + vs)
            racc = racc + p
            out.append(cols[c] + jnp.sum(p, axis=0))
        rowacc_ref[at, :] = racc.reshape(ROWS, LANES)
        return tuple(out)

    cols = (jnp.zeros((8, LANES), F32),) * chunks
    if straight:
        for r in range(rows // ROWS):
            cols = body(r, cols)
    else:
        cols = lax.fori_loop(0, rows // ROWS, body, cols, unroll=4)
    return [jnp.sum(c, axis=0, keepdims=True) for c in cols]


def tile_peak(d_ref, u, vs_ref):
    rows = d_ref.shape[0]
    best = jnp.full((8, LANES), -3.0e38, F32)

    def body(r, best):
        at = pl.ds(pl.multiple_of(r * ROWS, ROWS), ROWS)
        val = (d_ref[at, 0:LANES] + u) + vs_ref[at, :]
        return jnp.maximum(best, jnp.max(val.reshape(ROWS // 8, 8, LANES), axis=0))

    best = lax.fori_loop(0, rows // ROWS, body, best, unroll=2)
    return jnp.max(jnp.max(best, axis=0, keepdims=True), axis=1, keepdims=True)


def start_peak(d_ref, u0, v_ref, vs_ref, peak_ref, rowacc_ref):
    rows = d_ref.shape[0]
    spread(v_ref, vs_ref, rows // LANES)
    peak = jnp.broadcast_to(tile_peak(d_ref, u0, vs_ref), (8, LANES))
    peak_ref[...] = peak
    vs_ref[...] = vs_ref[...] - peak[0:1, :]
    rowacc_ref[...] = jnp.zeros_like(rowacc_ref)


def finish(d_refs, u_ref, v_ref, vs_ref, rowacc_ref, colsum_ref, peak_ref, lrow_ref, lcol_ref):
    rows = d_refs[0].shape[0]
    nq = rows // LANES
    rowsum = [lane_fold(rowacc_ref[q * LANES : (q + 1) * LANES, :], jnp.sum) for q in range(nq)]
    rowsum = jnp.concatenate(rowsum, axis=0)
    colsum = colsum_ref[...]
    low = jnp.minimum(jnp.min(rowsum), jnp.min(colsum))
    high = jnp.maximum(jnp.max(rowsum), jnp.max(colsum))
    good = jnp.logical_and(low >= LOW, high <= HIGH)
    peak = peak_ref[0:1, :]

    @pl.when(good)
    def _():
        lrow_ref[0:nq, :] = (jnp.log2(rowsum) + peak) - v_ref[...]
        lcol_ref[...] = (jnp.log2(colsum) + peak) - u_ref[...]

    @pl.when(jnp.logical_not(good))
    def _():
        spread(v_ref, vs_ref, nq)

        def row_block(q, carry):
            part = pl.ds(pl.multiple_of(q * LANES, LANES), LANES)

            def scores(d_ref, first, c):
                at = pl.ds(pl.multiple_of(c * LANES, LANES), LANES)
                return d_ref[part, at] + u_ref[pl.ds(first + c, 1), :]

            best = jnp.full((LANES, LANES), -3.0e38, F32)
            first = 0
            for d_ref in d_refs:
                count = d_ref.shape[1] // LANES
                best = lax.fori_loop(
                    0, count, lambda c, best: jnp.maximum(best, scores(d_ref, first, c)), best
                )
                first += count
            top = jnp.max(best, axis=1, keepdims=True)
            acc = jnp.zeros((LANES, LANES), F32)
            first = 0
            for d_ref in d_refs:
                count = d_ref.shape[1] // LANES
                acc = lax.fori_loop(
                    0, count, lambda c, acc: acc + jnp.exp2(scores(d_ref, first, c) - top), acc
                )
                first += count
            log_sum = jnp.log2(jnp.sum(acc, axis=1, keepdims=True)) + top
            lrow_ref[pl.ds(q, 1), :] = lane_fold(jnp.broadcast_to(log_sum, (LANES, LANES)), jnp.max)
            return carry

        lax.fori_loop(0, nq, row_block, 0)
        first = 0
        for d_ref in d_refs:
            count = d_ref.shape[1] // LANES

            def column(c, carry):
                at = pl.ds(pl.multiple_of(c * LANES, LANES), LANES)

                def block(r):
                    part = pl.ds(pl.multiple_of(r * ROWS, ROWS), ROWS)
                    return d_ref[part, at] + vs_ref[part, :]

                top = lax.fori_loop(
                    0,
                    rows // ROWS,
                    lambda r, best: jnp.maximum(best, jnp.max(block(r), axis=0, keepdims=True)),
                    jnp.full((1, LANES), -3.0e38, F32),
                )
                total = lax.fori_loop(
                    0,
                    rows // ROWS,
                    lambda r, acc: acc + jnp.sum(jnp.exp2(block(r) - top), axis=0, keepdims=True),
                    jnp.zeros((1, LANES), F32),
                )
                lcol_ref[pl.ds(first + c, 1), :] = top + jnp.log2(total)
                return carry

            lax.fori_loop(0, count, column, 0)
            first += count


def entry_kernel(gen_hbm, ref_hbm, gweight_hbm, rweight_hbm, own_ref, gen_ref, tile_ref, gweight_ref, rweight_ref, sem):
    count = own_ref.shape[0]
    at = pl.ds(pl.multiple_of(lax.axis_index("ref") * count, count), count)
    pairs = (
        (gen_hbm.at[at, :], own_ref),
        (gweight_hbm, gweight_ref),
        (rweight_hbm, rweight_ref),
        (gen_hbm, gen_ref),
        (ref_hbm.at[: tile_ref.shape[0], :], tile_ref),
    )
    copies = [pltpu.make_async_copy(src, dst, sem.at[k]) for k, (src, dst) in enumerate(pairs)]
    for copy in copies:
        copy.start()
    for copy in copies:
        copy.wait()


def entry(gen, ref, gweight, rweight):
    vmem = pl.BlockSpec(memory_space=pltpu.VMEM)
    hbm = pl.BlockSpec(memory_space=pltpu.HBM)
    width = gen.shape[1]
    return pl.pallas_call(
        entry_kernel,
        in_specs=[hbm] * 4,
        out_shape=(
            pltpu.VMEM((LANES, width), gen.dtype),
            pltpu.VMEM(gen.shape, gen.dtype),
            pltpu.VMEM((TILE, width), ref.dtype),
            pltpu.VMEM(gweight.shape, F32),
            pltpu.VMEM(rweight.shape, F32),
        ),
        out_specs=(vmem,) * 5,
        scratch_shapes=[pltpu.SemaphoreType.DMA((5,))],
        compiler_params=pltpu.CompilerParams(vmem_limit_bytes=4 << 20),
        name="entry",
    )(*[hbm_array(x) for x in (gen, ref, gweight, rweight)])


def total(x):
    return jnp.sum(jnp.sum(x, axis=0, keepdims=True), axis=1, keepdims=True)


def first_kernel(first_tile, steps, *refs):
    leading = first_tile == 0
    if leading:
        gen_ref, first_ref, gweight_ref, rweight_ref, ref_hbm, *refs = refs
        d_ref, hcol_ref, hrow_ref, mass_ref, ahead_ref, vs_ref, rowacc_ref, u_ref, colsum_ref, peak_ref, *refs = refs
        tile_ref, stage_ref, v_ref, sem = refs
    else:
        gen_ref, first_ref, rweight_ref, hrow_ref, ref_hbm, before_ref, *refs = refs
        hcol0_ref, vs_ref, rowacc0_ref, u0_ref, colsum0_ref, peak_ref, *refs = refs
        d_ref, lrow_ref, lcol_ref, hcol_ref, tile_ref, stage_ref, v_ref, rowacc_ref, u_ref, colsum_ref, sem = refs
    rows, width = gen_ref.shape
    nq = rows // LANES
    chunks = TILE // LANES
    half_scale = 0.5 * LOG2E / (EPS * width)
    dot_scale = LOG2E / (EPS * width)

    def load(j):
        at = pl.ds(pl.multiple_of((first_tile + j) * TILE, TILE), TILE)
        return pltpu.make_async_copy(ref_hbm.at[at, :], tile_ref.at[j], sem.at[j])

    def product(j, tile, out_ref, columns):
        for c, half in enumerate(norms(tile, 0, chunks, half_scale)):
            row = pl.ds((first_tile + j) * chunks + c, 1)
            hcol_ref[row, :] = half
            u_ref[row, :] = jnp.log2(rweight_ref[row, :]) - half
        dots = lax.dot_general(gen_ref[...], tile[...], (((1,), (1,)), ((), ())), preferred_element_type=F32)
        out_ref[:, columns] = dots * dot_scale

    def sums(j, straight, src_ref, base, keep):
        mine = [u_ref[pl.ds(j * chunks + c, 1), :] for c in range(chunks)]
        for c, part in enumerate(sweep(src_ref, base, chunks, mine, vs_ref, rowacc_ref, straight, keep)):
            colsum_ref[pl.ds(j * chunks + c, 1), :] = part

    whole = slice(0, TILE)
    load(1).start()
    if leading:
        ahead = pltpu.make_async_copy(ref_hbm.at[steps * TILE : (steps + 1) * TILE, :], ahead_ref, sem.at[steps])
        for q, part in enumerate(norms(gen_ref, 0, nq, half_scale)):
            hrow_ref[q : q + 1, :] = part
            v_ref[q : q + 1, :] = jnp.log2(gweight_ref[q : q + 1, :]) - part
            hrow_ref[nq + q : nq + q + 1, :] = gweight_ref[q : q + 1, :]
        mass_ref[...] = jnp.broadcast_to(total(gweight_ref[...]), (8, LANES))
        product(0, first_ref, stage_ref, whole)
        start_peak(stage_ref, u_ref[0:1, :], v_ref, vs_ref, peak_ref, rowacc_ref)
    else:
        v_ref[...] = jnp.log2(hrow_ref[nq : 2 * nq, :]) - hrow_ref[0:nq, :]
        lrow_ref[nq : 2 * nq, :] = jnp.broadcast_to(total(rweight_ref[...]), (nq, LANES))
        done = first_tile * chunks
        hcol_ref[0:done, :] = hcol0_ref[...]
        rowacc_ref[...] = rowacc0_ref[...]
        u_ref[0:done, :] = u0_ref[...]
        colsum_ref[0:done, :] = colsum0_ref[...]
        sums(first_tile - 1, True, before_ref, (first_tile - 1) * TILE, None)
        product(0, first_ref, stage_ref, whole)

    def step(j, carry):
        load(j).wait()

        @pl.when(j + 1 < steps)
        def _():
            load(j + 1).start()

        sums(first_tile + j - 1, True, stage_ref, 0, (d_ref, (j - 1) * TILE))
        product(j, tile_ref.at[j], stage_ref, whole)
        return carry

    if leading:
        lax.fori_loop(1, steps - 1, step, 0)
        load(steps - 1).wait()
        ahead.start()
        sums(steps - 2, True, stage_ref, 0, (d_ref, (steps - 2) * TILE))
        product(steps - 1, tile_ref.at[steps - 1], d_ref, slice((steps - 1) * TILE, steps * TILE))
        colsum_ref[(steps - 1) * chunks : steps * chunks, :] = jnp.zeros((chunks, LANES), F32)
        ahead.wait()
    else:
        lax.fori_loop(1, steps, step, 0)
        sums(first_tile + steps - 1, False, stage_ref, 0, (d_ref, (steps - 1) * TILE))
        finish([before_ref, d_ref], u_ref, v_ref, vs_ref, rowacc_ref, colsum_ref, peak_ref, lrow_ref, lcol_ref)


def first_pass(gen, first, ref, *more):
    rows, width = gen.shape
    nq, tiles = rows // LANES, ref.shape[0] // TILE
    leading = len(more) == 2
    first_tile, steps = (0, LEAD) if leading else (LEAD, tiles - LEAD)
    cols = steps * TILE
    nc, all_nc = cols // LANES, ref.shape[0] // LANES
    vmem = pl.BlockSpec(memory_space=pltpu.VMEM)
    hbm = pl.BlockSpec(memory_space=pltpu.HBM)
    vec = lambda n: jax.ShapeDtypeStruct((n, LANES), F32)
    lanes = pltpu.VMEM((rows, LANES), F32)
    scratch = [
        pltpu.VMEM((steps, TILE, width), jnp.bfloat16),
        pltpu.VMEM((rows, TILE), F32),
        pltpu.VMEM((nq, LANES), F32),
    ]
    if leading:
        gweight, rweight = more
        operands = [vmem_array(gen), vmem_array(first), gweight, rweight, hbm_array(ref)]
        outs = (
            pltpu.VMEM((rows, cols), F32), vec(nc), vec(2 * nq), vec(8), pltpu.VMEM((TILE, width), ref.dtype),
            lanes, lanes, vec(nc), vec(nc), vec(8),
        )
        specs = [vmem] * 4 + [hbm]
    else:
        rweight, hrow, before, hcol, vs, rowacc, u, colsum, peak = more
        operands = [vmem_array(gen), vmem_array(first), rweight, hrow, hbm_array(ref), vmem_array(before)]
        operands += [hcol, vmem_array(vs), vmem_array(rowacc), u, colsum, peak]
        outs = (pltpu.VMEM((rows, cols), F32), vec(2 * nq), vec(all_nc), vec(all_nc))
        specs = [vmem] * 4 + [hbm] + [vmem] * 7
        scratch += [
            pltpu.VMEM((rows, LANES), F32),
            pltpu.VMEM((all_nc, LANES), F32),
            pltpu.VMEM((all_nc, LANES), F32),
        ]
    return pl.pallas_call(
        functools.partial(first_kernel, first_tile, steps),
        in_specs=specs,
        out_shape=outs,
        out_specs=(vmem,) * len(outs),
        scratch_shapes=scratch + [pltpu.SemaphoreType.DMA((steps + 1,))],
        compiler_params=pltpu.CompilerParams(vmem_limit_bytes=20 << 20),
        name="cross_first_0" if leading else "cross_first_1",
    )(*operands)


def next_kernel(count, *refs):
    sources = refs[:count]
    u_ref, v_ref, lrow_ref, lcol_ref, vs_ref, rowacc_ref, colsum_ref, peak_ref = refs[count:]
    chunks = TILE // LANES
    start_peak(sources[0], u_ref[0:1, :], v_ref, vs_ref, peak_ref, rowacc_ref)
    first = 0
    for d_ref in sources:
        steps = d_ref.shape[1] // TILE

        def step(j, carry):
            u = [u_ref[pl.ds(first + j * chunks + c, 1), :] for c in range(chunks)]
            base = pl.multiple_of(j * TILE, TILE)
            for c, part in enumerate(sweep(d_ref, base, chunks, u, vs_ref, rowacc_ref)):
                colsum_ref[pl.ds(first + j * chunks + c, 1), :] = part
            return carry

        lax.fori_loop(0, steps, step, 0)
        first += steps * chunks
    finish(sources, u_ref, v_ref, vs_ref, rowacc_ref, colsum_ref, peak_ref, lrow_ref, lcol_ref)


def next_pass(parts, u, v):
    rows = parts[0].shape[0]
    cols = sum(part.shape[1] for part in parts)
    nq, nc = rows // LANES, cols // LANES
    vmem = pl.BlockSpec(memory_space=pltpu.VMEM)
    return pl.pallas_call(
        functools.partial(next_kernel, len(parts)),
        in_specs=[vmem] * (len(parts) + 2),
        out_shape=(jax.ShapeDtypeStruct((nq, LANES), F32), jax.ShapeDtypeStruct((nc, LANES), F32)),
        out_specs=(vmem, vmem),
        scratch_shapes=[
            pltpu.VMEM((rows, LANES), F32),
            pltpu.VMEM((rows, LANES), F32),
            pltpu.VMEM((nc, LANES), F32),
            pltpu.VMEM((8, LANES), F32),
        ],
        compiler_params=pltpu.CompilerParams(vmem_limit_bytes=8 << 20),
    )(*[vmem_array(part) for part in parts], u, v)


def self_first_kernel(count, first, *refs):
    own_ref, mate_ref = refs[:2]
    sources = refs[2 : 2 + count]
    rest = refs[2 + count :]
    half, width = own_ref.shape
    nq = half // LANES
    if first == 0:
        mine_ref, theirs_ref, place_ref, e_ref, z_ref, hs_ref, ws_ref = rest
        for at, vec_ref in ((0, mine_ref), (nq, theirs_ref)):
            spread(vec_ref, hs_ref, nq, 0, at)
            spread(vec_ref, ws_ref, nq, nq, at)
    else:
        hs_ref, ws_ref, place_ref, e_ref, z_ref = rest
    wide = 256
    chunks = wide // LANES
    half_scale = 0.5 * LOG2E / (EPS * width)
    dot_scale = LOG2E / (EPS * width)
    z_ref[...] = jnp.zeros_like(z_ref)
    tiles = [(src, k) for src in sources for k in range(src.shape[0] // wide)]
    piece_half = {}

    def product(t):
        src, k = tiles[t]
        view = src.at[k * wide : (k + 1) * wide, :]
        piece_half[t] = norms(view, 0, chunks, half_scale)
        for h, rows_ref in enumerate((own_ref, mate_ref)):
            e_ref[h * half : (h + 1) * half, t * wide : (t + 1) * wide] = lax.dot_general(
                rows_ref[...], view[...], (((1,), (1,)), ((), ())), preferred_element_type=F32
            )

    def sums(t, straight):
        def body(r, acc):
            at = row_block(r)
            hs = hs_ref[at, :]
            ws = ws_ref[at, :]
            out = []
            for c in range(chunks):
                part = slice(t * wide + c * LANES, t * wide + (c + 1) * LANES)
                e = jnp.exp2(e_ref[at, part] * dot_scale - (hs + piece_half[t][c]))
                e_ref[at, part] = e
                out.append(acc[c] + jnp.sum((e * ws).reshape(ROWS // 8, 8, LANES), axis=0))
            return tuple(out)

        acc = (jnp.zeros((8, LANES), F32),) * chunks
        if straight:
            for r in range(2 * half // ROWS):
                acc = body(r, acc)
        else:
            acc = lax.fori_loop(0, 2 * half // ROWS, body, acc, unroll=2)
        for c in range(chunks):
            z_ref[pl.ds(place_ref[first + t * chunks + c], 1), :] = jnp.sum(acc[c], axis=0, keepdims=True)

    product(0)
    for t in range(1, len(tiles)):
        sums(t - 1, True)
        product(t)
    sums(len(tiles) - 1, False)


def self_first(own, mate, sources, left, right, place, first):
    rows = 2 * own.shape[0]
    cols = sum(src.shape[0] for src in sources)
    vmem = pl.BlockSpec(memory_space=pltpu.VMEM)
    lanes = () if first else (pltpu.VMEM((rows, LANES), F32),) * 2
    if first:
        left, right = vmem_array(left), vmem_array(right)
    return pl.pallas_call(
        functools.partial(self_first_kernel, len(sources), first),
        in_specs=[vmem] * (4 + len(sources)) + [pl.BlockSpec(memory_space=pltpu.SMEM)],
        out_shape=(pltpu.VMEM((rows, cols), F32), jax.ShapeDtypeStruct((place.shape[0], LANES), F32)) + lanes,
        out_specs=(vmem,) * (2 + len(lanes)),
        compiler_params=pltpu.CompilerParams(vmem_limit_bytes=8 << 20),
    )(vmem_array(own), vmem_array(mate), *[vmem_array(src) for src in sources], left, right, place)


def self_cols_kernel(count, *refs):
    w_ref, place_ref, z_ref, ws_ref = refs[count:]
    rows = refs[0].shape[0]
    chunks = TILE // LANES
    spread(w_ref, ws_ref, rows // LANES)
    first = 0
    for e_ref in refs[:count]:
        for base in range(0, e_ref.shape[1], TILE):

            def body(r, acc):
                at = row_block(r)
                ws = ws_ref[at, :]
                out = []
                for c in range(chunks):
                    e = e_ref[at, base + c * LANES : base + (c + 1) * LANES] * ws
                    out.append(acc[c] + jnp.sum(e.reshape(ROWS // 8, 8, LANES), axis=0))
                return tuple(out)

            acc = lax.fori_loop(0, rows // ROWS, body, (jnp.zeros((8, LANES), F32),) * chunks, unroll=4)
            for c in range(chunks):
                z_ref[pl.ds(place_ref[first + c], 1), :] = jnp.sum(acc[c], axis=0, keepdims=True)
            first += chunks


def self_rows_kernel(count, *refs):
    w_ref, place_ref, y_ref, rowacc_ref = refs[count:]
    rows = refs[0].shape[0]
    first = 0
    for at_e, e_ref in enumerate(refs[:count]):
        chunks = e_ref.shape[1] // LANES
        w = [
            jnp.broadcast_to(w_ref[pl.ds(place_ref[first + c], 1), :], (8, LANES))[None] for c in range(chunks)
        ]

        def body(r, carry):
            at = row_block(r)
            parts = [
                e_ref[at, c * LANES : (c + 1) * LANES].reshape(ROWS // 8, 8, LANES) * w[c] for c in range(chunks)
            ]
            acc = sum(parts[1:], parts[0]).reshape(ROWS, LANES)
            rowacc_ref[at, :] = acc if at_e == 0 else rowacc_ref[at, :] + acc
            return carry

        lax.fori_loop(0, rows // ROWS, body, 0, unroll=4)
        first += chunks
    for q in range(rows // LANES):
        y_ref[q : q + 1, :] = lane_fold(rowacc_ref[q * LANES : (q + 1) * LANES, :], jnp.sum)


def self_apply(kernel, parts, w, place, out_rows):
    rows = parts[0].shape[0]
    vmem = pl.BlockSpec(memory_space=pltpu.VMEM)
    return pl.pallas_call(
        functools.partial(kernel, len(parts)),
        in_specs=[vmem] * (len(parts) + 1) + [pl.BlockSpec(memory_space=pltpu.SMEM)],
        out_shape=jax.ShapeDtypeStruct((out_rows, LANES), F32),
        out_specs=vmem,
        scratch_shapes=[pltpu.VMEM((rows, LANES), F32)],
        compiler_params=pltpu.CompilerParams(vmem_limit_bytes=8 << 20),
    )(*[vmem_array(part) for part in parts], w, place)


def log_add(parts):
    top = functools.reduce(jnp.maximum, parts)
    return top + jnp.log2(sum(jnp.exp2(part - top) for part in parts))


def build(n_z, n_y, n_core, n_ref):
    n_zy = n_z * n_y
    n_gen = n_zy * n_core
    assert n_z == n_y == n_ref == 4 and n_core == 2

    def place_of(g):
        return g // (n_y * n_core), (g // n_core) % n_y, g % n_core

    def gen_perm(move):
        out = []
        for g in range(n_gen):
            z, y, c = move(*place_of(g))
            out.append((g, ((z % n_z) * n_y + y % n_y) * n_core + c % n_core))
        return out

    core_stage = [gen_perm(lambda z, y, c: (z, y, c + 1))]
    y_stage = [gen_perm(lambda z, y, c: (z, y + k, c)) for k in (1, 2, 3)]
    z_stage = [gen_perm(lambda z, y, c: (z + k, y, c)) for k in (1, 2, 3)]
    ref_stage = [[(i, (i + k) % n_ref) for i in range(n_ref)] for k in (1, 2, 3)]
    first_axis = {k: gen_perm(lambda z, y, c: (z, y + k, c) if c == 0 else (z + k, y, c)) for k in (1, 2, 3)}
    second_axis = {k: gen_perm(lambda z, y, c: (z + k, y, c) if c == 0 else (z, y + k, c)) for k in (1, 3)}
    order = [(0, 0), (0, 1), (0, 2), (0, 3)]
    order += [(1, 0), (1, 1), (1, 2), (1, 3), (3, 0), (3, 1), (3, 2), (3, 3)]
    order += [(2, 0), (2, 1), (2, 2), (2, 3)]

    def shift(value, axis, perms):
        return [lax.ppermute(value, axis, perm) for perm in perms]

    def merge(parts, logs):
        top = log_add([part[:logs] for part in parts])
        if parts[0].shape[0] == logs:
            return top
        return jnp.concatenate([top, sum(part[logs:] for part in parts)], axis=0)

    def stage(value, axis, perms, logs):
        return merge([value] + shift(value, axis, perms), logs)

    def doubled(value, logs):
        for flip in (1, n_ref - 1):
            value = merge([value, lax.ppermute(value, "ref", [(i, i ^ flip) for i in range(n_ref)])], logs)
        return value

    def run(gen_features, gen_weight, ref_features, ref_weight, ref_self):
        gen_count = gen_features.shape[0]
        ref_count = ref_features.shape[0]
        nq, nc = gen_count // LANES, ref_count // LANES
        g = lax.axis_index("gen")
        x = lax.axis_index("ref")
        z, y, core = place_of(g)
        zy = z * n_y + y
        b, a = (lax.broadcasted_iota(jnp.int32, (len(order),), 0) for _ in range(2))
        b = functools.reduce(lambda v, k: jnp.where(a == k, order[k][0], v), range(len(order)), b)
        a = a % 4
        mine = ((z - b + n_z) % n_z) * n_y + (y - a + n_y) % n_y
        other = ((z - a + n_z) % n_z) * n_y + (y - b + n_y) % n_y
        place = jnp.where(core == 0, mine, other)
        at_zy = (lax.broadcasted_iota(jnp.int32, (n_zy, LANES), 0) == zy).astype(F32)
        at_x = (lax.broadcasted_iota(jnp.int32, (n_ref, LANES), 0) == x).astype(F32)
        wg = gen_weight.reshape(nq, LANES)
        wg, place, at_zy, at_x = lax.optimization_barrier((wg, place, at_zy, at_x))
        own, held, tile0, wg, wr = entry(
            gen_features, ref_features, wg, ref_weight.reshape(nc, LANES)
        )

        def to_cols(rows):
            picked = jnp.sum(jnp.where(at_x > 0, rows, 0.0), axis=0, keepdims=True)
            return jnp.where(at_zy > 0, picked, 0.0)

        def to_rows(cols):
            picked = jnp.sum(jnp.where(at_zy > 0, cols, 0.0), axis=0, keepdims=True)
            return jnp.where(at_x > 0, picked, 0.0)

        got = {}
        for k in (1, 3, 2):
            got[k] = lax.ppermute(own, "gen", first_axis[k])
        mate = lax.ppermute(held, "gen", core_stage[0])
        near = jnp.concatenate([own, got[1], got[2], got[3]], axis=0)
        up = lax.ppermute(near, "gen", second_axis[1])
        down = lax.ppermute(near, "gen", second_axis[3])
        low_far = lax.ppermute(up[: 2 * LANES], "gen", second_axis[1])
        high_far = lax.ppermute(down[2 * LANES :], "gen", second_axis[3])

        d0, hcol, mine, gmass, ahead, *carried = first_pass(held, tile0, ref_features, wg, wr)
        theirs = lax.ppermute(mine, "gen", core_stage[0])
        d1, row_part, lcol, hcol = first_pass(held, ahead, ref_features, wr, mine, d0, hcol, *carried)
        hrow = mine[:nq]
        weight = jnp.concatenate([wg, theirs[nq:]], axis=0)
        e0, z1_0, hs, ws = self_first(held, mate, [near], mine, theirs, place, 0)
        e1, z1_1 = self_first(held, mate, [up, down], hs, ws, place, 4)
        e2, z1_2 = self_first(held, mate, [low_far, high_far], hs, ws, place, 12)
        e = [e0, e1, e2]

        row_part = doubled(row_part, nq)
        col_part = jnp.concatenate([lcol, gmass], axis=0)
        col_part = stage(col_part, "gen", core_stage, nc)
        col_part = jnp.concatenate([col_part, to_cols(wg)], axis=0)
        col_part = stage(col_part, "gen", y_stage, nc)
        col_part = stage(col_part, "gen", z_stage, nc)
        gmass = col_part[nc : nc + 1]
        rmass = row_part[nq : nq + 1]
        wcols = col_part[nc + 8 :] / gmass
        gmass_log = jnp.log2(gmass)
        rmass_log = jnp.log2(rmass)
        f = hrow - (row_part[:nq] - rmass_log)
        c = hcol - (col_part[:nc] - gmass_log)
        ubase = jnp.log2(wr) - rmass_log - hcol
        vbase = jnp.log2(wg) - gmass_log - hrow
        share = wg / gmass

        lrow, lcol = next_pass([d0, d1], ubase + c, vbase + f)
        lrow = doubled(lrow, nq)
        lcol = stage(lcol, "gen", core_stage, nc)
        col_part = jnp.concatenate([lcol, z1_0 + z1_1 + z1_2], axis=0)
        col_part = stage(col_part, "gen", y_stage, nc)
        col_part = stage(col_part, "gen", z_stage, nc)
        f = 0.5 * (f + (hrow - lrow))
        c = 0.5 * (c + (hcol - col_part[:nc]))
        y1 = col_part[nc:] / gmass

        lrow, lcol = next_pass([d0, d1], ubase + c, vbase + f)
        y2 = self_apply(self_rows_kernel, e, wcols / y1, place, 2 * nq)
        row_part = jnp.concatenate([lrow, y2, to_rows(-jnp.log2(y1))], axis=0)
        row_part = stage(row_part, "ref", ref_stage, nq)
        f = 0.5 * (f + (hrow - row_part[:nq]))
        f_part = share * f
        f_part = jnp.concatenate([f_part, f_part], axis=0)
        mine = jnp.concatenate([lcol, f_part, row_part[nq:]], axis=0)
        theirs = shift(mine, "gen", core_stage)[0]
        lcol = log_add([lcol, theirs[:nc]])
        f_part = f_part + theirs[nc : nc + 8]
        y2, y2_mate, s1 = row_part[nq : 2 * nq], row_part[2 * nq : 3 * nq], row_part[3 * nq :]
        at = nc + 8
        y2 = y2 + theirs[at + nq : at + 2 * nq]
        y2_mate = y2_mate + theirs[at : at + nq]
        s1 = jnp.concatenate([s1, theirs[at + 2 * nq :]], axis=0)
        s2 = 0.5 * (s1 - jnp.log2(jnp.concatenate([y2, y2_mate], axis=0)))
        w3 = weight / gmass * jnp.exp2(s2)
        z3 = self_apply(self_cols_kernel, e, w3, place, n_zy)
        col_part = jnp.concatenate([lcol, f_part, z3, to_cols(s2[:nq])], axis=0)
        col_part = stage(col_part, "gen", y_stage, nc)
        col_part = stage(col_part, "gen", z_stage, nc)
        c = 0.5 * (c + (hcol - col_part[:nc]))
        f_part = col_part[nc : nc + nq]
        z3, s2 = col_part[nc + 8 : nc + 8 + n_zy], col_part[nc + 8 + n_zy :]

        unit = EPS / LOG2E
        ref_gap = c * unit - ref_self.reshape(nc, LANES)
        s3 = 0.5 * (s2 - jnp.log2(z3))
        s_part = jnp.sum((wcols * s3).reshape(2, 8, LANES), axis=0)
        s_part = s_part + shift(s_part, "gen", core_stage)[0]
        part = jnp.sum(((wr / rmass) * ref_gap).reshape(nc // 8, 8, LANES), axis=0) - unit * s_part
        row_part = jnp.concatenate([to_rows(s3), part], axis=0)
        row_part = row_part + sum(shift(row_part, "ref", ref_stage))
        gen_gap = (f - row_part[:nq]) * unit
        divergence = jnp.sum(unit * f_part + row_part[nq : 2 * nq] + row_part[2 * nq :])
        return gen_gap.reshape(gen_count), ref_gap.reshape(ref_count), divergence

    return run


def solution(mesh):
    n_gen, n_ref = mesh.shape["gen"], mesh.shape["ref"]
    n_core = 2
    n_y = 1
    while n_y * n_y * n_core < n_gen:
        n_y *= 2
    placed = (P("gen", None), P("gen"), P("ref", None), P("ref"), P("ref"))
    return jax.shard_map(
        build(n_gen // (n_y * n_core), n_y, n_core, n_ref),
        mesh=mesh,
        in_specs=placed,
        out_specs=(P("gen"), P("ref"), P()),
        check_vma=False,
    )
```

```python
import functools

import jax
import jax.numpy as jnp
from jax import lax
from jax.experimental import pallas as pl
from jax.experimental.pallas import tpu as pltpu
from jax.sharding import PartitionSpec as P


EPS = 0.1
LOG2E = 1.4426950408889634
F32 = jnp.float32
LANES = 128
TILE = 512
ROWS = 32
LEAD = 6
LOW = 2.0**-80
HIGH = 2.0**120


def vmem_array(x):
    return pltpu.with_memory_space_constraint(x, pltpu.VMEM)


def hbm_array(x):
    return pltpu.with_memory_space_constraint(x, pltpu.HBM)


def spread(vec_ref, out_ref, count, first=0, at=0):
    for q in range(count):
        block = jnp.broadcast_to(vec_ref[first + q : first + q + 1, :], (LANES, LANES))
        out_ref[(at + q) * LANES : (at + q + 1) * LANES, :] = block.T


def lane_fold(acc, op):
    return op(acc.T, axis=0, keepdims=True)


def norms(feat_ref, start, count, scale):
    width = feat_ref.shape[1]
    out = []
    for q in range(count):
        acc = jnp.zeros((LANES, LANES), F32)
        for c in range(width // LANES):
            x = feat_ref[start + q * LANES : start + (q + 1) * LANES, c * LANES : (c + 1) * LANES].astype(F32)
            acc = acc + x * x
        out.append(lane_fold(acc, jnp.sum) * scale)
    return out


def row_block(r):
    if isinstance(r, int):
        return slice(r * ROWS, (r + 1) * ROWS)
    return pl.ds(pl.multiple_of(r * ROWS, ROWS), ROWS)


def sweep(d_ref, base, chunks, u, vs_ref, rowacc_ref, straight=False, keep=None):
    rows = d_ref.shape[0]
    u = [jnp.broadcast_to(part, (8, LANES))[None] for part in u]

    def body(r, cols):
        at = row_block(r)
        vs = vs_ref[at, :].reshape(ROWS // 8, 8, LANES)
        racc = rowacc_ref[at, :].reshape(ROWS // 8, 8, LANES)
        out = []
        for c in range(chunks):
            d = d_ref[at, pl.ds(base + c * LANES, LANES)]
            if keep is not None:
                keep[0][at, pl.ds(pl.multiple_of(keep[1] + c * LANES, LANES), LANES)] = d
            p = jnp.exp2((d.reshape(ROWS // 8, 8, LANES) + u[c]) + vs)
            racc = racc + p
            out.append(cols[c] + jnp.sum(p, axis=0))
        rowacc_ref[at, :] = racc.reshape(ROWS, LANES)
        return tuple(out)

    cols = (jnp.zeros((8, LANES), F32),) * chunks
    if straight:
        for r in range(rows // ROWS):
            cols = body(r, cols)
    else:
        cols = lax.fori_loop(0, rows // ROWS, body, cols, unroll=4)
    return [jnp.sum(c, axis=0, keepdims=True) for c in cols]


def tile_peak(d_ref, u, vs_ref):
    rows = d_ref.shape[0]
    best = jnp.full((8, LANES), -3.0e38, F32)

    def body(r, best):
        at = pl.ds(pl.multiple_of(r * ROWS, ROWS), ROWS)
        val = (d_ref[at, 0:LANES] + u) + vs_ref[at, :]
        return jnp.maximum(best, jnp.max(val.reshape(ROWS // 8, 8, LANES), axis=0))

    best = lax.fori_loop(0, rows // ROWS, body, best, unroll=2)
    return jnp.max(jnp.max(best, axis=0, keepdims=True), axis=1, keepdims=True)


def start_peak(d_ref, u0, v_ref, vs_ref, peak_ref, rowacc_ref):
    rows = d_ref.shape[0]
    spread(v_ref, vs_ref, rows // LANES)
    peak = jnp.broadcast_to(tile_peak(d_ref, u0, vs_ref), (8, LANES))
    peak_ref[...] = peak
    vs_ref[...] = vs_ref[...] - peak[0:1, :]
    rowacc_ref[...] = jnp.zeros_like(rowacc_ref)


def finish(d_refs, u_ref, v_ref, vs_ref, rowacc_ref, colsum_ref, peak_ref, lrow_ref, lcol_ref):
    rows = d_refs[0].shape[0]
    nq = rows // LANES
    rowsum = [lane_fold(rowacc_ref[q * LANES : (q + 1) * LANES, :], jnp.sum) for q in range(nq)]
    rowsum = jnp.concatenate(rowsum, axis=0)
    colsum = colsum_ref[...]
    low = jnp.minimum(jnp.min(rowsum), jnp.min(colsum))
    high = jnp.maximum(jnp.max(rowsum), jnp.max(colsum))
    good = jnp.logical_and(low >= LOW, high <= HIGH)
    peak = peak_ref[0:1, :]

    @pl.when(good)
    def _():
        lrow_ref[0:nq, :] = (jnp.log2(rowsum) + peak) - v_ref[...]
        lcol_ref[...] = (jnp.log2(colsum) + peak) - u_ref[...]

    @pl.when(jnp.logical_not(good))
    def _():
        spread(v_ref, vs_ref, nq)

        def row_block(q, carry):
            part = pl.ds(pl.multiple_of(q * LANES, LANES), LANES)

            def scores(d_ref, first, c):
                at = pl.ds(pl.multiple_of(c * LANES, LANES), LANES)
                return d_ref[part, at] + u_ref[pl.ds(first + c, 1), :]

            best = jnp.full((LANES, LANES), -3.0e38, F32)
            first = 0
            for d_ref in d_refs:
                count = d_ref.shape[1] // LANES
                best = lax.fori_loop(
                    0, count, lambda c, best: jnp.maximum(best, scores(d_ref, first, c)), best
                )
                first += count
            top = jnp.max(best, axis=1, keepdims=True)
            acc = jnp.zeros((LANES, LANES), F32)
            first = 0
            for d_ref in d_refs:
                count = d_ref.shape[1] // LANES
                acc = lax.fori_loop(
                    0, count, lambda c, acc: acc + jnp.exp2(scores(d_ref, first, c) - top), acc
                )
                first += count
            log_sum = jnp.log2(jnp.sum(acc, axis=1, keepdims=True)) + top
            lrow_ref[pl.ds(q, 1), :] = lane_fold(jnp.broadcast_to(log_sum, (LANES, LANES)), jnp.max)
            return carry

        lax.fori_loop(0, nq, row_block, 0)
        first = 0
        for d_ref in d_refs:
            count = d_ref.shape[1] // LANES

            def column(c, carry):
                at = pl.ds(pl.multiple_of(c * LANES, LANES), LANES)

                def block(r):
                    part = pl.ds(pl.multiple_of(r * ROWS, ROWS), ROWS)
                    return d_ref[part, at] + vs_ref[part, :]

                top = lax.fori_loop(
                    0,
                    rows // ROWS,
                    lambda r, best: jnp.maximum(best, jnp.max(block(r), axis=0, keepdims=True)),
                    jnp.full((1, LANES), -3.0e38, F32),
                )
                total = lax.fori_loop(
                    0,
                    rows // ROWS,
                    lambda r, acc: acc + jnp.sum(jnp.exp2(block(r) - top), axis=0, keepdims=True),
                    jnp.zeros((1, LANES), F32),
                )
                lcol_ref[pl.ds(first + c, 1), :] = top + jnp.log2(total)
                return carry

            lax.fori_loop(0, count, column, 0)
            first += count


def entry_kernel(gen_hbm, ref_hbm, gweight_hbm, rweight_hbm, own_ref, gen_ref, tile_ref, gweight_ref, rweight_ref, sem):
    count = own_ref.shape[0]
    at = pl.ds(pl.multiple_of(lax.axis_index("ref") * count, count), count)
    pairs = (
        (gen_hbm.at[at, :], own_ref),
        (gweight_hbm, gweight_ref),
        (rweight_hbm, rweight_ref),
        (gen_hbm, gen_ref),
        (ref_hbm.at[: tile_ref.shape[0], :], tile_ref),
    )
    copies = [pltpu.make_async_copy(src, dst, sem.at[k]) for k, (src, dst) in enumerate(pairs)]
    for copy in copies:
        copy.start()
    for copy in copies:
        copy.wait()


def entry(gen, ref, gweight, rweight):
    vmem = pl.BlockSpec(memory_space=pltpu.VMEM)
    hbm = pl.BlockSpec(memory_space=pltpu.HBM)
    width = gen.shape[1]
    return pl.pallas_call(
        entry_kernel,
        in_specs=[hbm] * 4,
        out_shape=(
            pltpu.VMEM((LANES, width), gen.dtype),
            pltpu.VMEM(gen.shape, gen.dtype),
            pltpu.VMEM((TILE, width), ref.dtype),
            pltpu.VMEM(gweight.shape, F32),
            pltpu.VMEM(rweight.shape, F32),
        ),
        out_specs=(vmem,) * 5,
        scratch_shapes=[pltpu.SemaphoreType.DMA((5,))],
        compiler_params=pltpu.CompilerParams(vmem_limit_bytes=4 << 20),
        name="entry",
    )(*[hbm_array(x) for x in (gen, ref, gweight, rweight)])


def total(x):
    return jnp.sum(jnp.sum(x, axis=0, keepdims=True), axis=1, keepdims=True)


def first_kernel(first_tile, steps, *refs):
    leading = first_tile == 0
    if leading:
        gen_ref, first_ref, gweight_ref, rweight_ref, ref_hbm, *refs = refs
        d_ref, hcol_ref, hrow_ref, mass_ref, ahead_ref, vs_ref, rowacc_ref, u_ref, colsum_ref, peak_ref, *refs = refs
        tile_ref, stage_ref, v_ref, sem = refs
    else:
        gen_ref, first_ref, rweight_ref, hrow_ref, ref_hbm, before_ref, *refs = refs
        hcol0_ref, vs_ref, rowacc0_ref, u0_ref, colsum0_ref, peak_ref, *refs = refs
        d_ref, lrow_ref, lcol_ref, hcol_ref, tile_ref, stage_ref, v_ref, rowacc_ref, u_ref, colsum_ref, sem = refs
    rows, width = gen_ref.shape
    nq = rows // LANES
    chunks = TILE // LANES
    half_scale = 0.5 * LOG2E / (EPS * width)
    dot_scale = LOG2E / (EPS * width)

    def load(j):
        at = pl.ds(pl.multiple_of((first_tile + j) * TILE, TILE), TILE)
        return pltpu.make_async_copy(ref_hbm.at[at, :], tile_ref.at[j], sem.at[j])

    def product(j, tile, out_ref, columns):
        for c, half in enumerate(norms(tile, 0, chunks, half_scale)):
            row = pl.ds((first_tile + j) * chunks + c, 1)
            hcol_ref[row, :] = half
            u_ref[row, :] = jnp.log2(rweight_ref[row, :]) - half
        dots = lax.dot_general(gen_ref[...], tile[...], (((1,), (1,)), ((), ())), preferred_element_type=F32)
        out_ref[:, columns] = dots * dot_scale

    def sums(j, straight, src_ref, base, keep):
        mine = [u_ref[pl.ds(j * chunks + c, 1), :] for c in range(chunks)]
        for c, part in enumerate(sweep(src_ref, base, chunks, mine, vs_ref, rowacc_ref, straight, keep)):
            colsum_ref[pl.ds(j * chunks + c, 1), :] = part

    whole = slice(0, TILE)
    load(1).start()
    if leading:
        ahead = pltpu.make_async_copy(ref_hbm.at[steps * TILE : (steps + 1) * TILE, :], ahead_ref, sem.at[steps])
        for q, part in enumerate(norms(gen_ref, 0, nq, half_scale)):
            hrow_ref[q : q + 1, :] = part
            v_ref[q : q + 1, :] = jnp.log2(gweight_ref[q : q + 1, :]) - part
            hrow_ref[nq + q : nq + q + 1, :] = gweight_ref[q : q + 1, :]
        mass_ref[...] = jnp.broadcast_to(total(gweight_ref[...]), (8, LANES))
        product(0, first_ref, stage_ref, whole)
        start_peak(stage_ref, u_ref[0:1, :], v_ref, vs_ref, peak_ref, rowacc_ref)
    else:
        v_ref[...] = jnp.log2(hrow_ref[nq : 2 * nq, :]) - hrow_ref[0:nq, :]
        lrow_ref[nq : 2 * nq, :] = jnp.broadcast_to(total(rweight_ref[...]), (nq, LANES))
        done = first_tile * chunks
        hcol_ref[0:done, :] = hcol0_ref[...]
        rowacc_ref[...] = rowacc0_ref[...]
        u_ref[0:done, :] = u0_ref[...]
        colsum_ref[0:done, :] = colsum0_ref[...]
        sums(first_tile - 1, True, before_ref, (first_tile - 1) * TILE, None)
        product(0, first_ref, stage_ref, whole)

    def step(j, carry):
        load(j).wait()

        @pl.when(j + 1 < steps)
        def _():
            load(j + 1).start()

        sums(first_tile + j - 1, True, stage_ref, 0, (d_ref, (j - 1) * TILE))
        product(j, tile_ref.at[j], stage_ref, whole)
        return carry

    if leading:
        lax.fori_loop(1, steps - 1, step, 0)
        load(steps - 1).wait()
        ahead.start()
        sums(steps - 2, True, stage_ref, 0, (d_ref, (steps - 2) * TILE))
        product(steps - 1, tile_ref.at[steps - 1], d_ref, slice((steps - 1) * TILE, steps * TILE))
        colsum_ref[(steps - 1) * chunks : steps * chunks, :] = jnp.zeros((chunks, LANES), F32)
        ahead.wait()
    else:
        lax.fori_loop(1, steps, step, 0)
        sums(first_tile + steps - 1, False, stage_ref, 0, (d_ref, (steps - 1) * TILE))
        finish([before_ref, d_ref], u_ref, v_ref, vs_ref, rowacc_ref, colsum_ref, peak_ref, lrow_ref, lcol_ref)


def first_pass(gen, first, ref, *more):
    rows, width = gen.shape
    nq, tiles = rows // LANES, ref.shape[0] // TILE
    leading = len(more) == 2
    first_tile, steps = (0, LEAD) if leading else (LEAD, tiles - LEAD)
    cols = steps * TILE
    nc, all_nc = cols // LANES, ref.shape[0] // LANES
    vmem = pl.BlockSpec(memory_space=pltpu.VMEM)
    hbm = pl.BlockSpec(memory_space=pltpu.HBM)
    vec = lambda n: jax.ShapeDtypeStruct((n, LANES), F32)
    lanes = pltpu.VMEM((rows, LANES), F32)
    scratch = [
        pltpu.VMEM((steps, TILE, width), jnp.bfloat16),
        pltpu.VMEM((rows, TILE), F32),
        pltpu.VMEM((nq, LANES), F32),
    ]
    if leading:
        gweight, rweight = more
        operands = [vmem_array(gen), vmem_array(first), gweight, rweight, hbm_array(ref)]
        outs = (
            pltpu.VMEM((rows, cols), F32), vec(nc), vec(2 * nq), vec(8), pltpu.VMEM((TILE, width), ref.dtype),
            lanes, lanes, vec(nc), vec(nc), vec(8),
        )
        specs = [vmem] * 4 + [hbm]
    else:
        rweight, hrow, before, hcol, vs, rowacc, u, colsum, peak = more
        operands = [vmem_array(gen), vmem_array(first), rweight, hrow, hbm_array(ref), vmem_array(before)]
        operands += [hcol, vmem_array(vs), vmem_array(rowacc), u, colsum, peak]
        outs = (pltpu.VMEM((rows, cols), F32), vec(2 * nq), vec(all_nc), vec(all_nc))
        specs = [vmem] * 4 + [hbm] + [vmem] * 7
        scratch += [
            pltpu.VMEM((rows, LANES), F32),
            pltpu.VMEM((all_nc, LANES), F32),
            pltpu.VMEM((all_nc, LANES), F32),
        ]
    return pl.pallas_call(
        functools.partial(first_kernel, first_tile, steps),
        in_specs=specs,
        out_shape=outs,
        out_specs=(vmem,) * len(outs),
        scratch_shapes=scratch + [pltpu.SemaphoreType.DMA((steps + 1,))],
        compiler_params=pltpu.CompilerParams(vmem_limit_bytes=20 << 20),
        name="cross_first_0" if leading else "cross_first_1",
    )(*operands)


def next_kernel(count, *refs):
    sources = refs[:count]
    u_ref, v_ref, lrow_ref, lcol_ref, vs_ref, rowacc_ref, colsum_ref, peak_ref = refs[count:]
    chunks = TILE // LANES
    start_peak(sources[0], u_ref[0:1, :], v_ref, vs_ref, peak_ref, rowacc_ref)
    first = 0
    for d_ref in sources:
        steps = d_ref.shape[1] // TILE

        def step(j, carry):
            u = [u_ref[pl.ds(first + j * chunks + c, 1), :] for c in range(chunks)]
            base = pl.multiple_of(j * TILE, TILE)
            for c, part in enumerate(sweep(d_ref, base, chunks, u, vs_ref, rowacc_ref)):
                colsum_ref[pl.ds(first + j * chunks + c, 1), :] = part
            return carry

        lax.fori_loop(0, steps, step, 0)
        first += steps * chunks
    finish(sources, u_ref, v_ref, vs_ref, rowacc_ref, colsum_ref, peak_ref, lrow_ref, lcol_ref)


def next_pass(parts, u, v):
    rows = parts[0].shape[0]
    cols = sum(part.shape[1] for part in parts)
    nq, nc = rows // LANES, cols // LANES
    vmem = pl.BlockSpec(memory_space=pltpu.VMEM)
    return pl.pallas_call(
        functools.partial(next_kernel, len(parts)),
        in_specs=[vmem] * (len(parts) + 2),
        out_shape=(jax.ShapeDtypeStruct((nq, LANES), F32), jax.ShapeDtypeStruct((nc, LANES), F32)),
        out_specs=(vmem, vmem),
        scratch_shapes=[
            pltpu.VMEM((rows, LANES), F32),
            pltpu.VMEM((rows, LANES), F32),
            pltpu.VMEM((nc, LANES), F32),
            pltpu.VMEM((8, LANES), F32),
        ],
        compiler_params=pltpu.CompilerParams(vmem_limit_bytes=8 << 20),
    )(*[vmem_array(part) for part in parts], u, v)


def self_first_kernel(count, first, *refs):
    own_ref, mate_ref = refs[:2]
    sources = refs[2 : 2 + count]
    rest = refs[2 + count :]
    half, width = own_ref.shape
    nq = half // LANES
    if first == 0:
        mine_ref, theirs_ref, place_ref, e_ref, z_ref, hs_ref, ws_ref = rest
        for at, vec_ref in ((0, mine_ref), (nq, theirs_ref)):
            spread(vec_ref, hs_ref, nq, 0, at)
            spread(vec_ref, ws_ref, nq, nq, at)
    else:
        hs_ref, ws_ref, place_ref, e_ref, z_ref = rest
    wide = 256
    chunks = wide // LANES
    half_scale = 0.5 * LOG2E / (EPS * width)
    dot_scale = LOG2E / (EPS * width)
    z_ref[...] = jnp.zeros_like(z_ref)
    tiles = [(src, k) for src in sources for k in range(src.shape[0] // wide)]
    piece_half = {}

    def product(t):
        src, k = tiles[t]
        view = src.at[k * wide : (k + 1) * wide, :]
        piece_half[t] = norms(view, 0, chunks, half_scale)
        for h, rows_ref in enumerate((own_ref, mate_ref)):
            e_ref[h * half : (h + 1) * half, t * wide : (t + 1) * wide] = lax.dot_general(
                rows_ref[...], view[...], (((1,), (1,)), ((), ())), preferred_element_type=F32
            )

    def sums(t, straight):
        def body(r, acc):
            at = row_block(r)
            hs = hs_ref[at, :]
            ws = ws_ref[at, :]
            out = []
            for c in range(chunks):
                part = slice(t * wide + c * LANES, t * wide + (c + 1) * LANES)
                e = jnp.exp2(e_ref[at, part] * dot_scale - (hs + piece_half[t][c]))
                e_ref[at, part] = e
                out.append(acc[c] + jnp.sum((e * ws).reshape(ROWS // 8, 8, LANES), axis=0))
            return tuple(out)

        acc = (jnp.zeros((8, LANES), F32),) * chunks
        if straight:
            for r in range(2 * half // ROWS):
                acc = body(r, acc)
        else:
            acc = lax.fori_loop(0, 2 * half // ROWS, body, acc, unroll=2)
        for c in range(chunks):
            z_ref[pl.ds(place_ref[first + t * chunks + c], 1), :] = jnp.sum(acc[c], axis=0, keepdims=True)

    product(0)
    for t in range(1, len(tiles)):
        sums(t - 1, True)
        product(t)
    sums(len(tiles) - 1, False)


def self_first(own, mate, sources, left, right, place, first):
    rows = 2 * own.shape[0]
    cols = sum(src.shape[0] for src in sources)
    vmem = pl.BlockSpec(memory_space=pltpu.VMEM)
    lanes = () if first else (pltpu.VMEM((rows, LANES), F32),) * 2
    if first:
        left, right = vmem_array(left), vmem_array(right)
    return pl.pallas_call(
        functools.partial(self_first_kernel, len(sources), first),
        in_specs=[vmem] * (4 + len(sources)) + [pl.BlockSpec(memory_space=pltpu.SMEM)],
        out_shape=(pltpu.VMEM((rows, cols), F32), jax.ShapeDtypeStruct((place.shape[0], LANES), F32)) + lanes,
        out_specs=(vmem,) * (2 + len(lanes)),
        compiler_params=pltpu.CompilerParams(vmem_limit_bytes=8 << 20),
    )(vmem_array(own), vmem_array(mate), *[vmem_array(src) for src in sources], left, right, place)


def self_cols_kernel(count, *refs):
    w_ref, place_ref, z_ref, ws_ref = refs[count:]
    rows = refs[0].shape[0]
    chunks = TILE // LANES
    spread(w_ref, ws_ref, rows // LANES)
    first = 0
    for e_ref in refs[:count]:
        for base in range(0, e_ref.shape[1], TILE):

            def body(r, acc):
                at = row_block(r)
                ws = ws_ref[at, :]
                out = []
                for c in range(chunks):
                    e = e_ref[at, base + c * LANES : base + (c + 1) * LANES] * ws
                    out.append(acc[c] + jnp.sum(e.reshape(ROWS // 8, 8, LANES), axis=0))
                return tuple(out)

            acc = lax.fori_loop(0, rows // ROWS, body, (jnp.zeros((8, LANES), F32),) * chunks, unroll=4)
            for c in range(chunks):
                z_ref[pl.ds(place_ref[first + c], 1), :] = jnp.sum(acc[c], axis=0, keepdims=True)
            first += chunks


def self_rows_kernel(count, *refs):
    w_ref, place_ref, y_ref, rowacc_ref = refs[count:]
    rows = refs[0].shape[0]
    first = 0
    for at_e, e_ref in enumerate(refs[:count]):
        chunks = e_ref.shape[1] // LANES
        w = [
            jnp.broadcast_to(w_ref[pl.ds(place_ref[first + c], 1), :], (8, LANES))[None] for c in range(chunks)
        ]

        def body(r, carry):
            at = row_block(r)
            parts = [
                e_ref[at, c * LANES : (c + 1) * LANES].reshape(ROWS // 8, 8, LANES) * w[c] for c in range(chunks)
            ]
            acc = sum(parts[1:], parts[0]).reshape(ROWS, LANES)
            rowacc_ref[at, :] = acc if at_e == 0 else rowacc_ref[at, :] + acc
            return carry

        lax.fori_loop(0, rows // ROWS, body, 0, unroll=4)
        first += chunks
    for q in range(rows // LANES):
        y_ref[q : q + 1, :] = lane_fold(rowacc_ref[q * LANES : (q + 1) * LANES, :], jnp.sum)


def self_apply(kernel, parts, w, place, out_rows):
    rows = parts[0].shape[0]
    vmem = pl.BlockSpec(memory_space=pltpu.VMEM)
    return pl.pallas_call(
        functools.partial(kernel, len(parts)),
        in_specs=[vmem] * (len(parts) + 1) + [pl.BlockSpec(memory_space=pltpu.SMEM)],
        out_shape=jax.ShapeDtypeStruct((out_rows, LANES), F32),
        out_specs=vmem,
        scratch_shapes=[pltpu.VMEM((rows, LANES), F32)],
        compiler_params=pltpu.CompilerParams(vmem_limit_bytes=8 << 20),
    )(*[vmem_array(part) for part in parts], w, place)


def log_add(parts):
    top = functools.reduce(jnp.maximum, parts)
    return top + jnp.log2(sum(jnp.exp2(part - top) for part in parts))


def build(n_z, n_y, n_core, n_ref):
    n_zy = n_z * n_y
    n_gen = n_zy * n_core
    assert n_z == n_y == n_ref == 4 and n_core == 2

    def place_of(g):
        return g // (n_y * n_core), (g // n_core) % n_y, g % n_core

    def gen_perm(move):
        out = []
        for g in range(n_gen):
            z, y, c = move(*place_of(g))
            out.append((g, ((z % n_z) * n_y + y % n_y) * n_core + c % n_core))
        return out

    core_stage = [gen_perm(lambda z, y, c: (z, y, c + 1))]
    y_stage = [gen_perm(lambda z, y, c: (z, y + k, c)) for k in (1, 2, 3)]
    z_stage = [gen_perm(lambda z, y, c: (z + k, y, c)) for k in (1, 2, 3)]
    ref_stage = [[(i, (i + k) % n_ref) for i in range(n_ref)] for k in (1, 2, 3)]
    first_axis = {k: gen_perm(lambda z, y, c: (z, y + k, c) if c == 0 else (z + k, y, c)) for k in (1, 2, 3)}
    second_axis = {k: gen_perm(lambda z, y, c: (z + k, y, c) if c == 0 else (z, y + k, c)) for k in (1, 3)}
    order = [(0, 0), (0, 1), (0, 2), (0, 3)]
    order += [(1, 0), (1, 1), (1, 2), (1, 3), (3, 0), (3, 1), (3, 2), (3, 3)]
    order += [(2, 0), (2, 1), (2, 2), (2, 3)]

    def shift(value, axis, perms):
        return [lax.ppermute(value, axis, perm) for perm in perms]

    def merge(parts, logs):
        top = log_add([part[:logs] for part in parts])
        if parts[0].shape[0] == logs:
            return top
        return jnp.concatenate([top, sum(part[logs:] for part in parts)], axis=0)

    def stage(value, axis, perms, logs):
        return merge([value] + shift(value, axis, perms), logs)

    def doubled(value, logs):
        for flip in (1, n_ref - 1):
            value = merge([value, lax.ppermute(value, "ref", [(i, i ^ flip) for i in range(n_ref)])], logs)
        return value

    def run(gen_features, gen_weight, ref_features, ref_weight, ref_self):
        gen_count = gen_features.shape[0]
        ref_count = ref_features.shape[0]
        nq, nc = gen_count // LANES, ref_count // LANES
        g = lax.axis_index("gen")
        x = lax.axis_index("ref")
        z, y, core = place_of(g)
        zy = z * n_y + y
        b, a = (lax.broadcasted_iota(jnp.int32, (len(order),), 0) for _ in range(2))
        b = functools.reduce(lambda v, k: jnp.where(a == k, order[k][0], v), range(len(order)), b)
        a = a % 4
        mine = ((z - b + n_z) % n_z) * n_y + (y - a + n_y) % n_y
        other = ((z - a + n_z) % n_z) * n_y + (y - b + n_y) % n_y
        place = jnp.where(core == 0, mine, other)
        at_zy = (lax.broadcasted_iota(jnp.int32, (n_zy, LANES), 0) == zy).astype(F32)
        at_x = (lax.broadcasted_iota(jnp.int32, (n_ref, LANES), 0) == x).astype(F32)
        wg = gen_weight.reshape(nq, LANES)
        wg, place, at_zy, at_x = lax.optimization_barrier((wg, place, at_zy, at_x))
        own, held, tile0, wg, wr = entry(
            gen_features, ref_features, wg, ref_weight.reshape(nc, LANES)
        )

        def to_cols(rows):
            picked = jnp.sum(jnp.where(at_x > 0, rows, 0.0), axis=0, keepdims=True)
            return jnp.where(at_zy > 0, picked, 0.0)

        def to_rows(cols):
            picked = jnp.sum(jnp.where(at_zy > 0, cols, 0.0), axis=0, keepdims=True)
            return jnp.where(at_x > 0, picked, 0.0)

        got = {}
        for k in (1, 3, 2):
            got[k] = lax.ppermute(own, "gen", first_axis[k])
        mate = lax.ppermute(held, "gen", core_stage[0])
        low = jnp.concatenate([own, got[1]], axis=0)
        high = jnp.concatenate([got[2], got[3]], axis=0)
        low_up = lax.ppermute(low, "gen", second_axis[1])
        high_down = lax.ppermute(high, "gen", second_axis[3])
        high_up = lax.ppermute(high, "gen", second_axis[1])
        low_down = lax.ppermute(low, "gen", second_axis[3])
        low_far = lax.ppermute(low_up, "gen", second_axis[1])
        high_far = lax.ppermute(high_down, "gen", second_axis[3])

        d0, hcol, mine, gmass, ahead, *carried = first_pass(held, tile0, ref_features, wg, wr)
        theirs = lax.ppermute(mine, "gen", core_stage[0])
        d1, row_part, lcol, hcol = first_pass(held, ahead, ref_features, wr, mine, d0, hcol, *carried)
        hrow = mine[:nq]
        weight = jnp.concatenate([wg, theirs[nq:]], axis=0)
        e0, z1_0, hs, ws = self_first(held, mate, [low, high], mine, theirs, place, 0)
        e1, z1_1 = self_first(held, mate, [low_up, high_up, low_down, high_down], hs, ws, place, 4)
        e2, z1_2 = self_first(held, mate, [low_far, high_far], hs, ws, place, 12)
        e = [e0, e1, e2]

        row_part = doubled(row_part, nq)
        col_part = jnp.concatenate([lcol, gmass], axis=0)
        col_part = stage(col_part, "gen", core_stage, nc)
        col_part = jnp.concatenate([col_part, to_cols(wg)], axis=0)
        col_part = stage(col_part, "gen", y_stage, nc)
        col_part = stage(col_part, "gen", z_stage, nc)
        gmass = col_part[nc : nc + 1]
        rmass = row_part[nq : nq + 1]
        wcols = col_part[nc + 8 :] / gmass
        gmass_log = jnp.log2(gmass)
        rmass_log = jnp.log2(rmass)
        f = hrow - (row_part[:nq] - rmass_log)
        c = hcol - (col_part[:nc] - gmass_log)
        ubase = jnp.log2(wr) - rmass_log - hcol
        vbase = jnp.log2(wg) - gmass_log - hrow
        share = wg / gmass

        lrow, lcol = next_pass([d0, d1], ubase + c, vbase + f)
        lrow = doubled(lrow, nq)
        lcol = stage(lcol, "gen", core_stage, nc)
        col_part = jnp.concatenate([lcol, z1_0 + z1_1 + z1_2], axis=0)
        col_part = stage(col_part, "gen", y_stage, nc)
        col_part = stage(col_part, "gen", z_stage, nc)
        f = 0.5 * (f + (hrow - lrow))
        c = 0.5 * (c + (hcol - col_part[:nc]))
        y1 = col_part[nc:] / gmass

        lrow, lcol = next_pass([d0, d1], ubase + c, vbase + f)
        y2 = self_apply(self_rows_kernel, e, wcols / y1, place, 2 * nq)
        row_part = jnp.concatenate([lrow, y2, to_rows(-jnp.log2(y1))], axis=0)
        row_part = stage(row_part, "ref", ref_stage, nq)
        f = 0.5 * (f + (hrow - row_part[:nq]))
        f_part = share * f
        f_part = jnp.concatenate([f_part, f_part], axis=0)
        mine = jnp.concatenate([lcol, f_part, row_part[nq:]], axis=0)
        theirs = shift(mine, "gen", core_stage)[0]
        lcol = log_add([lcol, theirs[:nc]])
        f_part = f_part + theirs[nc : nc + 8]
        y2, y2_mate, s1 = row_part[nq : 2 * nq], row_part[2 * nq : 3 * nq], row_part[3 * nq :]
        at = nc + 8
        y2 = y2 + theirs[at + nq : at + 2 * nq]
        y2_mate = y2_mate + theirs[at : at + nq]
        s1 = jnp.concatenate([s1, theirs[at + 2 * nq :]], axis=0)
        s2 = 0.5 * (s1 - jnp.log2(jnp.concatenate([y2, y2_mate], axis=0)))
        w3 = weight / gmass * jnp.exp2(s2)
        z3 = self_apply(self_cols_kernel, e, w3, place, n_zy)
        col_part = jnp.concatenate([lcol, f_part, z3, to_cols(s2[:nq])], axis=0)
        col_part = stage(col_part, "gen", y_stage, nc)
        col_part = stage(col_part, "gen", z_stage, nc)
        c = 0.5 * (c + (hcol - col_part[:nc]))
        f_part = col_part[nc : nc + nq]
        z3, s2 = col_part[nc + 8 : nc + 8 + n_zy], col_part[nc + 8 + n_zy :]

        unit = EPS / LOG2E
        ref_gap = c * unit - ref_self.reshape(nc, LANES)
        s3 = 0.5 * (s2 - jnp.log2(z3))
        s_part = jnp.sum((wcols * s3).reshape(2, 8, LANES), axis=0)
        s_part = s_part + shift(s_part, "gen", core_stage)[0]
        part = jnp.sum(((wr / rmass) * ref_gap).reshape(nc // 8, 8, LANES), axis=0) - unit * s_part
        row_part = jnp.concatenate([to_rows(s3), part], axis=0)
        row_part = row_part + sum(shift(row_part, "ref", ref_stage))
        gen_gap = (f - row_part[:nq]) * unit
        divergence = jnp.sum(unit * f_part + row_part[nq : 2 * nq] + row_part[2 * nq :])
        return gen_gap.reshape(gen_count), ref_gap.reshape(ref_count), divergence

    return run


def solution(mesh):
    n_gen, n_ref = mesh.shape["gen"], mesh.shape["ref"]
    n_core = 2
    n_y = 1
    while n_y * n_y * n_core < n_gen:
        n_y *= 2
    placed = (P("gen", None), P("gen"), P("ref", None), P("ref"), P("ref"))
    return jax.shard_map(
        build(n_gen // (n_y * n_core), n_y, n_core, n_ref),
        mesh=mesh,
        in_specs=placed,
        out_specs=(P("gen"), P("ref"), P()),
        check_vma=False,
    )
```

```python
import functools

import jax
import jax.numpy as jnp
from jax import lax
from jax.experimental import pallas as pl
from jax.experimental.pallas import tpu as pltpu
from jax.sharding import PartitionSpec as P


EPS = 0.1
LOG2E = 1.4426950408889634
F32 = jnp.float32
LANES = 128
TILE = 512
ROWS = 32
LEAD = 6
LOW = 2.0**-80
HIGH = 2.0**120


def vmem_array(x):
    return pltpu.with_memory_space_constraint(x, pltpu.VMEM)


def hbm_array(x):
    return pltpu.with_memory_space_constraint(x, pltpu.HBM)


def spread(vec_ref, out_ref, count, first=0, at=0):
    for q in range(count):
        block = jnp.broadcast_to(vec_ref[first + q : first + q + 1, :], (LANES, LANES))
        out_ref[(at + q) * LANES : (at + q + 1) * LANES, :] = block.T


def lane_fold(acc, op):
    return op(acc.T, axis=0, keepdims=True)


def norms(feat_ref, start, count, scale):
    width = feat_ref.shape[1]
    out = []
    for q in range(count):
        acc = jnp.zeros((LANES, LANES), F32)
        for c in range(width // LANES):
            x = feat_ref[start + q * LANES : start + (q + 1) * LANES, c * LANES : (c + 1) * LANES].astype(F32)
            acc = acc + x * x
        out.append(lane_fold(acc, jnp.sum) * scale)
    return out


def row_block(r):
    if isinstance(r, int):
        return slice(r * ROWS, (r + 1) * ROWS)
    return pl.ds(pl.multiple_of(r * ROWS, ROWS), ROWS)


def sweep(d_ref, base, chunks, u, vs_ref, rowacc_ref, straight=False, keep=None):
    rows = d_ref.shape[0]
    u = [jnp.broadcast_to(part, (8, LANES))[None] for part in u]

    def body(r, cols):
        at = row_block(r)
        vs = vs_ref[at, :].reshape(ROWS // 8, 8, LANES)
        racc = rowacc_ref[at, :].reshape(ROWS // 8, 8, LANES)
        out = []
        for c in range(chunks):
            d = d_ref[at, pl.ds(base + c * LANES, LANES)]
            if keep is not None:
                keep[0][at, pl.ds(pl.multiple_of(keep[1] + c * LANES, LANES), LANES)] = d
            p = jnp.exp2((d.reshape(ROWS // 8, 8, LANES) + u[c]) + vs)
            racc = racc + p
            out.append(cols[c] + jnp.sum(p, axis=0))
        rowacc_ref[at, :] = racc.reshape(ROWS, LANES)
        return tuple(out)

    cols = (jnp.zeros((8, LANES), F32),) * chunks
    if straight:
        for r in range(rows // ROWS):
            cols = body(r, cols)
    else:
        cols = lax.fori_loop(0, rows // ROWS, body, cols, unroll=4)
    return [jnp.sum(c, axis=0, keepdims=True) for c in cols]


def tile_peak(d_ref, u, vs_ref):
    rows = d_ref.shape[0]
    best = jnp.full((8, LANES), -3.0e38, F32)

    def body(r, best):
        at = pl.ds(pl.multiple_of(r * ROWS, ROWS), ROWS)
        val = (d_ref[at, 0:LANES] + u) + vs_ref[at, :]
        return jnp.maximum(best, jnp.max(val.reshape(ROWS // 8, 8, LANES), axis=0))

    best = lax.fori_loop(0, rows // ROWS, body, best, unroll=2)
    return jnp.max(jnp.max(best, axis=0, keepdims=True), axis=1, keepdims=True)


def start_peak(d_ref, u0, v_ref, vs_ref, peak_ref, rowacc_ref):
    rows = d_ref.shape[0]
    spread(v_ref, vs_ref, rows // LANES)
    peak = jnp.broadcast_to(tile_peak(d_ref, u0, vs_ref), (8, LANES))
    peak_ref[...] = peak
    vs_ref[...] = vs_ref[...] - peak[0:1, :]
    rowacc_ref[...] = jnp.zeros_like(rowacc_ref)


def finish(d_refs, u_ref, v_ref, vs_ref, rowacc_ref, colsum_ref, peak_ref, lrow_ref, lcol_ref):
    rows = d_refs[0].shape[0]
    nq = rows // LANES
    rowsum = [lane_fold(rowacc_ref[q * LANES : (q + 1) * LANES, :], jnp.sum) for q in range(nq)]
    rowsum = jnp.concatenate(rowsum, axis=0)
    colsum = colsum_ref[...]
    low = jnp.minimum(jnp.min(rowsum), jnp.min(colsum))
    high = jnp.maximum(jnp.max(rowsum), jnp.max(colsum))
    good = jnp.logical_and(low >= LOW, high <= HIGH)
    peak = peak_ref[0:1, :]

    @pl.when(good)
    def _():
        lrow_ref[0:nq, :] = (jnp.log2(rowsum) + peak) - v_ref[...]
        lcol_ref[...] = (jnp.log2(colsum) + peak) - u_ref[...]

    @pl.when(jnp.logical_not(good))
    def _():
        spread(v_ref, vs_ref, nq)

        def row_block(q, carry):
            part = pl.ds(pl.multiple_of(q * LANES, LANES), LANES)

            def scores(d_ref, first, c):
                at = pl.ds(pl.multiple_of(c * LANES, LANES), LANES)
                return d_ref[part, at] + u_ref[pl.ds(first + c, 1), :]

            best = jnp.full((LANES, LANES), -3.0e38, F32)
            first = 0
            for d_ref in d_refs:
                count = d_ref.shape[1] // LANES
                best = lax.fori_loop(
                    0, count, lambda c, best: jnp.maximum(best, scores(d_ref, first, c)), best
                )
                first += count
            top = jnp.max(best, axis=1, keepdims=True)
            acc = jnp.zeros((LANES, LANES), F32)
            first = 0
            for d_ref in d_refs:
                count = d_ref.shape[1] // LANES
                acc = lax.fori_loop(
                    0, count, lambda c, acc: acc + jnp.exp2(scores(d_ref, first, c) - top), acc
                )
                first += count
            log_sum = jnp.log2(jnp.sum(acc, axis=1, keepdims=True)) + top
            lrow_ref[pl.ds(q, 1), :] = lane_fold(jnp.broadcast_to(log_sum, (LANES, LANES)), jnp.max)
            return carry

        lax.fori_loop(0, nq, row_block, 0)
        first = 0
        for d_ref in d_refs:
            count = d_ref.shape[1] // LANES

            def column(c, carry):
                at = pl.ds(pl.multiple_of(c * LANES, LANES), LANES)

                def block(r):
                    part = pl.ds(pl.multiple_of(r * ROWS, ROWS), ROWS)
                    return d_ref[part, at] + vs_ref[part, :]

                top = lax.fori_loop(
                    0,
                    rows // ROWS,
                    lambda r, best: jnp.maximum(best, jnp.max(block(r), axis=0, keepdims=True)),
                    jnp.full((1, LANES), -3.0e38, F32),
                )
                total = lax.fori_loop(
                    0,
                    rows // ROWS,
                    lambda r, acc: acc + jnp.sum(jnp.exp2(block(r) - top), axis=0, keepdims=True),
                    jnp.zeros((1, LANES), F32),
                )
                lcol_ref[pl.ds(first + c, 1), :] = top + jnp.log2(total)
                return carry

            lax.fori_loop(0, count, column, 0)
            first += count


def entry_kernel(gen_hbm, ref_hbm, gweight_hbm, rweight_hbm, own_ref, gen_ref, tile_ref, gweight_ref, rweight_ref, sem):
    count = own_ref.shape[0]
    at = pl.ds(pl.multiple_of(lax.axis_index("ref") * count, count), count)
    pairs = (
        (gen_hbm.at[at, :], own_ref),
        (gweight_hbm, gweight_ref),
        (rweight_hbm, rweight_ref),
        (gen_hbm, gen_ref),
        (ref_hbm.at[: tile_ref.shape[0], :], tile_ref),
    )
    copies = [pltpu.make_async_copy(src, dst, sem.at[k]) for k, (src, dst) in enumerate(pairs)]
    for copy in copies:
        copy.start()
    for copy in copies:
        copy.wait()


def entry(gen, ref, gweight, rweight):
    vmem = pl.BlockSpec(memory_space=pltpu.VMEM)
    hbm = pl.BlockSpec(memory_space=pltpu.HBM)
    width = gen.shape[1]
    return pl.pallas_call(
        entry_kernel,
        in_specs=[hbm] * 4,
        out_shape=(
            pltpu.VMEM((LANES, width), gen.dtype),
            pltpu.VMEM(gen.shape, gen.dtype),
            pltpu.VMEM((TILE, width), ref.dtype),
            pltpu.VMEM(gweight.shape, F32),
            pltpu.VMEM(rweight.shape, F32),
        ),
        out_specs=(vmem,) * 5,
        scratch_shapes=[pltpu.SemaphoreType.DMA((5,))],
        compiler_params=pltpu.CompilerParams(vmem_limit_bytes=4 << 20),
        name="entry",
    )(*[hbm_array(x) for x in (gen, ref, gweight, rweight)])


def total(x):
    return jnp.sum(jnp.sum(x, axis=0, keepdims=True), axis=1, keepdims=True)


def first_kernel(first_tile, steps, *refs):
    leading = first_tile == 0
    if leading:
        gen_ref, first_ref, gweight_ref, rweight_ref, ref_hbm, *refs = refs
        d_ref, hcol_ref, hrow_ref, mass_ref, ahead_ref, vs_ref, rowacc_ref, u_ref, colsum_ref, peak_ref, *refs = refs
        tile_ref, stage_ref, v_ref, sem = refs
    else:
        gen_ref, first_ref, rweight_ref, hrow_ref, ref_hbm, before_ref, *refs = refs
        hcol0_ref, vs_ref, rowacc0_ref, u0_ref, colsum0_ref, peak_ref, *refs = refs
        d_ref, lrow_ref, lcol_ref, hcol_ref, tile_ref, stage_ref, v_ref, rowacc_ref, u_ref, colsum_ref, sem = refs
    rows, width = gen_ref.shape
    nq = rows // LANES
    chunks = TILE // LANES
    half_scale = 0.5 * LOG2E / (EPS * width)
    dot_scale = LOG2E / (EPS * width)

    def load(j):
        at = pl.ds(pl.multiple_of((first_tile + j) * TILE, TILE), TILE)
        return pltpu.make_async_copy(ref_hbm.at[at, :], tile_ref.at[j], sem.at[j])

    def product(j, tile, out_ref, columns):
        for c, half in enumerate(norms(tile, 0, chunks, half_scale)):
            row = pl.ds((first_tile + j) * chunks + c, 1)
            hcol_ref[row, :] = half
            u_ref[row, :] = jnp.log2(rweight_ref[row, :]) - half
        dots = lax.dot_general(gen_ref[...], tile[...], (((1,), (1,)), ((), ())), preferred_element_type=F32)
        out_ref[:, columns] = dots * dot_scale

    def sums(j, straight, src_ref, base, keep):
        mine = [u_ref[pl.ds(j * chunks + c, 1), :] for c in range(chunks)]
        for c, part in enumerate(sweep(src_ref, base, chunks, mine, vs_ref, rowacc_ref, straight, keep)):
            colsum_ref[pl.ds(j * chunks + c, 1), :] = part

    whole = slice(0, TILE)
    load(1).start()
    if leading:
        ahead = pltpu.make_async_copy(ref_hbm.at[steps * TILE : (steps + 1) * TILE, :], ahead_ref, sem.at[steps])
        for q, part in enumerate(norms(gen_ref, 0, nq, half_scale)):
            hrow_ref[q : q + 1, :] = part
            v_ref[q : q + 1, :] = jnp.log2(gweight_ref[q : q + 1, :]) - part
            hrow_ref[nq + q : nq + q + 1, :] = gweight_ref[q : q + 1, :]
        mass_ref[...] = jnp.broadcast_to(total(gweight_ref[...]), (8, LANES))
        product(0, first_ref, stage_ref, whole)
        start_peak(stage_ref, u_ref[0:1, :], v_ref, vs_ref, peak_ref, rowacc_ref)
    else:
        v_ref[...] = jnp.log2(hrow_ref[nq : 2 * nq, :]) - hrow_ref[0:nq, :]
        lrow_ref[nq : 2 * nq, :] = jnp.broadcast_to(total(rweight_ref[...]), (nq, LANES))
        done = first_tile * chunks
        hcol_ref[0:done, :] = hcol0_ref[...]
        rowacc_ref[...] = rowacc0_ref[...]
        u_ref[0:done, :] = u0_ref[...]
        colsum_ref[0:done, :] = colsum0_ref[...]
        sums(first_tile - 1, True, before_ref, (first_tile - 1) * TILE, None)
        product(0, first_ref, stage_ref, whole)

    def step(j, carry):
        load(j).wait()

        @pl.when(j + 1 < steps)
        def _():
            load(j + 1).start()

        sums(first_tile + j - 1, True, stage_ref, 0, (d_ref, (j - 1) * TILE))
        product(j, tile_ref.at[j], stage_ref, whole)
        return carry

    if leading:
        lax.fori_loop(1, steps - 1, step, 0)
        load(steps - 1).wait()
        ahead.start()
        sums(steps - 2, True, stage_ref, 0, (d_ref, (steps - 2) * TILE))
        product(steps - 1, tile_ref.at[steps - 1], d_ref, slice((steps - 1) * TILE, steps * TILE))
        colsum_ref[(steps - 1) * chunks : steps * chunks, :] = jnp.zeros((chunks, LANES), F32)
        ahead.wait()
    else:
        lax.fori_loop(1, steps, step, 0)
        sums(first_tile + steps - 1, False, stage_ref, 0, (d_ref, (steps - 1) * TILE))
        finish([before_ref, d_ref], u_ref, v_ref, vs_ref, rowacc_ref, colsum_ref, peak_ref, lrow_ref, lcol_ref)


def first_pass(gen, first, ref, *more):
    rows, width = gen.shape
    nq, tiles = rows // LANES, ref.shape[0] // TILE
    leading = len(more) == 2
    first_tile, steps = (0, LEAD) if leading else (LEAD, tiles - LEAD)
    cols = steps * TILE
    nc, all_nc = cols // LANES, ref.shape[0] // LANES
    vmem = pl.BlockSpec(memory_space=pltpu.VMEM)
    hbm = pl.BlockSpec(memory_space=pltpu.HBM)
    vec = lambda n: jax.ShapeDtypeStruct((n, LANES), F32)
    lanes = pltpu.VMEM((rows, LANES), F32)
    scratch = [
        pltpu.VMEM((steps, TILE, width), jnp.bfloat16),
        pltpu.VMEM((rows, TILE), F32),
        pltpu.VMEM((nq, LANES), F32),
    ]
    if leading:
        gweight, rweight = more
        operands = [vmem_array(gen), vmem_array(first), gweight, rweight, hbm_array(ref)]
        outs = (
            pltpu.VMEM((rows, cols), F32), vec(nc), vec(2 * nq), vec(8), pltpu.VMEM((TILE, width), ref.dtype),
            lanes, lanes, vec(nc), vec(nc), vec(8),
        )
        specs = [vmem] * 4 + [hbm]
    else:
        rweight, hrow, before, hcol, vs, rowacc, u, colsum, peak = more
        operands = [vmem_array(gen), vmem_array(first), rweight, hrow, hbm_array(ref), vmem_array(before)]
        operands += [hcol, vmem_array(vs), vmem_array(rowacc), u, colsum, peak]
        outs = (pltpu.VMEM((rows, cols), F32), vec(2 * nq), vec(all_nc), vec(all_nc))
        specs = [vmem] * 4 + [hbm] + [vmem] * 7
        scratch += [
            pltpu.VMEM((rows, LANES), F32),
            pltpu.VMEM((all_nc, LANES), F32),
            pltpu.VMEM((all_nc, LANES), F32),
        ]
    return pl.pallas_call(
        functools.partial(first_kernel, first_tile, steps),
        in_specs=specs,
        out_shape=outs,
        out_specs=(vmem,) * len(outs),
        scratch_shapes=scratch + [pltpu.SemaphoreType.DMA((steps + 1,))],
        compiler_params=pltpu.CompilerParams(vmem_limit_bytes=20 << 20),
        name="cross_first_0" if leading else "cross_first_1",
    )(*operands)


def next_kernel(count, *refs):
    sources = refs[:count]
    u_ref, v_ref, lrow_ref, lcol_ref, vs_ref, rowacc_ref, colsum_ref, peak_ref = refs[count:]
    chunks = TILE // LANES
    start_peak(sources[0], u_ref[0:1, :], v_ref, vs_ref, peak_ref, rowacc_ref)
    first = 0
    for d_ref in sources:
        steps = d_ref.shape[1] // TILE

        def step(j, carry):
            u = [u_ref[pl.ds(first + j * chunks + c, 1), :] for c in range(chunks)]
            base = pl.multiple_of(j * TILE, TILE)
            for c, part in enumerate(sweep(d_ref, base, chunks, u, vs_ref, rowacc_ref)):
                colsum_ref[pl.ds(first + j * chunks + c, 1), :] = part
            return carry

        lax.fori_loop(0, steps, step, 0)
        first += steps * chunks
    finish(sources, u_ref, v_ref, vs_ref, rowacc_ref, colsum_ref, peak_ref, lrow_ref, lcol_ref)


def next_pass(parts, u, v):
    rows = parts[0].shape[0]
    cols = sum(part.shape[1] for part in parts)
    nq, nc = rows // LANES, cols // LANES
    vmem = pl.BlockSpec(memory_space=pltpu.VMEM)
    return pl.pallas_call(
        functools.partial(next_kernel, len(parts)),
        in_specs=[vmem] * (len(parts) + 2),
        out_shape=(jax.ShapeDtypeStruct((nq, LANES), F32), jax.ShapeDtypeStruct((nc, LANES), F32)),
        out_specs=(vmem, vmem),
        scratch_shapes=[
            pltpu.VMEM((rows, LANES), F32),
            pltpu.VMEM((rows, LANES), F32),
            pltpu.VMEM((nc, LANES), F32),
            pltpu.VMEM((8, LANES), F32),
        ],
        compiler_params=pltpu.CompilerParams(vmem_limit_bytes=8 << 20),
    )(*[vmem_array(part) for part in parts], u, v)


def self_first_kernel(count, first, *refs):
    own_ref, mate_ref = refs[:2]
    sources = refs[2 : 2 + count]
    rest = refs[2 + count :]
    half, width = own_ref.shape
    nq = half // LANES
    if first == 0:
        mine_ref, theirs_ref, place_ref, e_ref, z_ref, hs_ref, ws_ref = rest
        for at, vec_ref in ((0, mine_ref), (nq, theirs_ref)):
            spread(vec_ref, hs_ref, nq, 0, at)
            spread(vec_ref, ws_ref, nq, nq, at)
    else:
        hs_ref, ws_ref, place_ref, e_ref, z_ref = rest
    wide = 256
    chunks = wide // LANES
    half_scale = 0.5 * LOG2E / (EPS * width)
    dot_scale = LOG2E / (EPS * width)
    z_ref[...] = jnp.zeros_like(z_ref)
    tiles = [(src, k) for src in sources for k in range(src.shape[0] // wide)]
    piece_half = {}

    def product(t):
        src, k = tiles[t]
        view = src.at[k * wide : (k + 1) * wide, :]
        piece_half[t] = norms(view, 0, chunks, half_scale)
        for h, rows_ref in enumerate((own_ref, mate_ref)):
            e_ref[h * half : (h + 1) * half, t * wide : (t + 1) * wide] = lax.dot_general(
                rows_ref[...], view[...], (((1,), (1,)), ((), ())), preferred_element_type=F32
            )

    def sums(t, straight):
        def body(r, acc):
            at = row_block(r)
            hs = hs_ref[at, :]
            ws = ws_ref[at, :]
            out = []
            for c in range(chunks):
                part = slice(t * wide + c * LANES, t * wide + (c + 1) * LANES)
                e = jnp.exp2(e_ref[at, part] * dot_scale - (hs + piece_half[t][c]))
                e_ref[at, part] = e
                out.append(acc[c] + jnp.sum((e * ws).reshape(ROWS // 8, 8, LANES), axis=0))
            return tuple(out)

        acc = (jnp.zeros((8, LANES), F32),) * chunks
        if straight:
            for r in range(2 * half // ROWS):
                acc = body(r, acc)
        else:
            acc = lax.fori_loop(0, 2 * half // ROWS, body, acc, unroll=2)
        for c in range(chunks):
            z_ref[pl.ds(place_ref[first + t * chunks + c], 1), :] = jnp.sum(acc[c], axis=0, keepdims=True)

    product(0)
    for t in range(1, len(tiles)):
        sums(t - 1, True)
        product(t)
    sums(len(tiles) - 1, False)


def self_first(own, mate, sources, left, right, place, first):
    rows = 2 * own.shape[0]
    cols = sum(src.shape[0] for src in sources)
    vmem = pl.BlockSpec(memory_space=pltpu.VMEM)
    lanes = () if first else (pltpu.VMEM((rows, LANES), F32),) * 2
    if first:
        left, right = vmem_array(left), vmem_array(right)
    return pl.pallas_call(
        functools.partial(self_first_kernel, len(sources), first),
        in_specs=[vmem] * (4 + len(sources)) + [pl.BlockSpec(memory_space=pltpu.SMEM)],
        out_shape=(pltpu.VMEM((rows, cols), F32), jax.ShapeDtypeStruct((place.shape[0], LANES), F32)) + lanes,
        out_specs=(vmem,) * (2 + len(lanes)),
        compiler_params=pltpu.CompilerParams(vmem_limit_bytes=8 << 20),
    )(vmem_array(own), vmem_array(mate), *[vmem_array(src) for src in sources], left, right, place)


def self_cols_kernel(count, *refs):
    w_ref, place_ref, z_ref, ws_ref = refs[count:]
    rows = refs[0].shape[0]
    chunks = TILE // LANES
    spread(w_ref, ws_ref, rows // LANES)
    first = 0
    for e_ref in refs[:count]:
        for base in range(0, e_ref.shape[1], TILE):

            def body(r, acc):
                at = row_block(r)
                ws = ws_ref[at, :]
                out = []
                for c in range(chunks):
                    e = e_ref[at, base + c * LANES : base + (c + 1) * LANES] * ws
                    out.append(acc[c] + jnp.sum(e.reshape(ROWS // 8, 8, LANES), axis=0))
                return tuple(out)

            acc = lax.fori_loop(0, rows // ROWS, body, (jnp.zeros((8, LANES), F32),) * chunks, unroll=4)
            for c in range(chunks):
                z_ref[pl.ds(place_ref[first + c], 1), :] = jnp.sum(acc[c], axis=0, keepdims=True)
            first += chunks


def self_rows_kernel(count, *refs):
    w_ref, place_ref, y_ref, rowacc_ref = refs[count:]
    rows = refs[0].shape[0]
    first = 0
    for at_e, e_ref in enumerate(refs[:count]):
        chunks = e_ref.shape[1] // LANES
        w = [
            jnp.broadcast_to(w_ref[pl.ds(place_ref[first + c], 1), :], (8, LANES))[None] for c in range(chunks)
        ]

        def body(r, carry):
            at = row_block(r)
            parts = [
                e_ref[at, c * LANES : (c + 1) * LANES].reshape(ROWS // 8, 8, LANES) * w[c] for c in range(chunks)
            ]
            acc = sum(parts[1:], parts[0]).reshape(ROWS, LANES)
            rowacc_ref[at, :] = acc if at_e == 0 else rowacc_ref[at, :] + acc
            return carry

        lax.fori_loop(0, rows // ROWS, body, 0, unroll=4)
        first += chunks
    for q in range(rows // LANES):
        y_ref[q : q + 1, :] = lane_fold(rowacc_ref[q * LANES : (q + 1) * LANES, :], jnp.sum)


def self_apply(kernel, parts, w, place, out_rows):
    rows = parts[0].shape[0]
    vmem = pl.BlockSpec(memory_space=pltpu.VMEM)
    return pl.pallas_call(
        functools.partial(kernel, len(parts)),
        in_specs=[vmem] * (len(parts) + 1) + [pl.BlockSpec(memory_space=pltpu.SMEM)],
        out_shape=jax.ShapeDtypeStruct((out_rows, LANES), F32),
        out_specs=vmem,
        scratch_shapes=[pltpu.VMEM((rows, LANES), F32)],
        compiler_params=pltpu.CompilerParams(vmem_limit_bytes=8 << 20),
    )(*[vmem_array(part) for part in parts], w, place)


def log_add(parts):
    top = functools.reduce(jnp.maximum, parts)
    return top + jnp.log2(sum(jnp.exp2(part - top) for part in parts))


def build(n_z, n_y, n_core, n_ref):
    n_zy = n_z * n_y
    n_gen = n_zy * n_core
    assert n_z == n_y == n_ref == 4 and n_core == 2

    def place_of(g):
        return g // (n_y * n_core), (g // n_core) % n_y, g % n_core

    def gen_perm(move):
        out = []
        for g in range(n_gen):
            z, y, c = move(*place_of(g))
            out.append((g, ((z % n_z) * n_y + y % n_y) * n_core + c % n_core))
        return out

    core_stage = [gen_perm(lambda z, y, c: (z, y, c + 1))]
    y_stage = [gen_perm(lambda z, y, c: (z, y + k, c)) for k in (1, 2, 3)]
    z_stage = [gen_perm(lambda z, y, c: (z + k, y, c)) for k in (1, 2, 3)]
    ref_stage = [[(i, (i + k) % n_ref) for i in range(n_ref)] for k in (1, 2, 3)]
    first_axis = {k: gen_perm(lambda z, y, c: (z, y + k, c) if c == 0 else (z + k, y, c)) for k in (1, 2, 3)}
    second_axis = {k: gen_perm(lambda z, y, c: (z + k, y, c) if c == 0 else (z, y + k, c)) for k in (1, 2, 3)}
    order = [(0, 0), (0, 1), (0, 2), (0, 3)]
    order += [(1, 0), (1, 1), (1, 2), (1, 3), (3, 0), (3, 1), (3, 2), (3, 3)]
    order += [(2, 0), (2, 1), (2, 2), (2, 3)]

    def shift(value, axis, perms):
        return [lax.ppermute(value, axis, perm) for perm in perms]

    def merge(parts, logs):
        top = log_add([part[:logs] for part in parts])
        if parts[0].shape[0] == logs:
            return top
        return jnp.concatenate([top, sum(part[logs:] for part in parts)], axis=0)

    def stage(value, axis, perms, logs):
        return merge([value] + shift(value, axis, perms), logs)

    def doubled(value, logs):
        for flip in (1, n_ref - 1):
            value = merge([value, lax.ppermute(value, "ref", [(i, i ^ flip) for i in range(n_ref)])], logs)
        return value

    def run(gen_features, gen_weight, ref_features, ref_weight, ref_self):
        gen_count = gen_features.shape[0]
        ref_count = ref_features.shape[0]
        nq, nc = gen_count // LANES, ref_count // LANES
        g = lax.axis_index("gen")
        x = lax.axis_index("ref")
        z, y, core = place_of(g)
        zy = z * n_y + y
        b, a = (lax.broadcasted_iota(jnp.int32, (len(order),), 0) for _ in range(2))
        b = functools.reduce(lambda v, k: jnp.where(a == k, order[k][0], v), range(len(order)), b)
        a = a % 4
        mine = ((z - b + n_z) % n_z) * n_y + (y - a + n_y) % n_y
        other = ((z - a + n_z) % n_z) * n_y + (y - b + n_y) % n_y
        place = jnp.where(core == 0, mine, other)
        at_zy = (lax.broadcasted_iota(jnp.int32, (n_zy, LANES), 0) == zy).astype(F32)
        at_x = (lax.broadcasted_iota(jnp.int32, (n_ref, LANES), 0) == x).astype(F32)
        wg = gen_weight.reshape(nq, LANES)
        wg, place, at_zy, at_x = lax.optimization_barrier((wg, place, at_zy, at_x))
        own, held, tile0, wg, wr = entry(
            gen_features, ref_features, wg, ref_weight.reshape(nc, LANES)
        )

        def to_cols(rows):
            picked = jnp.sum(jnp.where(at_x > 0, rows, 0.0), axis=0, keepdims=True)
            return jnp.where(at_zy > 0, picked, 0.0)

        def to_rows(cols):
            picked = jnp.sum(jnp.where(at_zy > 0, cols, 0.0), axis=0, keepdims=True)
            return jnp.where(at_x > 0, picked, 0.0)

        got = {}
        for k in (1, 3, 2):
            got[k] = lax.ppermute(own, "gen", first_axis[k])
        mate = lax.ppermute(held, "gen", core_stage[0])
        low = jnp.concatenate([own, got[1]], axis=0)
        high = jnp.concatenate([got[2], got[3]], axis=0)
        low_up = lax.ppermute(low, "gen", second_axis[1])
        high_down = lax.ppermute(high, "gen", second_axis[3])
        high_up = lax.ppermute(high, "gen", second_axis[1])
        low_down = lax.ppermute(low, "gen", second_axis[3])
        low_far = lax.ppermute(low_up, "gen", second_axis[1])
        high_far = lax.ppermute(high_down, "gen", second_axis[3])

        d0, hcol, mine, gmass, ahead, *carried = first_pass(held, tile0, ref_features, wg, wr)
        theirs = lax.ppermute(mine, "gen", core_stage[0])
        d1, row_part, lcol, hcol = first_pass(held, ahead, ref_features, wr, mine, d0, hcol, *carried)
        hrow = mine[:nq]
        weight = jnp.concatenate([wg, theirs[nq:]], axis=0)
        e0, z1_0, hs, ws = self_first(held, mate, [low, high], mine, theirs, place, 0)
        e1, z1_1 = self_first(held, mate, [low_up, high_up, low_down, high_down], hs, ws, place, 4)
        e2, z1_2 = self_first(held, mate, [low_far, high_far], hs, ws, place, 12)
        e = [e0, e1, e2]

        row_part = doubled(row_part, nq)
        col_part = jnp.concatenate([lcol, gmass], axis=0)
        col_part = stage(col_part, "gen", core_stage, nc)
        col_part = jnp.concatenate([col_part, to_cols(wg)], axis=0)
        col_part = stage(col_part, "gen", list(first_axis.values()), nc)
        col_part = stage(col_part, "gen", list(second_axis.values()), nc)
        gmass = col_part[nc : nc + 1]
        rmass = row_part[nq : nq + 1]
        wcols = col_part[nc + 8 :] / gmass
        gmass_log = jnp.log2(gmass)
        rmass_log = jnp.log2(rmass)
        f = hrow - (row_part[:nq] - rmass_log)
        c = hcol - (col_part[:nc] - gmass_log)
        ubase = jnp.log2(wr) - rmass_log - hcol
        vbase = jnp.log2(wg) - gmass_log - hrow
        share = wg / gmass

        lrow, lcol = next_pass([d0, d1], ubase + c, vbase + f)
        lrow = doubled(lrow, nq)
        lcol = stage(lcol, "gen", core_stage, nc)
        col_part = jnp.concatenate([lcol, z1_0 + z1_1 + z1_2], axis=0)
        col_part = stage(col_part, "gen", y_stage, nc)
        col_part = stage(col_part, "gen", z_stage, nc)
        f = 0.5 * (f + (hrow - lrow))
        c = 0.5 * (c + (hcol - col_part[:nc]))
        y1 = col_part[nc:] / gmass

        lrow, lcol = next_pass([d0, d1], ubase + c, vbase + f)
        y2 = self_apply(self_rows_kernel, e, wcols / y1, place, 2 * nq)
        row_part = jnp.concatenate([lrow, y2, to_rows(-jnp.log2(y1))], axis=0)
        row_part = stage(row_part, "ref", ref_stage, nq)
        f = 0.5 * (f + (hrow - row_part[:nq]))
        f_part = share * f
        f_part = jnp.concatenate([f_part, f_part], axis=0)
        mine = jnp.concatenate([lcol, f_part, row_part[nq:]], axis=0)
        theirs = shift(mine, "gen", core_stage)[0]
        lcol = log_add([lcol, theirs[:nc]])
        f_part = f_part + theirs[nc : nc + 8]
        y2, y2_mate, s1 = row_part[nq : 2 * nq], row_part[2 * nq : 3 * nq], row_part[3 * nq :]
        at = nc + 8
        y2 = y2 + theirs[at + nq : at + 2 * nq]
        y2_mate = y2_mate + theirs[at : at + nq]
        s1 = jnp.concatenate([s1, theirs[at + 2 * nq :]], axis=0)
        s2 = 0.5 * (s1 - jnp.log2(jnp.concatenate([y2, y2_mate], axis=0)))
        w3 = weight / gmass * jnp.exp2(s2)
        z3 = self_apply(self_cols_kernel, e, w3, place, n_zy)
        col_part = jnp.concatenate([lcol, f_part, z3, to_cols(s2[:nq])], axis=0)
        col_part = stage(col_part, "gen", y_stage, nc)
        col_part = stage(col_part, "gen", z_stage, nc)
        c = 0.5 * (c + (hcol - col_part[:nc]))
        f_part = col_part[nc : nc + nq]
        z3, s2 = col_part[nc + 8 : nc + 8 + n_zy], col_part[nc + 8 + n_zy :]

        unit = EPS / LOG2E
        ref_gap = c * unit - ref_self.reshape(nc, LANES)
        s3 = 0.5 * (s2 - jnp.log2(z3))
        s_part = jnp.sum((wcols * s3).reshape(2, 8, LANES), axis=0)
        s_part = s_part + shift(s_part, "gen", core_stage)[0]
        part = jnp.sum(((wr / rmass) * ref_gap).reshape(nc // 8, 8, LANES), axis=0) - unit * s_part
        row_part = jnp.concatenate([to_rows(s3), part], axis=0)
        row_part = row_part + sum(shift(row_part, "ref", ref_stage))
        gen_gap = (f - row_part[:nq]) * unit
        divergence = jnp.sum(unit * f_part + row_part[nq : 2 * nq] + row_part[2 * nq :])
        return gen_gap.reshape(gen_count), ref_gap.reshape(ref_count), divergence

    return run


def solution(mesh):
    n_gen, n_ref = mesh.shape["gen"], mesh.shape["ref"]
    n_core = 2
    n_y = 1
    while n_y * n_y * n_core < n_gen:
        n_y *= 2
    placed = (P("gen", None), P("gen"), P("ref", None), P("ref"), P("ref"))
    return jax.shard_map(
        build(n_gen // (n_y * n_core), n_y, n_core, n_ref),
        mesh=mesh,
        in_specs=placed,
        out_specs=(P("gen"), P("ref"), P()),
        check_vma=False,
    )
```
